32 devices in a mesh: dp: 4 (over z), freq: 2 (over core), tm: 4 (over y, x).
Axes of the slice: x: 2, y: 2, z: 4, core: 2. Of those that a mesh axis runs over, the one named last changes fastest.
Arguments:
- patches: bfloat16 [1312, 32, 768], P(('freq', 'tm'), 'dp'), may hold values from -6 to 6
- col_counts: int32 [4], replicated, may hold values from 26 to 27, as said below
- norm_gain: bfloat16 [2, 768], replicated, may hold values from 0.099609375 to 1.8984375
- norm_shift: bfloat16 [2, 768], replicated, may hold values from -3 to 3
- joint_proj: bfloat16 [768, 2304], replicated, may hold values from -0.3125 to 0.3125
- proj_bias: bfloat16 [2, 768], replicated, may hold values from -3 to 3
- out_proj: bfloat16 [768, 768], replicated, may hold values from -0.875 to 0.875
- up_proj: bfloat16 [768, 3072], replicated, may hold values from -0.21875 to 0.21875
- up_bias: bfloat16 [3072], replicated, may hold values from -3 to 3
- down_proj: bfloat16 [3072, 768], replicated, may hold values from -0.109375 to 0.109375
- out_bias: bfloat16 [2, 768], replicated, may hold values from -3 to 3
- cotangent: bfloat16 [1312, 32, 768], P(('freq', 'tm'), 'dp'), may hold values from -6 to 6
Outputs:
- output: bfloat16 [1312, 32, 768], P(('freq', 'tm'), 'dp')
- grad_patches: bfloat16 [1312, 32, 768], P(('freq', 'tm'), 'dp')
- grad_norm_gain: float32 [2, 768], P(None, ('freq', 'tm'))
- grad_norm_shift: float32 [2, 768], P(None, ('freq', 'tm'))
- grad_joint_proj: float32 [768, 2304], P(('freq', 'tm'))
- grad_proj_bias: float32 [2, 768], P(None, ('freq', 'tm'))
- grad_out_proj: float32 [768, 768], P(('freq', 'tm'))
- grad_up_proj: float32 [768, 3072], P(('freq', 'tm'))
- grad_up_bias: float32 [3072], P(('freq', 'tm'))
- grad_down_proj: float32 [3072, 768], P(('freq', 'tm'))
- grad_out_bias: float32 [2, 768], P(None, ('freq', 'tm'))
The draws below stay inside these ranges and needn't reach their ends.
Inputs may be any that keep to these rules, and one draw needn't show every extreme that they name: `col_counts`: each entry is 26 or 27, and both occur in every draw.
All inputs are finite; a program needn't handle non-finite values.
Results may differ from the reference program's by a relative error of at most 0.019.
Values may be sent and summed in bfloat16 or wider, within the bound.
No kernel may reach another device: no remote copies, remote signals or barrier semaphores. Data moves between devices by JAX's collectives and lax.ppermute only.
A program may use at most 448 MiB of HBM per device.

```python
import math
import jax
import jax.numpy as jnp
from jax import lax

D = 768
HEADS = 12
DH = 64
FF = 3072
FREQ_ROWS = 12
COLS_CAP = 27
SLOTS = 164
KEYS = 1312
CLIPS = 32
N_FREQ = 2
N_TM = 4


def draw_col_counts(key, part):
    shorter = jax.random.randint(jax.random.fold_in(key, 11), (N_TM,), 0, 2)
    order = jax.random.permutation(jax.random.fold_in(key, 12), N_TM)
    shorter = shorter.at[order[0]].set(0)
    shorter = shorter.at[order[1]].set(1)
    return (COLS_CAP - shorter).astype(jnp.int32)


def shard_levels(own_key, extent, cuts, least, top_value):
    loudness, own = 1.0, jax.random.fold_in(own_key, 6)
    for position, blocks in cuts:
        steps = jnp.exp(jax.random.uniform(jax.random.fold_in(own, position), (blocks,), jnp.float32, least / len(cuts), top_value / len(cuts)))
        loudness = loudness * jnp.repeat(steps, extent[position] // blocks).reshape([-1 if axis == position else 1 for axis in range(len(extent))])
    return loudness


def noise(stream_key, shape, scale, reach, pieces=(), kind=jnp.bfloat16):
    drawn = scale * jax.random.normal(stream_key, shape, jnp.float32)
    if pieces:
        drawn = drawn * shard_levels(stream_key, shape, pieces, -0.22, 0.18)
    return jnp.clip(drawn, -reach, reach).astype(kind)


def setup_inputs(seed: int = 0) -> dict:
    splits = jax.random.split(jax.random.key(seed), 13)
    patches = noise(splits[0], (KEYS, CLIPS, D), 1.0, 6.0, ((0, 8), (1, 4)))
    col_counts = draw_col_counts(jax.random.fold_in(splits[12], 71), 0)
    norm_gain = jnp.clip(1.0 + 0.18 * jax.random.normal(splits[2], (2, D), jnp.float32), 0.099609375, 1.8984375).astype(jnp.bfloat16)
    norm_shift = noise(splits[3], (2, D), 0.5, 3.0)
    joint_proj = noise(splits[4], (D, 3 * D), (D // 2) ** -0.5, 0.3125)
    proj_bias = noise(splits[5], (2, D), 0.5, 3.0)
    out_proj = noise(splits[6], (D, D), (D // 16) ** -0.5, 0.875)
    up_proj = noise(splits[7], (D, FF), D ** -0.5, 0.21875)
    up_bias = noise(splits[8], (FF,), 0.5, 3.0)
    down_proj = noise(splits[9], (FF, D), FF ** -0.5, 0.109375)
    out_bias = noise(splits[10], (2, D), 0.5, 3.0)
    cotangent = noise(splits[11], (KEYS, CLIPS, D), 1.0, 6.0, ((0, 8), (1, 4)))
    return dict(patches=patches, col_counts=col_counts, norm_gain=norm_gain, norm_shift=norm_shift, joint_proj=joint_proj, proj_bias=proj_bias, out_proj=out_proj, up_proj=up_proj, up_bias=up_bias, down_proj=down_proj, out_bias=out_bias, cotangent=cotangent)


EPS = 1e-06
NEG = -1000000000.0
HIGHEST = lax.Precision.HIGHEST

@jax.custom_vjp
def low(v):
    return lax.optimization_barrier(v.astype(jnp.bfloat16)).astype(jnp.float32)

@jax.custom_vjp
def low_back(v):
    return v

def low_keep(v):
    return (low(v), None)

def low_pass(kept, grad):
    return (grad,)

def back_keep(v):
    return (v, None)

def back_low(kept, grad):
    return (low(grad),)
low.defvjp(low_keep, low_pass)
low_back.defvjp(back_keep, back_low)

def live_slots(col_counts, slot_ids, freq_ids, time_ids, freq_rows, cap_cols):
    table = jnp.arange(col_counts.shape[0], dtype=jnp.int32)
    live_cols = lax.optimization_barrier(jnp.sum(jnp.where(time_ids[:, None] == table[None, :], col_counts[None, :], 0), axis=1))
    in_grid = slot_ids < freq_rows * cap_cols
    column_live = slot_ids // freq_rows < live_cols
    extra_live = (time_ids == 0) & (freq_ids == 0)
    return jnp.where(in_grid, column_live, extra_live)

def norm_rows(values, gain, shift):
    centered = values - lax.optimization_barrier(jnp.mean(values, axis=-1, keepdims=True))
    inverse = lax.rsqrt(lax.optimization_barrier(jnp.mean(centered * centered, axis=-1, keepdims=True)) + EPS)
    return centered * inverse * gain + shift

def gelu_exact(values):
    return jax.nn.gelu(values, approximate=False)

def layer(values, norm_gain, norm_shift, joint_proj, proj_bias, out_proj, up_proj, up_bias, down_proj, out_bias, key_live):
    width = values.shape[1]
    normed1 = low(norm_rows(values, norm_gain[0], norm_shift[0]))
    joint = jnp.dot(normed1, joint_proj, precision=HIGHEST)
    query = low(low_back(joint[:, :width] + proj_bias[0]))
    keys = low(low_back(joint[:, width:2 * width]))
    memory = low(low_back(joint[:, 2 * width:] + proj_bias[1]))
    query_heads = query.reshape(-1, HEADS, DH)
    key_heads = keys.reshape(-1, HEADS, DH)
    memory_heads = memory.reshape(-1, HEADS, DH)
    scores = low_back(jnp.einsum('qhd,khd->hqk', query_heads, key_heads, precision=HIGHEST) * (1.0 / math.sqrt(DH)))
    scores = jnp.where(key_live[None, None, :], scores, NEG)
    attention = low(jax.nn.softmax(scores, axis=-1))
    mixed = jnp.einsum('hqk,khd->qhd', attention, memory_heads, precision=HIGHEST).reshape(-1, width)
    mixed = low(low_back(mixed))
    middle = values + low_back(jnp.dot(mixed, out_proj, precision=HIGHEST) + out_bias[0])
    normed2 = low(norm_rows(middle, norm_gain[1], norm_shift[1]))
    hidden = low(gelu_exact(low_back(jnp.dot(normed2, up_proj, precision=HIGHEST) + up_bias)))
    final = middle + low_back(jnp.dot(hidden, down_proj, precision=HIGHEST) + out_bias[1])
    return final * key_live[:, None].astype(final.dtype)

def reference(patches, col_counts, norm_gain, norm_shift, joint_proj, proj_bias, out_proj, up_proj, up_bias, down_proj, out_bias, cotangent):
    freq_rows = FREQ_ROWS // N_FREQ
    key_ids = jnp.arange(KEYS, dtype=jnp.int32)
    key_group = key_ids // SLOTS
    key_live = live_slots(col_counts, key_ids % SLOTS, key_group // N_TM, key_group % N_TM, freq_rows, COLS_CAP)
    weights = (norm_gain.astype(jnp.float32), norm_shift.astype(jnp.float32), joint_proj.astype(jnp.float32), proj_bias.astype(jnp.float32), out_proj.astype(jnp.float32), up_proj.astype(jnp.float32), up_bias.astype(jnp.float32), down_proj.astype(jnp.float32), out_bias.astype(jnp.float32))

    def forward(values, gain_in, shift_in, joint_in, bias_in, outp_in, up_in, upb_in, down_in, outb_in):
        return layer(values, gain_in, shift_in, joint_in, bias_in, outp_in, up_in, upb_in, down_in, outb_in, key_live)

    def one_clip(sums, clip_pair):
        clip_in, clip_grad = clip_pair
        result, pullback = jax.vjp(forward, clip_in.astype(jnp.float32), weights[0], weights[1], weights[2], weights[3], weights[4], weights[5], weights[6], weights[7], weights[8])
        grads = pullback(clip_grad.astype(jnp.float32))
        new_sums = tuple((running + member for running, member in zip(sums, grads[1:])))
        return (new_sums, (result.astype(jnp.bfloat16), grads[0].astype(jnp.bfloat16)))
    initial = tuple((jnp.zeros_like(member) for member in weights))
    sums, (outputs, grad_inputs) = lax.scan(one_clip, initial, (jnp.moveaxis(patches, 1, 0), jnp.moveaxis(cotangent, 1, 0)))
    return (jnp.moveaxis(outputs, 0, 1), jnp.moveaxis(grad_inputs, 0, 1), sums[0], sums[1], sums[2], sums[3], sums[4], sums[5], sums[6], sums[7], sums[8])
```

```python
import math

import jax
import jax.numpy as jnp
from jax import lax
from jax.experimental import pallas as pl
from jax.experimental.pallas import tpu as pltpu
from jax.sharding import PartitionSpec as P

HEADS = 12
DH = 64
FREQ_ROWS = 12


EPS = 1e-06
NEG = -1000000000.0


def live_slots(col_counts, slot_ids, freq_ids, time_ids, freq_rows, cap_cols):
    table = jnp.arange(col_counts.shape[0], dtype=jnp.int32)
    live_cols = jnp.sum(
        jnp.where(time_ids[:, None] == table[None, :], col_counts[None, :], 0), axis=1
    )
    in_grid = slot_ids < freq_rows * cap_cols
    column_live = slot_ids // freq_rows < live_cols
    extra_live = (time_ids == 0) & (freq_ids == 0)
    return jnp.where(in_grid, column_live, extra_live)


def norm_rows(values, gain, shift):
    centered = values - jnp.mean(values, axis=-1, keepdims=True)
    inverse = lax.rsqrt(jnp.mean(centered * centered, axis=-1, keepdims=True) + EPS)
    return centered * inverse * gain + shift


def gelu_exact(values):
    return jax.nn.gelu(values, approximate=False)


def matmul(left, right):
    return jnp.dot(left, right, preferred_element_type=jnp.float32)


def matmul_tn(left, right):
    return lax.dot_general(
        left, right, (((0,), (0,)), ((), ())), preferred_element_type=jnp.float32
    )


def matmul_nt(left, right):
    return lax.dot_general(
        left, right, (((1,), (1,)), ((), ())), preferred_element_type=jnp.float32
    )


def head_pair(array, offset, lane_width, head_size):
    section = lax.dynamic_slice_in_dim(array, offset, lane_width, 2)
    return section.reshape(section.shape[0], section.shape[1], 2, head_size)


def add_lanes(target, addend, offset):
    current = lax.dynamic_slice_in_dim(target, offset, addend.shape[2], 2)
    return lax.dynamic_update_slice_in_dim(target, current + addend, offset, 2)


def pair_probs(query_pair, key_pair, log_pair, mask, scale):
    scores = (
        jnp.einsum("qchd,kchd->chqk", query_pair, key_pair, preferred_element_type=jnp.float32)
        * scale
        + mask
    )
    return jnp.exp(scores - jnp.transpose(log_pair, (1, 2, 0))[..., None])


def per_device_gathered(
    patches,
    col_counts,
    norm_gain,
    norm_shift,
    joint_proj,
    proj_bias,
    out_proj,
    up_proj,
    up_bias,
    down_proj,
    out_bias,
    cotangent,
):
    slots, clips, width = patches.shape
    row_count = slots * clips
    lane_width = 2 * DH
    pair_count = HEADS // 2
    scale = 1.0 / math.sqrt(DH)
    freq_size = lax.axis_size("freq")
    time_size = lax.axis_size("tm")
    freq_rows = FREQ_ROWS // freq_size
    cap_cols = (slots - 2) // freq_rows
    key_count = slots * freq_size * time_size
    slot_ids = jnp.arange(slots, dtype=jnp.int32)
    own_live = live_slots(
        col_counts,
        slot_ids,
        jnp.full((slots,), lax.axis_index("freq"), jnp.int32),
        jnp.full((slots,), lax.axis_index("tm"), jnp.int32),
        freq_rows,
        cap_cols,
    )
    key_ids = jnp.arange(key_count, dtype=jnp.int32)
    key_group = key_ids // slots
    key_live = live_slots(
        col_counts,
        key_ids % slots,
        key_group // time_size,
        key_group % time_size,
        freq_rows,
        cap_cols,
    )
    key_mask = jnp.where(key_live, 0.0, NEG).astype(jnp.float32)
    row_live = (
        jnp.broadcast_to(own_live[:, None], (slots, clips))
        .reshape(row_count, 1)
        .astype(jnp.float32)
    )
    gain_full = norm_gain.astype(jnp.float32)
    shift_full = norm_shift.astype(jnp.float32)
    bias_full = proj_bias.astype(jnp.float32)
    outb_full = out_bias.astype(jnp.float32)
    upb_full = up_bias.astype(jnp.float32)
    inputs = patches.reshape(row_count, width).astype(jnp.float32)
    normed1, ln1_back = jax.vjp(norm_rows, inputs, gain_full[0], shift_full[0])
    normed1_low = normed1.astype(jnp.bfloat16)
    joint = matmul(normed1_low, joint_proj)
    query_low = (joint[:, :width] + bias_full[0]).astype(jnp.bfloat16)
    keys_low = joint[:, width : 2 * width].astype(jnp.bfloat16)
    memory_low = (joint[:, 2 * width :] + bias_full[1]).astype(jnp.bfloat16)
    query3 = query_low.reshape(slots, clips, width)
    key_value = jnp.concatenate([keys_low, memory_low], axis=1).reshape(slots, clips, 2 * width)
    all_memory = lax.all_gather(key_value, ("freq", "tm"), axis=0, tiled=True)

    def forward_pair(number, state):
        mixed_acc, log_acc = state
        offset = number * lane_width
        query_pair = head_pair(query3, offset, lane_width, DH)
        key_pair = head_pair(all_memory, offset, lane_width, DH)
        value_pair = head_pair(all_memory, width + offset, lane_width, DH)
        scores = (
            jnp.einsum("qchd,kchd->chqk", query_pair, key_pair, preferred_element_type=jnp.float32)
            * scale
            + key_mask
        )
        highest = jnp.max(scores, axis=-1, keepdims=True)
        exponent = jnp.exp(scores - highest)
        summed = jnp.sum(exponent, axis=-1, keepdims=True)
        attention = (exponent / summed).astype(jnp.bfloat16)
        mixed = jnp.einsum(
            "chqk,kchd->qchd", attention, value_pair, preferred_element_type=jnp.float32
        )
        log_pair = jnp.transpose((highest + jnp.log(summed))[..., 0], (2, 0, 1))
        mixed_acc = lax.dynamic_update_slice_in_dim(
            mixed_acc, mixed.reshape(slots, clips, lane_width), offset, 2
        )
        log_acc = lax.dynamic_update_slice_in_dim(log_acc, log_pair, 2 * number, 2)
        return (mixed_acc, log_acc)

    mixed_full, log_rows = lax.fori_loop(
        0,
        pair_count,
        forward_pair,
        (
            jnp.zeros((slots, clips, width), jnp.float32),
            jnp.zeros((slots, clips, HEADS), jnp.float32),
        ),
    )
    mixed_low = mixed_full.reshape(row_count, width).astype(jnp.bfloat16)
    middle = inputs + matmul(mixed_low, out_proj) + outb_full[0]
    normed2, ln2_back = jax.vjp(norm_rows, middle, gain_full[1], shift_full[1])
    normed2_low = normed2.astype(jnp.bfloat16)
    pre_act = matmul(normed2_low, up_proj) + upb_full
    activated, gelu_back = jax.vjp(gelu_exact, pre_act)
    hidden_low = activated.astype(jnp.bfloat16)
    final = middle + matmul(hidden_low, down_proj) + outb_full[1]
    output = (final * row_live).astype(jnp.bfloat16).reshape(slots, clips, width)
    grad_out_rows = cotangent.reshape(row_count, width).astype(jnp.float32) * row_live
    grad_out_low = grad_out_rows.astype(jnp.bfloat16)
    grad_down_part = matmul_tn(hidden_low, grad_out_low)
    grad_outb_mlp = jnp.sum(grad_out_rows, axis=0)
    grad_hidden = matmul_nt(grad_out_low, down_proj)
    grad_pre_low = gelu_back(grad_hidden)[0].astype(jnp.bfloat16)
    grad_up_part = matmul_tn(normed2_low, grad_pre_low)
    grad_upb_part = jnp.sum(grad_pre_low.astype(jnp.float32), axis=0)
    grad_normed2 = matmul_nt(grad_pre_low, up_proj)
    grad_mid_part, grad_gain_mlp, grad_shift_mlp = ln2_back(grad_normed2)
    grad_middle = grad_out_rows + grad_mid_part
    grad_branch = grad_middle.astype(jnp.bfloat16)
    grad_outp_part = matmul_tn(mixed_low, grad_branch)
    grad_outb_attn = jnp.sum(grad_branch.astype(jnp.float32), axis=0)
    grad_mixed_low = matmul_nt(grad_branch, out_proj).astype(jnp.bfloat16)
    grad_mixed3 = grad_mixed_low.reshape(slots, clips, width)

    def query_side(number):
        offset = number * lane_width
        query_pair = head_pair(query3, offset, lane_width, DH)
        grad_pair = head_pair(grad_mixed3, offset, lane_width, DH)
        key_pair = head_pair(all_memory, offset, lane_width, DH)
        value_pair = head_pair(all_memory, width + offset, lane_width, DH)
        log_pair = lax.dynamic_slice_in_dim(log_rows, 2 * number, 2, 2)
        probability = pair_probs(query_pair, key_pair, log_pair, key_mask, scale)
        grad_probs = jnp.einsum(
            "qchd,kchd->chqk", grad_pair, value_pair, preferred_element_type=jnp.float32
        )
        delta = jnp.sum(probability * grad_probs, axis=-1, keepdims=True)
        grad_scores = (probability * (grad_probs - delta)).astype(jnp.bfloat16)
        grad_query = (
            jnp.einsum("chqk,kchd->qchd", grad_scores, key_pair, preferred_element_type=jnp.float32)
            * scale
        )
        return (
            offset,
            query_pair,
            grad_pair,
            probability,
            grad_scores,
            delta,
            grad_query.reshape(slots, clips, lane_width),
        )

    zero_query = jnp.zeros((slots, clips, width), jnp.float32)

    def backward_pair(number, state):
        grad_query_acc, grad_memory = state
        side = query_side(number)
        offset = side[0]
        grad_keys = (
            jnp.einsum("chqk,qchd->kchd", side[4], side[1], preferred_element_type=jnp.float32)
            * scale
        )
        grad_values = jnp.einsum(
            "chqk,qchd->kchd",
            side[3].astype(jnp.bfloat16),
            side[2],
            preferred_element_type=jnp.float32,
        )
        grad_memory = add_lanes(
            grad_memory, grad_keys.reshape(key_count, clips, lane_width), offset
        )
        grad_memory = add_lanes(
            grad_memory, grad_values.reshape(key_count, clips, lane_width), width + offset
        )
        return (add_lanes(grad_query_acc, side[6], offset), grad_memory)

    grad_query_full, grad_memory_all = lax.fori_loop(
        0,
        pair_count,
        backward_pair,
        (zero_query, jnp.zeros((key_count, clips, 2 * width), jnp.float32)),
    )
    grad_memory_own = lax.psum_scatter(
        grad_memory_all, ("freq", "tm"), scatter_dimension=0, tiled=True
    )
    grad_query_low = grad_query_full.reshape(row_count, width).astype(jnp.bfloat16)
    grad_memory_low = grad_memory_own.reshape(row_count, 2 * width).astype(jnp.bfloat16)
    grad_joint = jnp.concatenate([grad_query_low, grad_memory_low], axis=1)
    grad_joint_part = matmul_tn(normed1_low, grad_joint)
    grad_bias_cols = jnp.stack(
        [
            jnp.sum(grad_query_low.astype(jnp.float32), axis=0),
            jnp.sum(grad_memory_low[:, width:].astype(jnp.float32), axis=0),
        ],
        axis=1,
    )
    grad_normed1 = matmul_nt(grad_joint, joint_proj)
    grad_in_part, grad_gain_attn, grad_shift_attn = ln1_back(grad_normed1)
    grad_patches = (grad_middle + grad_in_part).astype(jnp.bfloat16).reshape(slots, clips, width)
    shares = (
        lax.psum_scatter(
            grad_joint_part.astype(jnp.bfloat16), ("freq", "tm"), scatter_dimension=0, tiled=True
        ).astype(jnp.float32),
        lax.psum_scatter(
            grad_bias_cols.astype(jnp.bfloat16), ("freq", "tm"), scatter_dimension=0, tiled=True
        ).astype(jnp.float32),
        lax.psum_scatter(
            grad_outp_part.astype(jnp.bfloat16), ("freq", "tm"), scatter_dimension=0, tiled=True
        ).astype(jnp.float32),
        lax.psum_scatter(
            grad_outb_attn.astype(jnp.bfloat16), ("freq", "tm"), scatter_dimension=0, tiled=True
        ).astype(jnp.float32),
        lax.psum_scatter(
            grad_gain_attn.astype(jnp.bfloat16), ("freq", "tm"), scatter_dimension=0, tiled=True
        ).astype(jnp.float32),
        lax.psum_scatter(
            grad_shift_attn.astype(jnp.bfloat16), ("freq", "tm"), scatter_dimension=0, tiled=True
        ).astype(jnp.float32),
        lax.psum_scatter(
            grad_up_part.astype(jnp.bfloat16), ("freq", "tm"), scatter_dimension=0, tiled=True
        ).astype(jnp.float32),
        lax.psum_scatter(
            grad_upb_part.astype(jnp.bfloat16), ("freq", "tm"), scatter_dimension=0, tiled=True
        ).astype(jnp.float32),
        lax.psum_scatter(
            grad_down_part.astype(jnp.bfloat16), ("freq", "tm"), scatter_dimension=0, tiled=True
        ).astype(jnp.float32),
        lax.psum_scatter(
            grad_outb_mlp.astype(jnp.bfloat16), ("freq", "tm"), scatter_dimension=0, tiled=True
        ).astype(jnp.float32),
        lax.psum_scatter(
            grad_gain_mlp.astype(jnp.bfloat16), ("freq", "tm"), scatter_dimension=0, tiled=True
        ).astype(jnp.float32),
        lax.psum_scatter(
            grad_shift_mlp.astype(jnp.bfloat16), ("freq", "tm"), scatter_dimension=0, tiled=True
        ).astype(jnp.float32),
    )
    summed_all = (
        lax.psum(shares[0].astype(jnp.bfloat16), "dp").astype(jnp.float32),
        lax.psum(shares[1].astype(jnp.bfloat16), "dp").astype(jnp.float32),
        lax.psum(shares[2].astype(jnp.bfloat16), "dp").astype(jnp.float32),
        lax.psum(shares[3].astype(jnp.bfloat16), "dp").astype(jnp.float32),
        lax.psum(shares[4].astype(jnp.bfloat16), "dp").astype(jnp.float32),
        lax.psum(shares[5].astype(jnp.bfloat16), "dp").astype(jnp.float32),
        lax.psum(shares[6].astype(jnp.bfloat16), "dp").astype(jnp.float32),
        lax.psum(shares[7].astype(jnp.bfloat16), "dp").astype(jnp.float32),
        lax.psum(shares[8].astype(jnp.bfloat16), "dp").astype(jnp.float32),
        lax.psum(shares[9].astype(jnp.bfloat16), "dp").astype(jnp.float32),
        lax.psum(shares[10].astype(jnp.bfloat16), "dp").astype(jnp.float32),
        lax.psum(shares[11].astype(jnp.bfloat16), "dp").astype(jnp.float32),
    )
    attn_summed = summed_all[:6]
    mlp_summed = summed_all[6:]
    grad_norm_gain = jnp.stack([attn_summed[4], mlp_summed[4]])
    grad_norm_shift = jnp.stack([attn_summed[5], mlp_summed[5]])
    grad_out_bias = jnp.stack([attn_summed[3], mlp_summed[3]])
    grad_proj_bias = jnp.transpose(attn_summed[1])
    return (
        output,
        grad_patches,
        grad_norm_gain,
        grad_norm_shift,
        attn_summed[0],
        grad_proj_bias,
        attn_summed[2],
        mlp_summed[0],
        mlp_summed[1],
        mlp_summed[2],
        grad_out_bias,
    )


LOG2E = 1.4426950408889634
LANES = 128
F32 = jnp.float32
BF16 = jnp.bfloat16


def attention_forward_kernel(q_ref, k_ref, v_ref, live_ref, o_ref, rn_ref, p_ref, qs, vt, ot, sa, sb):
    tokens = q_ref.shape[0]
    lane = lax.broadcasted_iota(jnp.int32, (tokens, LANES), 1)
    query = q_ref[...].astype(F32) * (1.0 / math.sqrt(DH))
    qs[0:tokens, :] = jnp.where(lane < DH, query, 0.0).astype(BF16)
    qs[tokens : 2 * tokens, :] = jnp.where(lane < DH, 0.0, query).astype(BF16)
    live = live_ref[0:1, :]
    vt[0:LANES, :] = (jnp.transpose(v_ref[...].astype(F32)) * live).astype(BF16)
    vt[LANES : LANES + 16, :] = jnp.broadcast_to(live, (16, tokens)).astype(BF16)

    def scores(head):
        return matmul_nt(k_ref[...], qs[head * tokens : (head + 1) * tokens, :])

    def finish(head, score):
        highest = jnp.max(score, axis=0, keepdims=True)
        weight = jnp.exp2(score * LOG2E - highest * LOG2E).astype(BF16)
        p_ref[0, :, head * tokens : (head + 1) * tokens] = weight
        ot[:, head * tokens : (head + 1) * tokens] = matmul(vt[...], weight)

    sa[...] = scores(0)
    sb[...] = scores(1)
    finish(0, sa[...])
    finish(1, sb[...])
    row = lax.broadcasted_iota(jnp.int32, (LANES, tokens), 0)
    inverse = jnp.where(
        row < DH,
        jnp.broadcast_to(1.0 / ot[LANES : LANES + 1, 0:tokens], (LANES, tokens)),
        jnp.broadcast_to(1.0 / ot[LANES : LANES + 1, tokens : 2 * tokens], (LANES, tokens)),
    )
    mixed = jnp.where(row < DH, ot[0:LANES, 0:tokens], ot[0:LANES, tokens : 2 * tokens]) * inverse
    o_ref[...] = jnp.transpose(mixed).astype(BF16)
    rn_ref[...] = jnp.transpose(inverse)


def attention_forward(query, keys, memory, live_row):
    tokens, width = query.shape
    pairs = width // LANES
    block = pl.BlockSpec((tokens, LANES), lambda pair: (0, pair))
    return pl.pallas_call(
        attention_forward_kernel,
        grid=(pairs,),
        in_specs=[block, block, block, pl.BlockSpec((8, tokens), lambda pair: (0, 0))],
        out_specs=[block, block, pl.BlockSpec((1, tokens, 2 * tokens), lambda pair: (pair, 0, 0))],
        out_shape=[
            jax.ShapeDtypeStruct((tokens, width), BF16),
            jax.ShapeDtypeStruct((tokens, width), F32),
            jax.ShapeDtypeStruct((pairs, tokens, 2 * tokens), BF16),
        ],
        scratch_shapes=[
            pltpu.VMEM((2 * tokens, LANES), BF16),
            pltpu.VMEM((LANES + 16, tokens), BF16),
            pltpu.VMEM((LANES + 16, 2 * tokens), F32),
            pltpu.VMEM((tokens, tokens), F32),
            pltpu.VMEM((tokens, tokens), F32),
        ],
        compiler_params=pltpu.CompilerParams(vmem_limit_bytes=60 << 20),
        cost_estimate=pl.CostEstimate(
            flops=8 * pairs * tokens * tokens * LANES,
            transcendentals=2 * pairs * tokens * tokens,
            bytes_accessed=4 * pairs * tokens * tokens,
        ),
    )(query, keys, memory, live_row)


def attention_backward_kernel(
    q_ref, k_ref, v_ref, o_ref, do_ref, rn_ref, live_ref, keep_ref, p_ref,
    dq_ref, dk_ref, dv_ref, qs, gs, kt, dqt, delta,
):
    tokens = q_ref.shape[0]
    scale = 1.0 / math.sqrt(DH)
    lane = lax.broadcasted_iota(jnp.int32, (tokens, LANES), 1)
    query = q_ref[...].astype(F32) * scale
    qs[0:tokens, :] = jnp.where(lane < DH, query, 0.0).astype(BF16)
    qs[tokens : 2 * tokens, :] = jnp.where(lane < DH, 0.0, query).astype(BF16)
    grad = do_ref[...].astype(F32) * rn_ref[...]
    gs[0:tokens, :] = jnp.where(lane < DH, grad, 0.0).astype(BF16)
    gs[tokens : 2 * tokens, :] = jnp.where(lane < DH, 0.0, grad).astype(BF16)
    kt[...] = (jnp.transpose(k_ref[...].astype(F32)) * (live_ref[0:1, :] * scale)).astype(BF16)
    product = jnp.transpose(grad * o_ref[...].astype(F32))
    for head in range(2):
        total = jnp.sum(product[head * DH : (head + 1) * DH], axis=0, keepdims=True)
        delta[:, head * tokens : (head + 1) * tokens] = jnp.broadcast_to(total, (8, tokens))
    grad_keys = grad_values = None
    for head in range(2):
        span = slice(head * tokens, (head + 1) * tokens)
        weight = p_ref[0, :, span]
        grad_weight = matmul_nt(v_ref[...], gs[span, :])
        grad_score = (weight.astype(F32) * (grad_weight - delta[0:1, span])).astype(BF16)
        dqt[:, span] = matmul(kt[...], grad_score)
        part_values = matmul(weight, gs[span, :])
        part_keys = matmul(grad_score, qs[span, :])
        grad_values = part_values if grad_values is None else grad_values + part_values
        grad_keys = part_keys if grad_keys is None else grad_keys + part_keys
    row = lax.broadcasted_iota(jnp.int32, (LANES, tokens), 0)
    dq_ref[...] = jnp.transpose(
        jnp.where(row < DH, dqt[:, 0:tokens], dqt[:, tokens : 2 * tokens])
    ).astype(BF16)
    keep = keep_ref[...] > 0
    dk_ref[...] = jnp.where(keep, grad_keys, 0.0).astype(BF16)
    dv_ref[...] = jnp.where(keep, grad_values, 0.0).astype(BF16)


def attention_backward(query, keys, memory, mixed, grad_mixed, inverse, live_row, live_lanes, weights):
    tokens, width = query.shape
    pairs = width // LANES
    block = pl.BlockSpec((tokens, LANES), lambda pair: (0, pair))
    return pl.pallas_call(
        attention_backward_kernel,
        grid=(pairs,),
        in_specs=[block] * 6
        + [
            pl.BlockSpec((8, tokens), lambda pair: (0, 0)),
            pl.BlockSpec((tokens, LANES), lambda pair: (0, 0)),
            pl.BlockSpec((1, tokens, 2 * tokens), lambda pair: (pair, 0, 0)),
        ],
        out_specs=[block] * 3,
        out_shape=[jax.ShapeDtypeStruct((tokens, width), BF16)] * 3,
        scratch_shapes=[
            pltpu.VMEM((2 * tokens, LANES), BF16),
            pltpu.VMEM((2 * tokens, LANES), BF16),
            pltpu.VMEM((LANES, tokens), BF16),
            pltpu.VMEM((LANES, 2 * tokens), F32),
            pltpu.VMEM((8, 2 * tokens), F32),
        ],
        compiler_params=pltpu.CompilerParams(vmem_limit_bytes=60 << 20),
        cost_estimate=pl.CostEstimate(
            flops=16 * pairs * tokens * tokens * LANES,
            transcendentals=0,
            bytes_accessed=4 * pairs * tokens * tokens,
        ),
    )(query, keys, memory, mixed, grad_mixed, inverse, live_row, live_lanes, weights)


def per_device(
    patches,
    col_counts,
    norm_gain,
    norm_shift,
    joint_proj,
    proj_bias,
    out_proj,
    up_proj,
    up_bias,
    down_proj,
    out_bias,
    cotangent,
):
    slots, clips, width = patches.shape
    group = ("freq", "tm")
    freq_size = lax.axis_size("freq")
    time_size = lax.axis_size("tm")
    members = freq_size * time_size
    freq_rows = FREQ_ROWS // freq_size
    cap_cols = (slots - 2) // freq_rows
    padded = -(-slots // 16) * 16
    tokens = members * padded

    def to_clip(array):
        blocks = jnp.pad(jnp.transpose(array, (1, 0, 2)), ((0, 0), (0, padded - slots), (0, 0)))
        return lax.all_to_all(blocks, group, 0, 0, tiled=True).reshape(tokens, width)

    def to_slots(array):
        blocks = lax.all_to_all(array.reshape(members, padded, width), group, 0, 0, tiled=True)
        return jnp.transpose(blocks[:, :slots], (1, 0, 2))

    token_ids = jnp.arange(tokens, dtype=jnp.int32)
    block_ids = token_ids // padded
    live = live_slots(
        col_counts,
        token_ids % padded,
        block_ids // time_size,
        block_ids % time_size,
        freq_rows,
        cap_cols,
    ) & (token_ids % padded < slots)
    live_full = live.astype(F32)
    row_live = live_full[:, None]
    live_row = jnp.broadcast_to(live_full[None, :], (8, tokens))
    live_lanes = jnp.broadcast_to(row_live, (tokens, LANES))

    gain_full = norm_gain.astype(F32)
    shift_full = norm_shift.astype(F32)
    bias_full = proj_bias.astype(F32)
    outb_full = out_bias.astype(F32)
    upb_full = up_bias.astype(F32)

    inputs = to_clip(patches).astype(F32)
    grad_out_low = to_clip(cotangent)
    normed1, ln1_back = jax.vjp(norm_rows, inputs, gain_full[0], shift_full[0])
    normed1_low = normed1.astype(BF16)
    joint = matmul(normed1_low, joint_proj)
    query_low = (joint[:, :width] + bias_full[0]).astype(BF16)
    keys_low = joint[:, width : 2 * width].astype(BF16)
    memory_low = (joint[:, 2 * width :] + bias_full[1]).astype(BF16)
    keys_low = jnp.where(row_live > 0, keys_low, keys_low[0:1])
    mixed_low, inverse, weights = attention_forward(query_low, keys_low, memory_low, live_row)

    middle = inputs + matmul(mixed_low, out_proj) + outb_full[0]
    normed2, ln2_back = jax.vjp(norm_rows, middle, gain_full[1], shift_full[1])
    normed2_low = normed2.astype(BF16)
    pre_act = matmul(normed2_low, up_proj) + upb_full
    activated, gelu_back = jax.vjp(gelu_exact, pre_act)
    hidden_low = activated.astype(BF16)
    final = middle + matmul(hidden_low, down_proj) + outb_full[1]
    output = to_slots((final * row_live).astype(BF16))
    grad_out_rows = grad_out_low.astype(F32) * row_live
    grad_out_low = grad_out_rows.astype(BF16)
    grad_down_part = matmul_tn(hidden_low, grad_out_low)
    grad_outb_mlp = jnp.sum(grad_out_rows, axis=0)
    grad_hidden = matmul_nt(grad_out_low, down_proj)
    grad_pre_low = gelu_back(grad_hidden)[0].astype(BF16)
    grad_up_part = matmul_tn(normed2_low, grad_pre_low)
    grad_upb_part = jnp.sum(grad_pre_low.astype(F32), axis=0)
    grad_normed2 = matmul_nt(grad_pre_low, up_proj)
    grad_mid_part, grad_gain_mlp, grad_shift_mlp = ln2_back(grad_normed2)
    grad_middle = grad_out_rows + grad_mid_part
    grad_branch = grad_middle.astype(BF16)
    grad_outp_part = matmul_tn(mixed_low, grad_branch)
    grad_outb_attn = jnp.sum(grad_branch.astype(F32), axis=0)
    grad_mixed_low = matmul_nt(grad_branch, out_proj).astype(BF16)

    grad_query_low, grad_keys_low, grad_values_low = attention_backward(
        query_low, keys_low, memory_low, mixed_low, grad_mixed_low, inverse, live_row, live_lanes, weights
    )
    grad_joint = jnp.concatenate([grad_query_low, grad_keys_low, grad_values_low], axis=1)
    grad_joint_part = matmul_tn(normed1_low, grad_joint)
    grad_normed1 = matmul_nt(grad_joint, joint_proj)
    grad_in_part, grad_gain_attn, grad_shift_attn = ln1_back(grad_normed1)
    grad_patches = to_slots((grad_middle + grad_in_part).astype(BF16))

    def share(part):
        return lax.psum_scatter(part.astype(BF16), group, scatter_dimension=0, tiled=True)

    small = jnp.concatenate(
        [
            part.reshape(members, -1)
            for part in (
                grad_gain_attn,
                grad_gain_mlp,
                grad_shift_attn,
                grad_shift_mlp,
                jnp.sum(grad_query_low.astype(F32), axis=0),
                jnp.sum(grad_values_low.astype(F32), axis=0),
                grad_outb_attn,
                grad_outb_mlp,
                grad_upb_part,
            )
        ],
        axis=1,
    )
    down_sum, up_sum, outp_sum, joint_sum, small_sum = (
        lax.psum(share(part), "dp").astype(F32)
        for part in (grad_down_part, grad_up_part, grad_outp_part, grad_joint_part, small)
    )
    chunk = width // members
    pieces = [small_sum[0, 2 * i * chunk : 2 * (i + 1) * chunk].reshape(2, chunk) for i in range(4)]
    return (
        output,
        grad_patches,
        pieces[0],
        pieces[1],
        joint_sum,
        pieces[2],
        outp_sum,
        up_sum,
        small_sum[0, 8 * chunk :],
        down_sum,
        pieces[3],
    )


def plan(patches, *others):
    members = lax.axis_size("freq") * lax.axis_size("tm")
    if patches.shape[1] == members:
        return per_device(patches, *others)
    return per_device_gathered(patches, *others)


def solution(mesh):
    return jax.shard_map(
        plan,
        mesh=mesh,
        in_specs=(
            P(("freq", "tm"), "dp", None),
            P(),
            P(),
            P(),
            P(),
            P(),
            P(),
            P(),
            P(),
            P(),
            P(),
            P(("freq", "tm"), "dp", None),
        ),
        out_specs=(
            P(("freq", "tm"), "dp", None),
            P(("freq", "tm"), "dp", None),
            P(None, ("freq", "tm")),
            P(None, ("freq", "tm")),
            P(("freq", "tm"), None),
            P(None, ("freq", "tm")),
            P(("freq", "tm"), None),
            P(("freq", "tm"), None),
            P(("freq", "tm")),
            P(("freq", "tm"), None),
            P(None, ("freq", "tm")),
        ),
        check_vma=False,
    )
```

```python
import functools
import math

import jax
import jax.numpy as jnp
from jax import lax
from jax.experimental import pallas as pl
from jax.experimental.pallas import tpu as pltpu
from jax.sharding import PartitionSpec as P

HEADS = 12
DH = 64
FREQ_ROWS = 12


EPS = 1e-06
NEG = -1000000000.0


def live_slots(col_counts, slot_ids, freq_ids, time_ids, freq_rows, cap_cols):
    table = jnp.arange(col_counts.shape[0], dtype=jnp.int32)
    live_cols = jnp.sum(
        jnp.where(time_ids[:, None] == table[None, :], col_counts[None, :], 0), axis=1
    )
    in_grid = slot_ids < freq_rows * cap_cols
    column_live = slot_ids // freq_rows < live_cols
    extra_live = (time_ids == 0) & (freq_ids == 0)
    return jnp.where(in_grid, column_live, extra_live)


def norm_rows(values, gain, shift):
    centered = values - jnp.mean(values, axis=-1, keepdims=True)
    inverse = lax.rsqrt(jnp.mean(centered * centered, axis=-1, keepdims=True) + EPS)
    return centered * inverse * gain + shift


def gelu_exact(values):
    return jax.nn.gelu(values, approximate=False)


def matmul(left, right):
    return jnp.dot(left, right, preferred_element_type=jnp.float32)


def matmul_tn(left, right):
    return lax.dot_general(
        left, right, (((0,), (0,)), ((), ())), preferred_element_type=jnp.float32
    )


def matmul_nt(left, right):
    return lax.dot_general(
        left, right, (((1,), (1,)), ((), ())), preferred_element_type=jnp.float32
    )


def head_pair(array, offset, lane_width, head_size):
    section = lax.dynamic_slice_in_dim(array, offset, lane_width, 2)
    return section.reshape(section.shape[0], section.shape[1], 2, head_size)


def add_lanes(target, addend, offset):
    current = lax.dynamic_slice_in_dim(target, offset, addend.shape[2], 2)
    return lax.dynamic_update_slice_in_dim(target, current + addend, offset, 2)


def pair_probs(query_pair, key_pair, log_pair, mask, scale):
    scores = (
        jnp.einsum("qchd,kchd->chqk", query_pair, key_pair, preferred_element_type=jnp.float32)
        * scale
        + mask
    )
    return jnp.exp(scores - jnp.transpose(log_pair, (1, 2, 0))[..., None])


def per_device_gathered(
    patches,
    col_counts,
    norm_gain,
    norm_shift,
    joint_proj,
    proj_bias,
    out_proj,
    up_proj,
    up_bias,
    down_proj,
    out_bias,
    cotangent,
):
    slots, clips, width = patches.shape
    row_count = slots * clips
    lane_width = 2 * DH
    pair_count = HEADS // 2
    scale = 1.0 / math.sqrt(DH)
    freq_size = lax.axis_size("freq")
    time_size = lax.axis_size("tm")
    freq_rows = FREQ_ROWS // freq_size
    cap_cols = (slots - 2) // freq_rows
    key_count = slots * freq_size * time_size
    slot_ids = jnp.arange(slots, dtype=jnp.int32)
    own_live = live_slots(
        col_counts,
        slot_ids,
        jnp.full((slots,), lax.axis_index("freq"), jnp.int32),
        jnp.full((slots,), lax.axis_index("tm"), jnp.int32),
        freq_rows,
        cap_cols,
    )
    key_ids = jnp.arange(key_count, dtype=jnp.int32)
    key_group = key_ids // slots
    key_live = live_slots(
        col_counts,
        key_ids % slots,
        key_group // time_size,
        key_group % time_size,
        freq_rows,
        cap_cols,
    )
    key_mask = jnp.where(key_live, 0.0, NEG).astype(jnp.float32)
    row_live = (
        jnp.broadcast_to(own_live[:, None], (slots, clips))
        .reshape(row_count, 1)
        .astype(jnp.float32)
    )
    gain_full = norm_gain.astype(jnp.float32)
    shift_full = norm_shift.astype(jnp.float32)
    bias_full = proj_bias.astype(jnp.float32)
    outb_full = out_bias.astype(jnp.float32)
    upb_full = up_bias.astype(jnp.float32)
    inputs = patches.reshape(row_count, width).astype(jnp.float32)
    normed1, ln1_back = jax.vjp(norm_rows, inputs, gain_full[0], shift_full[0])
    normed1_low = normed1.astype(jnp.bfloat16)
    joint = matmul(normed1_low, joint_proj)
    query_low = (joint[:, :width] + bias_full[0]).astype(jnp.bfloat16)
    keys_low = joint[:, width : 2 * width].astype(jnp.bfloat16)
    memory_low = (joint[:, 2 * width :] + bias_full[1]).astype(jnp.bfloat16)
    query3 = query_low.reshape(slots, clips, width)
    key_value = jnp.concatenate([keys_low, memory_low], axis=1).reshape(slots, clips, 2 * width)
    all_memory = lax.all_gather(key_value, ("freq", "tm"), axis=0, tiled=True)

    def forward_pair(number, state):
        mixed_acc, log_acc = state
        offset = number * lane_width
        query_pair = head_pair(query3, offset, lane_width, DH)
        key_pair = head_pair(all_memory, offset, lane_width, DH)
        value_pair = head_pair(all_memory, width + offset, lane_width, DH)
        scores = (
            jnp.einsum("qchd,kchd->chqk", query_pair, key_pair, preferred_element_type=jnp.float32)
            * scale
            + key_mask
        )
        highest = jnp.max(scores, axis=-1, keepdims=True)
        exponent = jnp.exp(scores - highest)
        summed = jnp.sum(exponent, axis=-1, keepdims=True)
        attention = (exponent / summed).astype(jnp.bfloat16)
        mixed = jnp.einsum(
            "chqk,kchd->qchd", attention, value_pair, preferred_element_type=jnp.float32
        )
        log_pair = jnp.transpose((highest + jnp.log(summed))[..., 0], (2, 0, 1))
        mixed_acc = lax.dynamic_update_slice_in_dim(
            mixed_acc, mixed.reshape(slots, clips, lane_width), offset, 2
        )
        log_acc = lax.dynamic_update_slice_in_dim(log_acc, log_pair, 2 * number, 2)
        return (mixed_acc, log_acc)

    mixed_full, log_rows = lax.fori_loop(
        0,
        pair_count,
        forward_pair,
        (
            jnp.zeros((slots, clips, width), jnp.float32),
            jnp.zeros((slots, clips, HEADS), jnp.float32),
        ),
    )
    mixed_low = mixed_full.reshape(row_count, width).astype(jnp.bfloat16)
    middle = inputs + matmul(mixed_low, out_proj) + outb_full[0]
    normed2, ln2_back = jax.vjp(norm_rows, middle, gain_full[1], shift_full[1])
    normed2_low = normed2.astype(jnp.bfloat16)
    pre_act = matmul(normed2_low, up_proj) + upb_full
    activated, gelu_back = jax.vjp(gelu_exact, pre_act)
    hidden_low = activated.astype(jnp.bfloat16)
    final = middle + matmul(hidden_low, down_proj) + outb_full[1]
    output = (final * row_live).astype(jnp.bfloat16).reshape(slots, clips, width)
    grad_out_rows = cotangent.reshape(row_count, width).astype(jnp.float32) * row_live
    grad_out_low = grad_out_rows.astype(jnp.bfloat16)
    grad_down_part = matmul_tn(hidden_low, grad_out_low)
    grad_outb_mlp = jnp.sum(grad_out_rows, axis=0)
    grad_hidden = matmul_nt(grad_out_low, down_proj)
    grad_pre_low = gelu_back(grad_hidden)[0].astype(jnp.bfloat16)
    grad_up_part = matmul_tn(normed2_low, grad_pre_low)
    grad_upb_part = jnp.sum(grad_pre_low.astype(jnp.float32), axis=0)
    grad_normed2 = matmul_nt(grad_pre_low, up_proj)
    grad_mid_part, grad_gain_mlp, grad_shift_mlp = ln2_back(grad_normed2)
    grad_middle = grad_out_rows + grad_mid_part
    grad_branch = grad_middle.astype(jnp.bfloat16)
    grad_outp_part = matmul_tn(mixed_low, grad_branch)
    grad_outb_attn = jnp.sum(grad_branch.astype(jnp.float32), axis=0)
    grad_mixed_low = matmul_nt(grad_branch, out_proj).astype(jnp.bfloat16)
    grad_mixed3 = grad_mixed_low.reshape(slots, clips, width)

    def query_side(number):
        offset = number * lane_width
        query_pair = head_pair(query3, offset, lane_width, DH)
        grad_pair = head_pair(grad_mixed3, offset, lane_width, DH)
        key_pair = head_pair(all_memory, offset, lane_width, DH)
        value_pair = head_pair(all_memory, width + offset, lane_width, DH)
        log_pair = lax.dynamic_slice_in_dim(log_rows, 2 * number, 2, 2)
        probability = pair_probs(query_pair, key_pair, log_pair, key_mask, scale)
        grad_probs = jnp.einsum(
            "qchd,kchd->chqk", grad_pair, value_pair, preferred_element_type=jnp.float32
        )
        delta = jnp.sum(probability * grad_probs, axis=-1, keepdims=True)
        grad_scores = (probability * (grad_probs - delta)).astype(jnp.bfloat16)
        grad_query = (
            jnp.einsum("chqk,kchd->qchd", grad_scores, key_pair, preferred_element_type=jnp.float32)
            * scale
        )
        return (
            offset,
            query_pair,
            grad_pair,
            probability,
            grad_scores,
            delta,
            grad_query.reshape(slots, clips, lane_width),
        )

    zero_query = jnp.zeros((slots, clips, width), jnp.float32)

    def backward_pair(number, state):
        grad_query_acc, grad_memory = state
        side = query_side(number)
        offset = side[0]
        grad_keys = (
            jnp.einsum("chqk,qchd->kchd", side[4], side[1], preferred_element_type=jnp.float32)
            * scale
        )
        grad_values = jnp.einsum(
            "chqk,qchd->kchd",
            side[3].astype(jnp.bfloat16),
            side[2],
            preferred_element_type=jnp.float32,
        )
        grad_memory = add_lanes(
            grad_memory, grad_keys.reshape(key_count, clips, lane_width), offset
        )
        grad_memory = add_lanes(
            grad_memory, grad_values.reshape(key_count, clips, lane_width), width + offset
        )
        return (add_lanes(grad_query_acc, side[6], offset), grad_memory)

    grad_query_full, grad_memory_all = lax.fori_loop(
        0,
        pair_count,
        backward_pair,
        (zero_query, jnp.zeros((key_count, clips, 2 * width), jnp.float32)),
    )
    grad_memory_own = lax.psum_scatter(
        grad_memory_all, ("freq", "tm"), scatter_dimension=0, tiled=True
    )
    grad_query_low = grad_query_full.reshape(row_count, width).astype(jnp.bfloat16)
    grad_memory_low = grad_memory_own.reshape(row_count, 2 * width).astype(jnp.bfloat16)
    grad_joint = jnp.concatenate([grad_query_low, grad_memory_low], axis=1)
    grad_joint_part = matmul_tn(normed1_low, grad_joint)
    grad_bias_cols = jnp.stack(
        [
            jnp.sum(grad_query_low.astype(jnp.float32), axis=0),
            jnp.sum(grad_memory_low[:, width:].astype(jnp.float32), axis=0),
        ],
        axis=1,
    )
    grad_normed1 = matmul_nt(grad_joint, joint_proj)
    grad_in_part, grad_gain_attn, grad_shift_attn = ln1_back(grad_normed1)
    grad_patches = (grad_middle + grad_in_part).astype(jnp.bfloat16).reshape(slots, clips, width)
    shares = (
        lax.psum_scatter(
            grad_joint_part.astype(jnp.bfloat16), ("freq", "tm"), scatter_dimension=0, tiled=True
        ).astype(jnp.float32),
        lax.psum_scatter(
            grad_bias_cols.astype(jnp.bfloat16), ("freq", "tm"), scatter_dimension=0, tiled=True
        ).astype(jnp.float32),
        lax.psum_scatter(
            grad_outp_part.astype(jnp.bfloat16), ("freq", "tm"), scatter_dimension=0, tiled=True
        ).astype(jnp.float32),
        lax.psum_scatter(
            grad_outb_attn.astype(jnp.bfloat16), ("freq", "tm"), scatter_dimension=0, tiled=True
        ).astype(jnp.float32),
        lax.psum_scatter(
            grad_gain_attn.astype(jnp.bfloat16), ("freq", "tm"), scatter_dimension=0, tiled=True
        ).astype(jnp.float32),
        lax.psum_scatter(
            grad_shift_attn.astype(jnp.bfloat16), ("freq", "tm"), scatter_dimension=0, tiled=True
        ).astype(jnp.float32),
        lax.psum_scatter(
            grad_up_part.astype(jnp.bfloat16), ("freq", "tm"), scatter_dimension=0, tiled=True
        ).astype(jnp.float32),
        lax.psum_scatter(
            grad_upb_part.astype(jnp.bfloat16), ("freq", "tm"), scatter_dimension=0, tiled=True
        ).astype(jnp.float32),
        lax.psum_scatter(
            grad_down_part.astype(jnp.bfloat16), ("freq", "tm"), scatter_dimension=0, tiled=True
        ).astype(jnp.float32),
        lax.psum_scatter(
            grad_outb_mlp.astype(jnp.bfloat16), ("freq", "tm"), scatter_dimension=0, tiled=True
        ).astype(jnp.float32),
        lax.psum_scatter(
            grad_gain_mlp.astype(jnp.bfloat16), ("freq", "tm"), scatter_dimension=0, tiled=True
        ).astype(jnp.float32),
        lax.psum_scatter(
            grad_shift_mlp.astype(jnp.bfloat16), ("freq", "tm"), scatter_dimension=0, tiled=True
        ).astype(jnp.float32),
    )
    summed_all = (
        lax.psum(shares[0].astype(jnp.bfloat16), "dp").astype(jnp.float32),
        lax.psum(shares[1].astype(jnp.bfloat16), "dp").astype(jnp.float32),
        lax.psum(shares[2].astype(jnp.bfloat16), "dp").astype(jnp.float32),
        lax.psum(shares[3].astype(jnp.bfloat16), "dp").astype(jnp.float32),
        lax.psum(shares[4].astype(jnp.bfloat16), "dp").astype(jnp.float32),
        lax.psum(shares[5].astype(jnp.bfloat16), "dp").astype(jnp.float32),
        lax.psum(shares[6].astype(jnp.bfloat16), "dp").astype(jnp.float32),
        lax.psum(shares[7].astype(jnp.bfloat16), "dp").astype(jnp.float32),
        lax.psum(shares[8].astype(jnp.bfloat16), "dp").astype(jnp.float32),
        lax.psum(shares[9].astype(jnp.bfloat16), "dp").astype(jnp.float32),
        lax.psum(shares[10].astype(jnp.bfloat16), "dp").astype(jnp.float32),
        lax.psum(shares[11].astype(jnp.bfloat16), "dp").astype(jnp.float32),
    )
    attn_summed = summed_all[:6]
    mlp_summed = summed_all[6:]
    grad_norm_gain = jnp.stack([attn_summed[4], mlp_summed[4]])
    grad_norm_shift = jnp.stack([attn_summed[5], mlp_summed[5]])
    grad_out_bias = jnp.stack([attn_summed[3], mlp_summed[3]])
    grad_proj_bias = jnp.transpose(attn_summed[1])
    return (
        output,
        grad_patches,
        grad_norm_gain,
        grad_norm_shift,
        attn_summed[0],
        grad_proj_bias,
        attn_summed[2],
        mlp_summed[0],
        mlp_summed[1],
        mlp_summed[2],
        grad_out_bias,
    )


LOG2E = 1.4426950408889634
LANES = 128
F32 = jnp.float32
BF16 = jnp.bfloat16
VMEM_LIMIT = 62 << 20
SAFE_RANGE = 100.0
COLLECT_FLOPS = 40 * 10**9


def normalize(values):
    centered = values - jnp.mean(values, axis=-1, keepdims=True)
    inverse = lax.rsqrt(jnp.mean(centered * centered, axis=-1, keepdims=True) + EPS)
    return centered * inverse, inverse


def norm_back(normed, inverse, incoming, gain):
    scaled = incoming * gain
    mean = jnp.mean(scaled, axis=-1, keepdims=True)
    slope = jnp.mean(scaled * normed, axis=-1, keepdims=True)
    return (scaled - mean - normed * slope) * inverse


def column_sum(values):
    return jnp.sum(values, axis=0, keepdims=True)


def project_kernel(x_ref, live_ref, w_ref, vec_ref, n_ref, q_ref, k_ref, v_ref, first_key):
    width = x_ref.shape[1]
    normed, _ = normalize(x_ref[...].astype(F32))
    low = (normed * vec_ref[0:1, :] + vec_ref[1:2, :]).astype(BF16)
    n_ref[...] = low
    q_ref[...] = (matmul(low, w_ref[:, 0:width]) + vec_ref[2:3, :]).astype(BF16)
    keys = matmul(low, w_ref[:, width : 2 * width]).astype(BF16).astype(F32)

    @pl.when(pl.program_id(0) == 0)
    def _():
        first_key[...] = jnp.broadcast_to(keys[0:1, :], first_key.shape)

    k_ref[...] = jnp.where(live_ref[:, 0:1] > 0, keys, first_key[0:1, :]).astype(BF16)
    v_ref[...] = (matmul(low, w_ref[:, 2 * width : 3 * width]) + vec_ref[3:4, :]).astype(BF16)


def project(inputs, live_lanes, joint_proj, vectors, steps=4):
    tokens, width = inputs.shape
    rows = tokens // steps
    block = pl.BlockSpec((rows, width), lambda step: (step, 0))
    return pl.pallas_call(
        project_kernel,
        grid=(steps,),
        in_specs=[
            block,
            pl.BlockSpec((rows, LANES), lambda step: (step, 0)),
            pl.BlockSpec((width, 3 * width), lambda step: (0, 0), pipeline_mode=pl.Buffered(1)),
            pl.BlockSpec((8, width), lambda step: (0, 0)),
        ],
        out_specs=[block] * 4,
        out_shape=[jax.ShapeDtypeStruct((tokens, width), BF16)] * 4,
        scratch_shapes=[pltpu.VMEM((8, width), F32)],
        compiler_params=pltpu.CompilerParams(vmem_limit_bytes=VMEM_LIMIT),
        cost_estimate=pl.CostEstimate(
            flops=6 * tokens * width * width, transcendentals=tokens, bytes_accessed=10 * tokens * width
        ),
    )(inputs, live_lanes, joint_proj, vectors)


def attention_forward_kernel(q_ref, k_ref, v_ref, live_ref, o_ref, rn_ref, p_ref, qs, vt, ot, sa):
    tokens = q_ref.shape[0]
    lane = lax.broadcasted_iota(jnp.int32, (tokens, LANES), 1)
    query = q_ref[...].astype(F32) * (1.0 / math.sqrt(DH))
    keys = k_ref[...].astype(F32)
    qs[0:tokens, :] = jnp.where(lane < DH, query, 0.0).astype(BF16)
    qs[tokens : 2 * tokens, :] = jnp.where(lane < DH, 0.0, query).astype(BF16)
    live = live_ref[0:1, :]
    vt[0:LANES, :] = (jnp.transpose(v_ref[...].astype(F32)) * live).astype(BF16)
    vt[LANES : LANES + 16, :] = jnp.broadcast_to(live, (16, tokens)).astype(BF16)

    def largest(values, head):
        squares = jnp.where((lane < DH) == (head == 0), values * values, 0.0)
        return jnp.max(jnp.sum(squares, axis=1, keepdims=True))

    limit = (SAFE_RANGE / LOG2E) ** 2
    bound = jnp.maximum(
        largest(query, 0) * largest(keys, 0), largest(query, 1) * largest(keys, 1)
    )
    bounded = bound <= limit

    def finish(span, weight):
        p_ref[0, :, span] = weight
        ot[:, span] = matmul(vt[...], weight)

    @pl.when(bounded)
    def _():
        for head in range(2):
            span = slice(head * tokens, (head + 1) * tokens)
            finish(span, jnp.exp2(matmul_nt(k_ref[...], qs[span, :]) * LOG2E).astype(BF16))

    @pl.when(jnp.logical_not(bounded))
    def _():
        for head in range(2):
            for start in range(0, tokens, sa.shape[1]):
                span = slice(head * tokens + start, head * tokens + start + sa.shape[1])
                sa[...] = matmul_nt(k_ref[...], qs[span, :])
                score = sa[...]
                highest = jnp.max(score, axis=0, keepdims=True)
                finish(span, jnp.exp2(score * LOG2E - highest * LOG2E).astype(BF16))

    row = lax.broadcasted_iota(jnp.int32, (LANES, tokens), 0)
    inverse = jnp.where(
        row < DH,
        jnp.broadcast_to(1.0 / ot[LANES : LANES + 1, 0:tokens], (LANES, tokens)),
        jnp.broadcast_to(1.0 / ot[LANES : LANES + 1, tokens : 2 * tokens], (LANES, tokens)),
    )
    mixed = jnp.where(row < DH, ot[0:LANES, 0:tokens], ot[0:LANES, tokens : 2 * tokens]) * inverse
    o_ref[...] = jnp.transpose(mixed).astype(BF16)
    rn_ref[...] = jnp.transpose(inverse)


def attention_forward(query, keys, memory, live_row):
    tokens, width = query.shape
    pairs = width // LANES
    block = pl.BlockSpec((tokens, LANES), lambda pair: (0, pair))
    return pl.pallas_call(
        attention_forward_kernel,
        grid=(pairs,),
        in_specs=[block, block, block, pl.BlockSpec((8, tokens), lambda pair: (0, 0))],
        out_specs=[block, block, pl.BlockSpec((1, tokens, 2 * tokens), lambda pair: (pair, 0, 0))],
        out_shape=[
            jax.ShapeDtypeStruct((tokens, width), BF16),
            jax.ShapeDtypeStruct((tokens, width), F32),
            jax.ShapeDtypeStruct((pairs, tokens, 2 * tokens), BF16),
        ],
        scratch_shapes=[
            pltpu.VMEM((2 * tokens, LANES), BF16),
            pltpu.VMEM((LANES + 16, tokens), BF16),
            pltpu.VMEM((LANES + 16, 2 * tokens), F32),
            pltpu.VMEM((tokens, LANES), F32),
        ],
        compiler_params=pltpu.CompilerParams(vmem_limit_bytes=VMEM_LIMIT),
        cost_estimate=pl.CostEstimate(
            flops=8 * pairs * tokens * tokens * LANES,
            transcendentals=2 * pairs * tokens * tokens,
            bytes_accessed=4 * pairs * tokens * tokens,
        ),
    )(query, keys, memory, live_row)


def attention_backward_kernel(
    q_ref, k_ref, v_ref, o_ref, do_ref, rn_ref, live_ref, keep_ref, p_ref, n_ref, wq_ref, wk_ref, wv_ref,
    x_ref, res_ref, vec_ref, sums_ref, half_ref,
    kept_ref, sent_ref, dx_ref, qs, gs, kt, dqt, delta, dj, dn, vecs,
):
    tokens = q_ref.shape[0]
    scale = 1.0 / math.sqrt(DH)
    lane = lax.broadcasted_iota(jnp.int32, (tokens, LANES), 1)
    query = q_ref[...].astype(F32) * scale
    qs[0:tokens, :] = jnp.where(lane < DH, query, 0.0).astype(BF16)
    qs[tokens : 2 * tokens, :] = jnp.where(lane < DH, 0.0, query).astype(BF16)
    grad = do_ref[...].astype(F32) * rn_ref[...]
    gs[0:tokens, :] = jnp.where(lane < DH, grad, 0.0).astype(BF16)
    gs[tokens : 2 * tokens, :] = jnp.where(lane < DH, 0.0, grad).astype(BF16)
    kt[...] = (jnp.transpose(k_ref[...].astype(F32)) * (live_ref[0:1, :] * scale)).astype(BF16)
    product = jnp.transpose(grad * o_ref[...].astype(F32))
    for head in range(2):
        total = column_sum(product[head * DH : (head + 1) * DH])
        delta[:, head * tokens : (head + 1) * tokens] = jnp.broadcast_to(total, (8, tokens))
    grad_keys = grad_values = None
    for head in range(2):
        span = slice(head * tokens, (head + 1) * tokens)
        weight = p_ref[0, :, span]
        grad_weight = matmul_nt(v_ref[...], gs[span, :])
        grad_score = (weight.astype(F32) * (grad_weight - delta[0:1, span])).astype(BF16)
        dqt[:, span] = matmul(kt[...], grad_score)
        part_values = matmul(weight, gs[span, :])
        part_keys = matmul(grad_score, qs[span, :])
        grad_values = part_values if grad_values is None else grad_values + part_values
        grad_keys = part_keys if grad_keys is None else grad_keys + part_keys
    row = lax.broadcasted_iota(jnp.int32, (LANES, tokens), 0)
    grad_query = jnp.transpose(jnp.where(row < DH, dqt[:, 0:tokens], dqt[:, tokens : 2 * tokens]))
    keep = keep_ref[...] > 0
    dj[:, 0:LANES] = grad_query.astype(BF16)
    dj[:, LANES : 2 * LANES] = jnp.where(keep, grad_keys, 0.0).astype(BF16)
    dj[:, 2 * LANES : 3 * LANES] = jnp.where(keep, grad_values, 0.0).astype(BF16)
    joint = dj[...]
    grad_weights = matmul_tn(n_ref[...], joint).astype(BF16)
    half = grad_weights.shape[0] // 2
    first = half_ref[0] == 0
    columns = pl.ds(pl.multiple_of(pl.program_id(0) * (3 * LANES), LANES), 3 * LANES)
    kept_ref[:, columns] = jnp.where(first, grad_weights[:half], grad_weights[half:])
    sent_ref[:, columns] = jnp.where(first, grad_weights[half:], grad_weights[:half])
    sums = column_sum(joint.astype(F32))
    columns = pl.ds(pl.multiple_of(pl.program_id(0) * LANES, LANES), LANES)
    vecs[2:3, columns] = sums[:, 0:LANES]
    vecs[3:4, columns] = sums[:, 2 * LANES : 3 * LANES]
    weights = jnp.concatenate([wq_ref[...], wk_ref[...], wv_ref[...]], axis=1)
    grad_normed = matmul_nt(joint, weights)

    @pl.when(pl.program_id(0) == 0)
    def _():
        dn[...] = grad_normed

    @pl.when(pl.program_id(0) > 0)
    def _():
        dn[...] += grad_normed

    @pl.when(pl.program_id(0) == pl.num_programs(0) - 1)
    def _():
        vecs[0:2, :] = jnp.zeros((2, vecs.shape[1]), F32)
        vecs[4:8, :] = sums_ref[0:4, :]
        rows = 2 * LANES if tokens % (2 * LANES) == 0 else LANES

        def chunk(index, _):
            span = pl.ds(pl.multiple_of(index * rows, rows), rows)
            normed, inverse = normalize(x_ref[span, :].astype(F32))
            incoming = dn[span, :]
            vecs[0:1, :] += column_sum(incoming * normed)
            vecs[1:2, :] += column_sum(incoming)
            back = norm_back(normed, inverse, incoming, vec_ref[0:1, :])
            dx_ref[span, :] = (res_ref[span, :].astype(F32) + back).astype(BF16)
            return 0

        lax.fori_loop(0, tokens // rows, chunk, 0)
        turned = jnp.transpose(jnp.concatenate([vecs[...]] * (LANES // 8), axis=0)).astype(BF16)
        tail = kept_ref.shape[1] - LANES
        kept_ref[:, tail:] = jnp.where(first, turned[:half], turned[half:])
        sent_ref[:, tail:] = jnp.where(first, turned[half:], turned[:half])


def attention_backward(
    query, keys, memory, mixed, grad_mixed, inverse, live_row, live_lanes, weights, normed, joint_proj,
    inputs, residual, vectors, vector_grads, own_half,
):
    tokens, width = query.shape
    pairs = width // LANES
    block = pl.BlockSpec((tokens, LANES), lambda pair: (0, pair))
    once = pl.Buffered(1)

    def fixed(rows, columns):
        return pl.BlockSpec((rows, columns), lambda pair: (0, 0), pipeline_mode=once)

    def columns(part):
        return pl.BlockSpec((width, LANES), lambda pair: (0, part * pairs + pair))

    return pl.pallas_call(
        attention_backward_kernel,
        grid=(pairs,),
        in_specs=[block] * 6
        + [
            fixed(8, tokens),
            fixed(tokens, LANES),
            pl.BlockSpec((1, tokens, 2 * tokens), lambda pair: (pair, 0, 0)),
            fixed(tokens, width),
            columns(0),
            columns(1),
            columns(2),
            fixed(tokens, width),
            fixed(tokens, width),
            fixed(8, width),
            fixed(8, width),
            pl.BlockSpec(memory_space=pltpu.SMEM),
        ],
        out_specs=[fixed(width // 2, 3 * width + LANES), fixed(width // 2, 3 * width + LANES), fixed(tokens, width)],
        out_shape=[
            jax.ShapeDtypeStruct((width // 2, 3 * width + LANES), BF16),
            jax.ShapeDtypeStruct((width // 2, 3 * width + LANES), BF16),
            jax.ShapeDtypeStruct((tokens, width), BF16),
        ],
        scratch_shapes=[
            pltpu.VMEM((2 * tokens, LANES), BF16),
            pltpu.VMEM((2 * tokens, LANES), BF16),
            pltpu.VMEM((LANES, tokens), BF16),
            pltpu.VMEM((LANES, 2 * tokens), F32),
            pltpu.VMEM((8, 2 * tokens), F32),
            pltpu.VMEM((tokens, 3 * LANES), BF16),
            pltpu.VMEM((tokens, width), F32),
            pltpu.VMEM((8, width), F32),
        ],
        compiler_params=pltpu.CompilerParams(vmem_limit_bytes=VMEM_LIMIT),
        cost_estimate=pl.CostEstimate(
            flops=16 * pairs * tokens * tokens * LANES,
            transcendentals=0,
            bytes_accessed=4 * pairs * tokens * tokens,
        ),
    )(
        query, keys, memory, mixed, grad_mixed, inverse, live_row, live_lanes, weights, normed,
        joint_proj, joint_proj, joint_proj, inputs, residual, vectors, vector_grads,
        own_half,
    )


def feed_forward_kernel(
    x_ref, mixed_ref, cot_ref, live_ref, wo_ref, vec_ref, up_ref, down_ref, bias_ref,
    out_ref, branch_ref, gm_ref, packed_ref, ds_ref,
    normed, grad_out, middle, acc, acc_grad, hidden, grad_pre, down_buf, up_buf, down_sem, up_sem,
):
    step = pl.program_id(0)
    last = pl.num_programs(0) - 1
    tokens, width = x_ref.shape
    units = up_ref.shape[1]
    rows = tokens // 4
    block = tokens // out_ref.shape[0]

    @pl.when(step == 0)
    def _():
        def chunk(index, _):
            span = pl.ds(pl.multiple_of(index * rows, 32), rows)
            values = x_ref[span, :].astype(F32) + matmul(mixed_ref[span, :], wo_ref[...]) + vec_ref[2:3, :]
            middle[span, :] = values
            acc[span, :] = values + vec_ref[3:4, :]
            unit, _ = normalize(values)
            normed[span, :] = (unit * vec_ref[0:1, :] + vec_ref[1:2, :]).astype(BF16)
            grad_out[span, :] = (cot_ref[span, :].astype(F32) * live_ref[span, 0:1]).astype(BF16)
            acc_grad[span, :] = jnp.zeros((rows, width), F32)
            return 0

        lax.fori_loop(0, 4, chunk, 0)

    up = up_ref[...]
    down = down_ref[...]
    grad_bias = jnp.zeros((1, units), F32)
    half = tokens // 2
    for start in (0, half):
        span = slice(start, start + half)
        pre_act = matmul(normed[span, :], up) + bias_ref[0:1, :]
        grad_hidden = matmul_nt(grad_out[span, :], down)
        cumulative = 0.5 + 0.5 * lax.erf(pre_act * math.sqrt(0.5))
        density = jnp.exp2(pre_act * pre_act * (-0.5 * LOG2E)) * (1.0 / math.sqrt(2.0 * math.pi))
        low = (pre_act * cumulative).astype(BF16)
        grad_low = (grad_hidden * (cumulative + pre_act * density)).astype(BF16)
        grad_bias = grad_bias + column_sum(grad_low.astype(F32))
        hidden[span, :] = low
        grad_pre[span, :] = grad_low
        acc[span, :] += matmul(low, down)
        acc_grad[span, :] += matmul_nt(grad_low, up)
    slot = lax.rem(step, 2)
    _, cuts, quarters, share, _ = down_buf.shape
    own = units // cuts
    for cut in range(cuts):
        sums = jnp.broadcast_to(grad_bias[:, cut * own : (cut + 1) * own], (16, own)).astype(BF16)
        out_ref[step * cuts + cut, block + share : block + share + 16, 0:own] = sums
        out_ref[step * cuts + cut, block + share : block + share + 16, own:width] = jnp.zeros((16, width - own), BF16)

    def copies(at, slot):
        return (
            pltpu.make_async_copy(
                down_buf.at[slot], packed_ref.at[pl.ds(at * cuts, cuts), pl.ds(0, quarters)], down_sem.at[slot]
            ),
            pltpu.make_async_copy(up_buf.at[slot], packed_ref.at[:, quarters + at], up_sem.at[slot]),
        )

    @pl.when(step >= 2)
    def _():
        for copy in copies(step - 2, slot):
            copy.wait()

    grad_down = matmul_tn(hidden[...], grad_out[...]).astype(BF16)
    for cut in range(cuts):
        for quarter in range(quarters):
            base = (cut * quarters + quarter) * share
            down_buf[slot, cut, quarter] = grad_down[base : base + share]
    grad_up = matmul_tn(normed[...], grad_pre[...]).astype(BF16)
    for member in range(width // share):
        up_buf[slot, member] = grad_up[member * share : (member + 1) * share]
    for copy in copies(step, slot):
        copy.start()

    @pl.when(step == last)
    def _():
        ds_ref[...] = jnp.zeros_like(ds_ref)

        def chunk(index, _):
            span = pl.ds(pl.multiple_of(index * rows, 32), rows)
            final = (acc[span, :] * live_ref[span, 0:1]).astype(BF16)
            for part in range(rows // block):
                out_ref[index * (rows // block) + part, 0:block, :] = final[part * block : (part + 1) * block]
            unit, inverse = normalize(middle[span, :])
            incoming = acc_grad[span, :]
            start = grad_out[span, :].astype(F32)
            branch = (start + norm_back(unit, inverse, incoming, vec_ref[0:1, :])).astype(BF16)
            branch_ref[span, :] = branch
            gm_ref[span, :] = matmul_nt(branch, wo_ref[...]).astype(BF16)
            ds_ref[0:1, :] += column_sum(incoming * unit)
            ds_ref[1:2, :] += column_sum(incoming)
            ds_ref[2:3, :] += column_sum(branch.astype(F32))
            ds_ref[3:4, :] += column_sum(start)
            return 0

        lax.fori_loop(0, 4, chunk, 0)
        grad_outp = matmul_tn(mixed_ref[...], branch_ref[...]).astype(BF16)
        for member in range(width // share):
            out_ref[member, block : block + share, :] = grad_outp[member * share : (member + 1) * share]
        for copy in copies(step - 1, 1 - slot):
            copy.wait()
        for copy in copies(step, slot):
            copy.wait()


def feed_forward(inputs, mixed, cotangent, live_lanes, out_proj, vectors, up_proj, up_bias, down_proj, members):
    tokens, width = inputs.shape
    hidden_units = up_proj.shape[1]
    steps = hidden_units // width
    share = width // members
    cuts = members // steps
    quarters = hidden_units // members // share
    once = pl.Buffered(1)

    def fixed(rows, columns):
        return pl.BlockSpec((rows, columns), lambda step: (0, 0), pipeline_mode=once)

    return pl.pallas_call(
        feed_forward_kernel,
        grid=(steps,),
        in_specs=[
            fixed(tokens, width),
            fixed(tokens, width),
            fixed(tokens, width),
            fixed(tokens, LANES),
            fixed(width, width),
            fixed(8, width),
            pl.BlockSpec((width, width), lambda step: (0, step)),
            pl.BlockSpec((width, width), lambda step: (step, 0)),
            pl.BlockSpec((8, width), lambda step: (0, step)),
        ],
        out_specs=[
            pl.BlockSpec((members, tokens // members + share + 16, width), lambda step: (0, 0, 0), pipeline_mode=once),
            fixed(tokens, width),
            fixed(tokens, width),
            pl.BlockSpec(memory_space=pl.ANY),
            fixed(8, width),
        ],
        out_shape=[
            jax.ShapeDtypeStruct((members, tokens // members + share + 16, width), BF16),
            jax.ShapeDtypeStruct((tokens, width), BF16),
            jax.ShapeDtypeStruct((tokens, width), BF16),
            jax.ShapeDtypeStruct((members, quarters + steps, share, width), BF16),
            jax.ShapeDtypeStruct((8, width), F32),
        ],
        scratch_shapes=[
            pltpu.VMEM((tokens, width), BF16),
            pltpu.VMEM((tokens, width), BF16),
            pltpu.VMEM((tokens, width), F32),
            pltpu.VMEM((tokens, width), F32),
            pltpu.VMEM((tokens, width), F32),
            pltpu.VMEM((tokens, width), BF16),
            pltpu.VMEM((tokens, width), BF16),
            pltpu.VMEM((2, cuts, quarters, share, width), BF16),
            pltpu.VMEM((2, members, share, width), BF16),
            pltpu.SemaphoreType.DMA((2,)),
            pltpu.SemaphoreType.DMA((2,)),
        ],
        compiler_params=pltpu.CompilerParams(vmem_limit_bytes=VMEM_LIMIT),
        cost_estimate=pl.CostEstimate(
            flops=12 * tokens * width * hidden_units + 6 * tokens * width * width,
            transcendentals=2 * tokens * hidden_units,
            bytes_accessed=12 * tokens * width + 8 * width * hidden_units,
        ),
    )(inputs, mixed, cotangent, live_lanes, out_proj, vectors, up_proj, down_proj, up_bias)


def collect_joint_kernel(own_ref, *refs):
    pieces, (joint_ref, gain_ref, shift_ref, bias_ref, branch_ref, columns) = refs[:-6], refs[-6:]
    rows = pieces[0].shape[0]
    width = joint_ref.shape[1] // 3
    own = own_ref[0]
    columns[...] = jnp.zeros_like(columns)
    for place in range(len(pieces)):
        piece = pieces[place][...]
        for other in range(1, len(pieces)):
            piece = jnp.where(own == other, pieces[place ^ other][...], piece)
        piece = piece.astype(F32)
        span = slice(place * rows, (place + 1) * rows)
        for pair in range(width // LANES):
            for part in range(3):
                at = (pair * 3 + part) * LANES
                to = part * width + pair * LANES
                joint_ref[span, to : to + LANES] = piece[:, at : at + LANES]
        columns[span, :] = piece[:, 3 * width :]
    turned = jnp.transpose(columns[...])
    share = gain_ref.shape[1]
    gain_ref[0:1, :] = turned[0:1, 0:share]
    gain_ref[1:2, :] = turned[4:5, 0:share]
    shift_ref[0:1, :] = turned[1:2, 0:share]
    shift_ref[1:2, :] = turned[5:6, 0:share]
    bias_ref[...] = turned[2:4, 0:share]
    branch_ref[...] = turned[6:8, 0:share]


def collect_joint(own, pieces, share):
    width = (pieces[0].shape[1] - LANES) // 3
    vmem = pl.BlockSpec(memory_space=pltpu.VMEM)
    return pl.pallas_call(
        collect_joint_kernel,
        in_specs=[pl.BlockSpec(memory_space=pltpu.SMEM)] + [vmem] * len(pieces),
        out_specs=[vmem] * 5,
        out_shape=[jax.ShapeDtypeStruct((share, 3 * width), F32)] + [jax.ShapeDtypeStruct((2, share), F32)] * 4,
        scratch_shapes=[pltpu.VMEM((LANES, LANES), F32)],
    )(own, *pieces)


def collect_mlp_kernel(rows_ref, sums_ref, down_ref, up_ref, outp_ref, bias_ref):
    own, width = down_ref.shape
    share = outp_ref.shape[0]
    down_ref[...] = rows_ref[0:own, :].astype(F32)
    for part in range(own // share):
        rows = slice(own + part * share, own + (part + 1) * share)
        up_ref[:, part * width : (part + 1) * width] = rows_ref[rows, :].astype(F32)
    outp_ref[...] = sums_ref[0:share, :].astype(F32)
    bias_ref[...] = sums_ref[share : share + 16, 0:own].astype(F32)[0:1, :]


def collect_mlp(rows, sums, share):
    own, width = rows.shape[0] // 2, rows.shape[1]
    vmem = pl.BlockSpec(memory_space=pltpu.VMEM)
    return pl.pallas_call(
        collect_mlp_kernel,
        in_specs=[vmem] * 2,
        out_specs=[vmem] * 4,
        out_shape=[
            jax.ShapeDtypeStruct((own, width), F32),
            jax.ShapeDtypeStruct((share, own // share * width), F32),
            jax.ShapeDtypeStruct((share, width), F32),
            jax.ShapeDtypeStruct((1, own), F32),
        ],
        cost_estimate=pl.CostEstimate(flops=COLLECT_FLOPS, transcendentals=0, bytes_accessed=4 * rows.size),
    )(rows, sums)


def per_device(
    patches,
    col_counts,
    norm_gain,
    norm_shift,
    joint_proj,
    proj_bias,
    out_proj,
    up_proj,
    up_bias,
    down_proj,
    out_bias,
    cotangent,
):
    slots, clips, width = patches.shape
    group = ("freq", "tm")
    freq_size = lax.axis_size("freq")
    time_size = lax.axis_size("tm")
    groups = lax.axis_size("dp")
    members = freq_size * time_size
    freq_rows = FREQ_ROWS // freq_size
    cap_cols = (slots - 2) // freq_rows
    padded = -(-slots // 16) * 16
    tokens = members * padded
    pairs = width // LANES
    share = width // members
    hidden_units = up_proj.shape[1]

    def to_clip(array):
        blocks = jnp.pad(jnp.transpose(array, (1, 0, 2)), ((0, 0), (0, padded - slots), (0, 0)))
        return lax.all_to_all(blocks, group, 0, 0, tiled=True).reshape(tokens, width)

    def to_slots(array):
        blocks = lax.all_to_all(array.reshape(members, padded, width), group, 0, 0, tiled=True)
        return jnp.transpose(blocks[:, :slots], (1, 0, 2))

    token_ids = jnp.arange(tokens, dtype=jnp.int32)
    block_ids = token_ids // padded
    live = live_slots(
        col_counts,
        token_ids % padded,
        block_ids // time_size,
        block_ids % time_size,
        freq_rows,
        cap_cols,
    ) & (token_ids % padded < slots)
    live_full = live.astype(F32)
    live_row = jnp.broadcast_to(live_full[None, :], (8, tokens))
    live_lanes = jnp.broadcast_to(live_full[:, None], (tokens, LANES))

    def rows_of(*vectors):
        stacked = jnp.stack(vectors).astype(F32)
        return jnp.pad(stacked, ((0, 8 - len(vectors)), (0, 0)))

    vectors1 = rows_of(norm_gain[0], norm_shift[0], proj_bias[0], proj_bias[1])
    vectors2 = rows_of(norm_gain[1], norm_shift[1], out_bias[0], out_bias[1])
    bias_rows = jnp.broadcast_to(up_bias.astype(F32)[None, :], (8, hidden_units))

    inputs = to_clip(patches)
    cot = to_clip(cotangent)
    normed1, query, keys, memory = project(inputs, live_lanes, joint_proj, vectors1)
    mixed, inverse, weights = attention_forward(query, keys, memory, live_row)
    blocks, branch, grad_mixed, packed, vector_grads = feed_forward(
        inputs, mixed, cot, live_lanes, out_proj, vectors2, up_proj, bias_rows, down_proj, members
    )
    own = hidden_units // members
    mlp_rows = lax.psum_scatter(packed.reshape(members, 2 * own, width), group, scatter_dimension=0, tiled=True)[0]
    moved = lax.all_to_all(blocks, group, 0, 0, tiled=True)

    own_half = lax.axis_index("freq")
    own_group = lax.axis_index("dp")
    kept, sent, grad_tokens = attention_backward(
        query, keys, memory, mixed, grad_mixed, inverse, live_row, live_lanes, weights, normed1, joint_proj,
        inputs, branch, vectors1, vector_grads, own_half.reshape(1),
    )
    kept, sent, moved = lax.optimization_barrier((kept, sent, moved))
    got = lax.ppermute(sent, "freq", [(0, 1), (1, 0)])
    outp_rows = jnp.sum(moved[:, padded:].astype(F32), axis=0).astype(BF16)
    joint_half = (kept.astype(F32) + got.astype(F32)).astype(BF16).reshape(time_size, share, kept.shape[1])
    joint_half, mlp_rows, outp_rows = lax.optimization_barrier((joint_half, mlp_rows, outp_rows))
    mlp_sum, outp_sum = lax.psum((mlp_rows, outp_rows), "dp")
    arrived = lax.all_to_all(joint_half, "tm", 0, 0, tiled=True)
    joint_rows = jnp.sum(arrived.astype(F32), axis=0).astype(BF16)
    joint_rows, grad_tokens, moved = lax.optimization_barrier((joint_rows, grad_tokens, moved))

    def to_group(array, distance):
        return lax.ppermute(array, "dp", [(i, i ^ distance) for i in range(groups)])

    cut = joint_rows.reshape(groups, share // groups, kept.shape[1])
    piece = lax.dynamic_index_in_dim(cut, own_group, 0, False).astype(F32)
    for distance in range(1, groups):
        piece += to_group(lax.dynamic_index_in_dim(cut, own_group ^ distance, 0, False), distance).astype(F32)
    piece = piece.astype(BF16)
    pieces = [piece] + [to_group(piece, distance) for distance in range(1, groups)]
    output = jnp.transpose(moved[:, :slots], (1, 0, 2))
    grad_patches = to_slots(grad_tokens)

    pieces[1], mlp_sum, outp_sum = lax.optimization_barrier((pieces[1], mlp_sum, outp_sum))
    down_sum, up_sum, outp_sum, up_bias_sum = collect_mlp(mlp_sum, outp_sum, share)
    joint_sum, gain_sum, shift_sum, bias_sum, branch_sum = collect_joint(own_group.reshape(1), pieces, share)
    return (
        output,
        grad_patches,
        gain_sum,
        shift_sum,
        joint_sum,
        bias_sum,
        outp_sum,
        up_sum,
        up_bias_sum[0],
        down_sum,
        branch_sum,
    )


def plan(patches, *others):
    members = lax.axis_size("freq") * lax.axis_size("tm")
    if patches.shape[1] == members:
        return per_device(patches, *others)
    return per_device_gathered(patches, *others)


def solution(mesh):
    return jax.shard_map(
        plan,
        mesh=mesh,
        in_specs=(
            P(("freq", "tm"), "dp", None),
            P(),
            P(),
            P(),
            P(),
            P(),
            P(),
            P(),
            P(),
            P(),
            P(),
            P(("freq", "tm"), "dp", None),
        ),
        out_specs=(
            P(("freq", "tm"), "dp", None),
            P(("freq", "tm"), "dp", None),
            P(None, ("freq", "tm")),
            P(None, ("freq", "tm")),
            P(("freq", "tm"), None),
            P(None, ("freq", "tm")),
            P(("freq", "tm"), None),
            P(("freq", "tm"), None),
            P(("freq", "tm")),
            P(("freq", "tm"), None),
            P(None, ("freq", "tm")),
        ),
        check_vma=False,
    )
```

```python
import functools
import math

import jax
import jax.numpy as jnp
from jax import lax
from jax.experimental import pallas as pl
from jax.experimental.pallas import tpu as pltpu
from jax.sharding import PartitionSpec as P

HEADS = 12
DH = 64
FREQ_ROWS = 12


EPS = 1e-06
NEG = -1000000000.0


def live_slots(col_counts, slot_ids, freq_ids, time_ids, freq_rows, cap_cols):
    table = jnp.arange(col_counts.shape[0], dtype=jnp.int32)
    live_cols = jnp.sum(
        jnp.where(time_ids[:, None] == table[None, :], col_counts[None, :], 0), axis=1
    )
    in_grid = slot_ids < freq_rows * cap_cols
    column_live = slot_ids // freq_rows < live_cols
    extra_live = (time_ids == 0) & (freq_ids == 0)
    return jnp.where(in_grid, column_live, extra_live)


def norm_rows(values, gain, shift):
    centered = values - jnp.mean(values, axis=-1, keepdims=True)
    inverse = lax.rsqrt(jnp.mean(centered * centered, axis=-1, keepdims=True) + EPS)
    return centered * inverse * gain + shift


def gelu_exact(values):
    return jax.nn.gelu(values, approximate=False)


def matmul(left, right):
    return jnp.dot(left, right, preferred_element_type=jnp.float32)


def matmul_tn(left, right):
    return lax.dot_general(
        left, right, (((0,), (0,)), ((), ())), preferred_element_type=jnp.float32
    )


def matmul_nt(left, right):
    return lax.dot_general(
        left, right, (((1,), (1,)), ((), ())), preferred_element_type=jnp.float32
    )


def head_pair(array, offset, lane_width, head_size):
    section = lax.dynamic_slice_in_dim(array, offset, lane_width, 2)
    return section.reshape(section.shape[0], section.shape[1], 2, head_size)


def add_lanes(target, addend, offset):
    current = lax.dynamic_slice_in_dim(target, offset, addend.shape[2], 2)
    return lax.dynamic_update_slice_in_dim(target, current + addend, offset, 2)


def pair_probs(query_pair, key_pair, log_pair, mask, scale):
    scores = (
        jnp.einsum("qchd,kchd->chqk", query_pair, key_pair, preferred_element_type=jnp.float32)
        * scale
        + mask
    )
    return jnp.exp(scores - jnp.transpose(log_pair, (1, 2, 0))[..., None])


def per_device_gathered(
    patches,
    col_counts,
    norm_gain,
    norm_shift,
    joint_proj,
    proj_bias,
    out_proj,
    up_proj,
    up_bias,
    down_proj,
    out_bias,
    cotangent,
):
    slots, clips, width = patches.shape
    row_count = slots * clips
    lane_width = 2 * DH
    pair_count = HEADS // 2
    scale = 1.0 / math.sqrt(DH)
    freq_size = lax.axis_size("freq")
    time_size = lax.axis_size("tm")
    freq_rows = FREQ_ROWS // freq_size
    cap_cols = (slots - 2) // freq_rows
    key_count = slots * freq_size * time_size
    slot_ids = jnp.arange(slots, dtype=jnp.int32)
    own_live = live_slots(
        col_counts,
        slot_ids,
        jnp.full((slots,), lax.axis_index("freq"), jnp.int32),
        jnp.full((slots,), lax.axis_index("tm"), jnp.int32),
        freq_rows,
        cap_cols,
    )
    key_ids = jnp.arange(key_count, dtype=jnp.int32)
    key_group = key_ids // slots
    key_live = live_slots(
        col_counts,
        key_ids % slots,
        key_group // time_size,
        key_group % time_size,
        freq_rows,
        cap_cols,
    )
    key_mask = jnp.where(key_live, 0.0, NEG).astype(jnp.float32)
    row_live = (
        jnp.broadcast_to(own_live[:, None], (slots, clips))
        .reshape(row_count, 1)
        .astype(jnp.float32)
    )
    gain_full = norm_gain.astype(jnp.float32)
    shift_full = norm_shift.astype(jnp.float32)
    bias_full = proj_bias.astype(jnp.float32)
    outb_full = out_bias.astype(jnp.float32)
    upb_full = up_bias.astype(jnp.float32)
    inputs = patches.reshape(row_count, width).astype(jnp.float32)
    normed1, ln1_back = jax.vjp(norm_rows, inputs, gain_full[0], shift_full[0])
    normed1_low = normed1.astype(jnp.bfloat16)
    joint = matmul(normed1_low, joint_proj)
    query_low = (joint[:, :width] + bias_full[0]).astype(jnp.bfloat16)
    keys_low = joint[:, width : 2 * width].astype(jnp.bfloat16)
    memory_low = (joint[:, 2 * width :] + bias_full[1]).astype(jnp.bfloat16)
    query3 = query_low.reshape(slots, clips, width)
    key_value = jnp.concatenate([keys_low, memory_low], axis=1).reshape(slots, clips, 2 * width)
    all_memory = lax.all_gather(key_value, ("freq", "tm"), axis=0, tiled=True)

    def forward_pair(number, state):
        mixed_acc, log_acc = state
        offset = number * lane_width
        query_pair = head_pair(query3, offset, lane_width, DH)
        key_pair = head_pair(all_memory, offset, lane_width, DH)
        value_pair = head_pair(all_memory, width + offset, lane_width, DH)
        scores = (
            jnp.einsum("qchd,kchd->chqk", query_pair, key_pair, preferred_element_type=jnp.float32)
            * scale
            + key_mask
        )
        highest = jnp.max(scores, axis=-1, keepdims=True)
        exponent = jnp.exp(scores - highest)
        summed = jnp.sum(exponent, axis=-1, keepdims=True)
        attention = (exponent / summed).astype(jnp.bfloat16)
        mixed = jnp.einsum(
            "chqk,kchd->qchd", attention, value_pair, preferred_element_type=jnp.float32
        )
        log_pair = jnp.transpose((highest + jnp.log(summed))[..., 0], (2, 0, 1))
        mixed_acc = lax.dynamic_update_slice_in_dim(
            mixed_acc, mixed.reshape(slots, clips, lane_width), offset, 2
        )
        log_acc = lax.dynamic_update_slice_in_dim(log_acc, log_pair, 2 * number, 2)
        return (mixed_acc, log_acc)

    mixed_full, log_rows = lax.fori_loop(
        0,
        pair_count,
        forward_pair,
        (
            jnp.zeros((slots, clips, width), jnp.float32),
            jnp.zeros((slots, clips, HEADS), jnp.float32),
        ),
    )
    mixed_low = mixed_full.reshape(row_count, width).astype(jnp.bfloat16)
    middle = inputs + matmul(mixed_low, out_proj) + outb_full[0]
    normed2, ln2_back = jax.vjp(norm_rows, middle, gain_full[1], shift_full[1])
    normed2_low = normed2.astype(jnp.bfloat16)
    pre_act = matmul(normed2_low, up_proj) + upb_full
    activated, gelu_back = jax.vjp(gelu_exact, pre_act)
    hidden_low = activated.astype(jnp.bfloat16)
    final = middle + matmul(hidden_low, down_proj) + outb_full[1]
    output = (final * row_live).astype(jnp.bfloat16).reshape(slots, clips, width)
    grad_out_rows = cotangent.reshape(row_count, width).astype(jnp.float32) * row_live
    grad_out_low = grad_out_rows.astype(jnp.bfloat16)
    grad_down_part = matmul_tn(hidden_low, grad_out_low)
    grad_outb_mlp = jnp.sum(grad_out_rows, axis=0)
    grad_hidden = matmul_nt(grad_out_low, down_proj)
    grad_pre_low = gelu_back(grad_hidden)[0].astype(jnp.bfloat16)
    grad_up_part = matmul_tn(normed2_low, grad_pre_low)
    grad_upb_part = jnp.sum(grad_pre_low.astype(jnp.float32), axis=0)
    grad_normed2 = matmul_nt(grad_pre_low, up_proj)
    grad_mid_part, grad_gain_mlp, grad_shift_mlp = ln2_back(grad_normed2)
    grad_middle = grad_out_rows + grad_mid_part
    grad_branch = grad_middle.astype(jnp.bfloat16)
    grad_outp_part = matmul_tn(mixed_low, grad_branch)
    grad_outb_attn = jnp.sum(grad_branch.astype(jnp.float32), axis=0)
    grad_mixed_low = matmul_nt(grad_branch, out_proj).astype(jnp.bfloat16)
    grad_mixed3 = grad_mixed_low.reshape(slots, clips, width)

    def query_side(number):
        offset = number * lane_width
        query_pair = head_pair(query3, offset, lane_width, DH)
        grad_pair = head_pair(grad_mixed3, offset, lane_width, DH)
        key_pair = head_pair(all_memory, offset, lane_width, DH)
        value_pair = head_pair(all_memory, width + offset, lane_width, DH)
        log_pair = lax.dynamic_slice_in_dim(log_rows, 2 * number, 2, 2)
        probability = pair_probs(query_pair, key_pair, log_pair, key_mask, scale)
        grad_probs = jnp.einsum(
            "qchd,kchd->chqk", grad_pair, value_pair, preferred_element_type=jnp.float32
        )
        delta = jnp.sum(probability * grad_probs, axis=-1, keepdims=True)
        grad_scores = (probability * (grad_probs - delta)).astype(jnp.bfloat16)
        grad_query = (
            jnp.einsum("chqk,kchd->qchd", grad_scores, key_pair, preferred_element_type=jnp.float32)
            * scale
        )
        return (
            offset,
            query_pair,
            grad_pair,
            probability,
            grad_scores,
            delta,
            grad_query.reshape(slots, clips, lane_width),
        )

    zero_query = jnp.zeros((slots, clips, width), jnp.float32)

    def backward_pair(number, state):
        grad_query_acc, grad_memory = state
        side = query_side(number)
        offset = side[0]
        grad_keys = (
            jnp.einsum("chqk,qchd->kchd", side[4], side[1], preferred_element_type=jnp.float32)
            * scale
        )
        grad_values = jnp.einsum(
            "chqk,qchd->kchd",
            side[3].astype(jnp.bfloat16),
            side[2],
            preferred_element_type=jnp.float32,
        )
        grad_memory = add_lanes(
            grad_memory, grad_keys.reshape(key_count, clips, lane_width), offset
        )
        grad_memory = add_lanes(
            grad_memory, grad_values.reshape(key_count, clips, lane_width), width + offset
        )
        return (add_lanes(grad_query_acc, side[6], offset), grad_memory)

    grad_query_full, grad_memory_all = lax.fori_loop(
        0,
        pair_count,
        backward_pair,
        (zero_query, jnp.zeros((key_count, clips, 2 * width), jnp.float32)),
    )
    grad_memory_own = lax.psum_scatter(
        grad_memory_all, ("freq", "tm"), scatter_dimension=0, tiled=True
    )
    grad_query_low = grad_query_full.reshape(row_count, width).astype(jnp.bfloat16)
    grad_memory_low = grad_memory_own.reshape(row_count, 2 * width).astype(jnp.bfloat16)
    grad_joint = jnp.concatenate([grad_query_low, grad_memory_low], axis=1)
    grad_joint_part = matmul_tn(normed1_low, grad_joint)
    grad_bias_cols = jnp.stack(
        [
            jnp.sum(grad_query_low.astype(jnp.float32), axis=0),
            jnp.sum(grad_memory_low[:, width:].astype(jnp.float32), axis=0),
        ],
        axis=1,
    )
    grad_normed1 = matmul_nt(grad_joint, joint_proj)
    grad_in_part, grad_gain_attn, grad_shift_attn = ln1_back(grad_normed1)
    grad_patches = (grad_middle + grad_in_part).astype(jnp.bfloat16).reshape(slots, clips, width)
    shares = (
        lax.psum_scatter(
            grad_joint_part.astype(jnp.bfloat16), ("freq", "tm"), scatter_dimension=0, tiled=True
        ).astype(jnp.float32),
        lax.psum_scatter(
            grad_bias_cols.astype(jnp.bfloat16), ("freq", "tm"), scatter_dimension=0, tiled=True
        ).astype(jnp.float32),
        lax.psum_scatter(
            grad_outp_part.astype(jnp.bfloat16), ("freq", "tm"), scatter_dimension=0, tiled=True
        ).astype(jnp.float32),
        lax.psum_scatter(
            grad_outb_attn.astype(jnp.bfloat16), ("freq", "tm"), scatter_dimension=0, tiled=True
        ).astype(jnp.float32),
        lax.psum_scatter(
            grad_gain_attn.astype(jnp.bfloat16), ("freq", "tm"), scatter_dimension=0, tiled=True
        ).astype(jnp.float32),
        lax.psum_scatter(
            grad_shift_attn.astype(jnp.bfloat16), ("freq", "tm"), scatter_dimension=0, tiled=True
        ).astype(jnp.float32),
        lax.psum_scatter(
            grad_up_part.astype(jnp.bfloat16), ("freq", "tm"), scatter_dimension=0, tiled=True
        ).astype(jnp.float32),
        lax.psum_scatter(
            grad_upb_part.astype(jnp.bfloat16), ("freq", "tm"), scatter_dimension=0, tiled=True
        ).astype(jnp.float32),
        lax.psum_scatter(
            grad_down_part.astype(jnp.bfloat16), ("freq", "tm"), scatter_dimension=0, tiled=True
        ).astype(jnp.float32),
        lax.psum_scatter(
            grad_outb_mlp.astype(jnp.bfloat16), ("freq", "tm"), scatter_dimension=0, tiled=True
        ).astype(jnp.float32),
        lax.psum_scatter(
            grad_gain_mlp.astype(jnp.bfloat16), ("freq", "tm"), scatter_dimension=0, tiled=True
        ).astype(jnp.float32),
        lax.psum_scatter(
            grad_shift_mlp.astype(jnp.bfloat16), ("freq", "tm"), scatter_dimension=0, tiled=True
        ).astype(jnp.float32),
    )
    summed_all = (
        lax.psum(shares[0].astype(jnp.bfloat16), "dp").astype(jnp.float32),
        lax.psum(shares[1].astype(jnp.bfloat16), "dp").astype(jnp.float32),
        lax.psum(shares[2].astype(jnp.bfloat16), "dp").astype(jnp.float32),
        lax.psum(shares[3].astype(jnp.bfloat16), "dp").astype(jnp.float32),
        lax.psum(shares[4].astype(jnp.bfloat16), "dp").astype(jnp.float32),
        lax.psum(shares[5].astype(jnp.bfloat16), "dp").astype(jnp.float32),
        lax.psum(shares[6].astype(jnp.bfloat16), "dp").astype(jnp.float32),
        lax.psum(shares[7].astype(jnp.bfloat16), "dp").astype(jnp.float32),
        lax.psum(shares[8].astype(jnp.bfloat16), "dp").astype(jnp.float32),
        lax.psum(shares[9].astype(jnp.bfloat16), "dp").astype(jnp.float32),
        lax.psum(shares[10].astype(jnp.bfloat16), "dp").astype(jnp.float32),
        lax.psum(shares[11].astype(jnp.bfloat16), "dp").astype(jnp.float32),
    )
    attn_summed = summed_all[:6]
    mlp_summed = summed_all[6:]
    grad_norm_gain = jnp.stack([attn_summed[4], mlp_summed[4]])
    grad_norm_shift = jnp.stack([attn_summed[5], mlp_summed[5]])
    grad_out_bias = jnp.stack([attn_summed[3], mlp_summed[3]])
    grad_proj_bias = jnp.transpose(attn_summed[1])
    return (
        output,
        grad_patches,
        grad_norm_gain,
        grad_norm_shift,
        attn_summed[0],
        grad_proj_bias,
        attn_summed[2],
        mlp_summed[0],
        mlp_summed[1],
        mlp_summed[2],
        grad_out_bias,
    )


LOG2E = 1.4426950408889634
LANES = 128
F32 = jnp.float32
BF16 = jnp.bfloat16
VMEM_LIMIT = 62 << 20
SAFE_RANGE = 100.0
CHUNKS = 4
HALVES = 2
SPAN = 1024
COLLECT_FLOPS = 30 * 10**9


def normalize(values):
    centered = values - jnp.mean(values, axis=-1, keepdims=True)
    inverse = lax.rsqrt(jnp.mean(centered * centered, axis=-1, keepdims=True) + EPS)
    return centered * inverse, inverse


def norm_back(normed, inverse, incoming, gain):
    scaled = incoming * gain
    mean = jnp.mean(scaled, axis=-1, keepdims=True)
    slope = jnp.mean(scaled * normed, axis=-1, keepdims=True)
    return (scaled - mean - normed * slope) * inverse


def spans_of(tokens):
    return [slice(at, min(at + SPAN, 2 * tokens)) for at in range(0, 2 * tokens, SPAN)]


def column_sum(values):
    return jnp.sum(values, axis=0, keepdims=True)


def project_kernel(x_ref, live_ref, w_ref, vec_ref, rows_ref, n_ref, q_ref, k_ref, v_ref, first_key, rows):
    blocks, slots, width = x_ref.shape
    padded = rows.shape[0] // blocks

    @pl.when(pl.program_id(0) == 0)
    def _():
        rows[...] = jnp.zeros_like(rows)

    for block in range(blocks):
        rows[block * padded : block * padded + slots] = x_ref[block].astype(F32)
    rows_ref[...] = rows[...].astype(BF16)
    normed, _ = normalize(rows[...])
    low = (normed * vec_ref[0:1, :] + vec_ref[1:2, :]).astype(BF16)
    n_ref[...] = low
    q_ref[...] = (matmul(low, w_ref[:, 0:width]) + vec_ref[2:3, :]).astype(BF16)
    keys = matmul(low, w_ref[:, width : 2 * width]).astype(BF16).astype(F32)

    @pl.when(pl.program_id(0) == 0)
    def _():
        first_key[...] = jnp.broadcast_to(keys[0:1, :], first_key.shape)

    k_ref[...] = jnp.where(live_ref[:, 0:1] > 0, keys, first_key[0:1, :]).astype(BF16)
    v_ref[...] = (matmul(low, w_ref[:, 2 * width : 3 * width]) + vec_ref[3:4, :]).astype(BF16)


def project(blocks, live_lanes, joint_proj, vectors, steps=4):
    members, slots, width = blocks.shape
    tokens = live_lanes.shape[0]
    rows = tokens // steps
    block = pl.BlockSpec((rows, width), lambda step: (step, 0))
    return pl.pallas_call(
        project_kernel,
        grid=(steps,),
        in_specs=[
            pl.BlockSpec((members // steps, slots, width), lambda step: (step, 0, 0)),
            pl.BlockSpec((rows, LANES), lambda step: (step, 0)),
            pl.BlockSpec((width, 3 * width), lambda step: (0, 0), pipeline_mode=pl.Buffered(1)),
            pl.BlockSpec((8, width), lambda step: (0, 0)),
        ],
        out_specs=[block] * 5,
        out_shape=[jax.ShapeDtypeStruct((tokens, width), BF16)] * 5,
        scratch_shapes=[pltpu.VMEM((8, width), F32), pltpu.VMEM((rows, width), F32)],
        compiler_params=pltpu.CompilerParams(vmem_limit_bytes=VMEM_LIMIT),
        cost_estimate=pl.CostEstimate(
            flops=6 * tokens * width * width, transcendentals=tokens, bytes_accessed=10 * tokens * width
        ),
    )(blocks, live_lanes, joint_proj, vectors)


def attention_forward_kernel(q_ref, k_ref, v_ref, live_ref, o_ref, rn_ref, p_ref, qs, vt, ot, sa, p_buf, p_sem):
    tokens = q_ref.shape[0]
    pair = pl.program_id(0)
    slot = lax.rem(pair, 2)
    spans = spans_of(tokens)

    def copy_of(pair, slot, index):
        span = spans[index]
        columns = pl.ds(span.start, span.stop - span.start)
        return pltpu.make_async_copy(
            p_buf.at[slot, :, columns], p_ref.at[pair, :, columns], p_sem.at[slot, index]
        )

    @pl.when(pair >= 2)
    def _():
        for index in range(len(spans)):
            copy_of(pair - 2, slot, index).wait()

    lane = lax.broadcasted_iota(jnp.int32, (tokens, LANES), 1)
    query = q_ref[...].astype(F32) * (1.0 / math.sqrt(DH))
    keys = k_ref[...].astype(F32)
    qs[0:tokens, :] = jnp.where(lane < DH, query, 0.0).astype(BF16)
    qs[tokens : 2 * tokens, :] = jnp.where(lane < DH, 0.0, query).astype(BF16)
    live = live_ref[0:1, :]
    vt[0:LANES, :] = (jnp.transpose(v_ref[...].astype(F32)) * live).astype(BF16)
    vt[LANES : LANES + 16, :] = jnp.broadcast_to(live, (16, tokens)).astype(BF16)

    def largest(values, head):
        squares = jnp.where((lane < DH) == (head == 0), values * values, 0.0)
        return jnp.max(jnp.sum(squares, axis=1, keepdims=True))

    limit = (SAFE_RANGE / LOG2E) ** 2
    bound = jnp.maximum(
        largest(query, 0) * largest(keys, 0), largest(query, 1) * largest(keys, 1)
    )
    bounded = bound <= limit

    def finish(span, weight):
        p_buf[slot, :, span] = weight
        ot[:, span] = matmul(vt[...], weight)

    @pl.when(bounded)
    def _():
        for index, span in enumerate(spans):
            finish(span, jnp.exp2(matmul_nt(k_ref[...], qs[span, :]) * LOG2E).astype(BF16))
            copy_of(pair, slot, index).start()

    @pl.when(jnp.logical_not(bounded))
    def _():
        for index, span in enumerate(spans):
            for start in range(span.start, span.stop, LANES):
                part = slice(start, start + LANES)
                sa[...] = matmul_nt(k_ref[...], qs[part, :])
                score = sa[...]
                highest = jnp.max(score, axis=0, keepdims=True)
                finish(part, jnp.exp2(score * LOG2E - highest * LOG2E).astype(BF16))
            copy_of(pair, slot, index).start()

    row = lax.broadcasted_iota(jnp.int32, (LANES, tokens), 0)
    inverse = jnp.where(
        row < DH,
        jnp.broadcast_to(1.0 / ot[LANES : LANES + 1, 0:tokens], (LANES, tokens)),
        jnp.broadcast_to(1.0 / ot[LANES : LANES + 1, tokens : 2 * tokens], (LANES, tokens)),
    )
    mixed = jnp.where(row < DH, ot[0:LANES, 0:tokens], ot[0:LANES, tokens : 2 * tokens]) * inverse
    o_ref[...] = jnp.transpose(mixed).astype(BF16)
    rn_ref[...] = jnp.transpose(inverse)

    @pl.when(pair == pl.num_programs(0) - 1)
    def _():
        for index in range(len(spans)):
            copy_of(pair - 1, 1 - slot, index).wait()
        for index in range(len(spans)):
            copy_of(pair, slot, index).wait()


def attention_forward(query, keys, memory, live_row):
    tokens, width = query.shape
    pairs = width // LANES
    block = pl.BlockSpec((tokens, LANES), lambda pair: (0, pair))
    return pl.pallas_call(
        attention_forward_kernel,
        grid=(pairs,),
        in_specs=[block, block, block, pl.BlockSpec((8, tokens), lambda pair: (0, 0))],
        out_specs=[block, block, pl.BlockSpec(memory_space=pl.ANY)],
        out_shape=[
            jax.ShapeDtypeStruct((tokens, width), BF16),
            jax.ShapeDtypeStruct((tokens, width), F32),
            jax.ShapeDtypeStruct((pairs, tokens, 2 * tokens), BF16),
        ],
        scratch_shapes=[
            pltpu.VMEM((2 * tokens, LANES), BF16),
            pltpu.VMEM((LANES + 16, tokens), BF16),
            pltpu.VMEM((LANES + 16, 2 * tokens), F32),
            pltpu.VMEM((tokens, LANES), F32),
            pltpu.VMEM((2, tokens, 2 * tokens), BF16),
            pltpu.SemaphoreType.DMA((2, len(spans_of(tokens)))),
        ],
        compiler_params=pltpu.CompilerParams(vmem_limit_bytes=VMEM_LIMIT),
        cost_estimate=pl.CostEstimate(
            flops=8 * pairs * tokens * tokens * LANES,
            transcendentals=2 * pairs * tokens * tokens,
            bytes_accessed=4 * pairs * tokens * tokens,
        ),
    )(query, keys, memory, live_row)


def attention_backward_kernel(
    q_ref, k_ref, v_ref, o_ref, do_ref, rn_ref, live_ref, keep_ref, p_ref, n_ref, w_ref,
    x_ref, res_ref, vec_ref, sums_ref, half_ref, out_ref,
    kept_ref, sent_ref, rows_ref, qs, gs, kt, dqt, delta, dj, vecs, n_buf, w_buf, x_buf, res_buf, dx_buf, sem, dx_sem,
):
    tokens = q_ref.shape[0]
    pair = pl.program_id(0)

    late = [
        pltpu.make_async_copy(source, target, sem.at[index])
        for index, (source, target) in enumerate(
            ((n_ref, n_buf), (w_ref, w_buf), (x_ref, x_buf), (res_ref, res_buf))
        )
    ]

    @pl.when(pair == 0)
    def _():
        for copy in late:
            copy.start()

    scale = 1.0 / math.sqrt(DH)
    lane = lax.broadcasted_iota(jnp.int32, (tokens, LANES), 1)
    query = q_ref[...].astype(F32) * scale
    qs[0:tokens, :] = jnp.where(lane < DH, query, 0.0).astype(BF16)
    qs[tokens : 2 * tokens, :] = jnp.where(lane < DH, 0.0, query).astype(BF16)
    grad = do_ref[...].astype(F32) * rn_ref[...]
    gs[0:tokens, :] = jnp.where(lane < DH, grad, 0.0).astype(BF16)
    gs[tokens : 2 * tokens, :] = jnp.where(lane < DH, 0.0, grad).astype(BF16)
    kt[...] = (jnp.transpose(k_ref[...].astype(F32)) * (live_ref[0:1, :] * scale)).astype(BF16)
    product = jnp.transpose(grad * o_ref[...].astype(F32))
    for head in range(2):
        total = column_sum(product[head * DH : (head + 1) * DH])
        delta[:, head * tokens : (head + 1) * tokens] = jnp.broadcast_to(total, (8, tokens))
    grad_keys = grad_values = None
    for span in spans_of(tokens):
        weight = p_ref[0, :, span]
        grad_weight = matmul_nt(v_ref[...], gs[span, :])
        grad_score = (weight.astype(F32) * (grad_weight - delta[0:1, span])).astype(BF16)
        dqt[:, span] = matmul(kt[...], grad_score)
        part_values = matmul(weight, gs[span, :])
        part_keys = matmul(grad_score, qs[span, :])
        grad_values = part_values if grad_values is None else grad_values + part_values
        grad_keys = part_keys if grad_keys is None else grad_keys + part_keys
    row = lax.broadcasted_iota(jnp.int32, (LANES, tokens), 0)
    grad_query = jnp.transpose(jnp.where(row < DH, dqt[:, 0:tokens], dqt[:, tokens : 2 * tokens]))
    keep = keep_ref[...] > 0
    width = x_buf.shape[1]
    parts = (
        grad_query.astype(BF16),
        jnp.where(keep, grad_keys, 0.0).astype(BF16),
        jnp.where(keep, grad_values, 0.0).astype(BF16),
    )
    for part, value in enumerate(parts):
        columns = pl.ds(pl.multiple_of(part * width + pl.program_id(0) * LANES, LANES), LANES)
        dj[:, columns] = value
        if part != 1:
            columns = pl.ds(pl.multiple_of(pl.program_id(0) * LANES, LANES), LANES)
            vecs[2 + part // 2 : 3 + part // 2, columns] = column_sum(value.astype(F32))

    @pl.when(pl.program_id(0) == pl.num_programs(0) - 1)
    def _():
        for copy in late:
            copy.wait()
        first = half_ref[0] == 0
        half = width // 2
        for part in range(3):
            span = slice(part * width, (part + 1) * width)
            grad_weights = matmul_tn(n_buf[...], dj[:, span]).astype(BF16)
            kept_ref[:, span] = jnp.where(first, grad_weights[:half], grad_weights[half:])
            sent_ref[:, span] = jnp.where(first, grad_weights[half:], grad_weights[:half])
        vecs[4:8, :] = sums_ref[0:4, :]
        rows = tokens // CHUNKS
        block = tokens // rows_ref.shape[0]
        stores = []
        gain_sum = shift_sum = 0.0
        for start in range(0, tokens, rows):
            span = slice(start, start + rows)
            incoming = matmul_nt(dj[span, :], w_buf[...])
            normed, inverse = normalize(x_buf[span, :].astype(F32))
            gain_sum += column_sum(incoming * normed)
            shift_sum += column_sum(incoming)
            back = norm_back(normed, inverse, incoming, vec_ref[0:1, :])
            grad_rows = (res_buf[span, :].astype(F32) + back).astype(BF16)
            for part in range(rows // block):
                dx_buf[start // block + part] = grad_rows[part * block : part * block + dx_buf.shape[1]]
            stores.append(
                pltpu.make_async_copy(
                    dx_buf.at[pl.ds(start // block, rows // block)],
                    rows_ref.at[pl.ds(start // block, rows // block), 0],
                    dx_sem.at[start // rows],
                )
            )
            stores[-1].start()
        vecs[0:1, :] = gain_sum
        vecs[1:2, :] = shift_sum
        turned = jnp.transpose(jnp.concatenate([vecs[...]] * (LANES // 8), axis=0)).astype(BF16)
        tail = kept_ref.shape[1] - LANES
        kept_ref[:, tail:] = jnp.where(first, turned[:half], turned[half:])
        sent_ref[:, tail:] = jnp.where(first, turned[half:], turned[:half])
        for copy in stores:
            copy.wait()


def attention_backward(
    query, keys, memory, mixed, grad_mixed, inverse, live_row, live_lanes, weights, normed, joint_proj,
    inputs, residual, vectors, vector_grads, own_half, output,
):
    tokens, width = query.shape
    pairs = width // LANES
    block = pl.BlockSpec((tokens, LANES), lambda pair: (0, pair))
    once = pl.Buffered(1)
    anywhere = pl.BlockSpec(memory_space=pl.ANY)

    def fixed(rows, columns):
        return pl.BlockSpec((rows, columns), lambda pair: (0, 0), pipeline_mode=once)

    return pl.pallas_call(
        attention_backward_kernel,
        grid=(pairs,),
        in_specs=[block] * 6
        + [
            fixed(8, tokens),
            fixed(tokens, LANES),
            pl.BlockSpec((1, tokens, 2 * tokens), lambda pair: (pair, 0, 0)),
            anywhere,
            anywhere,
            anywhere,
            anywhere,
            fixed(8, width),
            fixed(8, width),
            pl.BlockSpec(memory_space=pltpu.SMEM),
            anywhere,
        ],
        out_specs=[fixed(width // 2, 3 * width + LANES), fixed(width // 2, 3 * width + LANES), anywhere],
        out_shape=[
            jax.ShapeDtypeStruct((width // 2, 3 * width + LANES), BF16),
            jax.ShapeDtypeStruct((width // 2, 3 * width + LANES), BF16),
            jax.ShapeDtypeStruct(output.shape, BF16),
        ],
        scratch_shapes=[
            pltpu.VMEM((2 * tokens, LANES), BF16),
            pltpu.VMEM((2 * tokens, LANES), BF16),
            pltpu.VMEM((LANES, tokens), BF16),
            pltpu.VMEM((LANES, 2 * tokens), F32),
            pltpu.VMEM((8, 2 * tokens), F32),
            pltpu.VMEM((tokens, 3 * width), BF16),
            pltpu.VMEM((8, width), F32),
            pltpu.VMEM((tokens, width), BF16),
            pltpu.VMEM((width, 3 * width), BF16),
            pltpu.VMEM((tokens, width), BF16),
            pltpu.VMEM((tokens, width), BF16),
            pltpu.VMEM((output.shape[0],) + output.shape[2:], BF16),
            pltpu.SemaphoreType.DMA((4,)),
            pltpu.SemaphoreType.DMA((CHUNKS,)),
        ],
        input_output_aliases={16: 2},
        compiler_params=pltpu.CompilerParams(vmem_limit_bytes=VMEM_LIMIT),
        cost_estimate=pl.CostEstimate(
            flops=16 * pairs * tokens * tokens * LANES,
            transcendentals=0,
            bytes_accessed=4 * pairs * tokens * tokens,
        ),
    )(
        query, keys, memory, mixed, grad_mixed, inverse, live_row, live_lanes, weights, normed,
        joint_proj, inputs, residual, vectors, vector_grads,
        own_half, output,
    )


def feed_forward_kernel(
    x_hbm, mixed_hbm, cot_hbm, live_ref, wo_ref, vec_ref, up_ref, down_ref, bias_ref,
    out_hbm, share_ref, branch_hbm, gm_hbm, packed_ref, ds_ref,
    x_ref, mixed_ref, cot_ref, out_ref, branch_ref, gm_ref,
    normed, grad_out, middle, acc, acc_grad, hidden, grad_pre, down_buf, up_buf, down_sem, up_sem, in_sem, out_sem,
):
    step = pl.program_id(0)
    last = pl.num_programs(0) - 1
    tokens, width = x_ref.shape
    units = up_ref.shape[1]
    rows = tokens // CHUNKS

    block = tokens // out_ref.shape[0]
    slots = out_ref.shape[1]
    parts = rows // block

    def rows_of_chunk(chunk):
        return pl.ds(pl.multiple_of(chunk * rows, 32), rows)

    def fetches(chunk):
        span = rows_of_chunk(chunk)
        pairs = ((x_hbm, x_ref), (mixed_hbm, mixed_ref), (cot_hbm, cot_ref))
        return [
            pltpu.make_async_copy(source.at[span], target.at[span], in_sem.at[chunk, index])
            for index, (source, target) in enumerate(pairs)
        ]

    def stores(chunk):
        span = rows_of_chunk(chunk)
        return [
            pltpu.make_async_copy(source.at[span], target.at[span], out_sem.at[chunk, index])
            for index, (source, target) in enumerate(((branch_ref, branch_hbm), (gm_ref, gm_hbm)))
        ] + [
            pltpu.make_async_copy(
                out_ref.at[pl.ds(chunk * parts, parts)],
                out_hbm.at[pl.ds(chunk * parts, parts), 1],
                out_sem.at[chunk, 2],
            )
        ]

    @pl.when(step == 0)
    def _():
        for chunk in range(CHUNKS):
            for copy in fetches(chunk):
                copy.start()

        def chunk_step(chunk, _):
            span = rows_of_chunk(chunk)
            for copy in fetches(chunk):
                copy.wait()
            values = x_ref[span, :].astype(F32) + matmul(mixed_ref[span, :], wo_ref[...]) + vec_ref[2:3, :]
            middle[span, :] = values
            acc[span, :] = values + vec_ref[3:4, :]
            unit, _ = normalize(values)
            normed[span, :] = (unit * vec_ref[0:1, :] + vec_ref[1:2, :]).astype(BF16)
            grad_out[span, :] = (cot_ref[span, :].astype(F32) * live_ref[span, 0:1]).astype(BF16)
            acc_grad[span, :] = jnp.zeros((rows, width), F32)
            return 0

        lax.fori_loop(0, CHUNKS, chunk_step, 0)

    up = up_ref[...]
    down = down_ref[...]
    half = tokens // HALVES

    def feed(index, grad_bias):
        span = pl.ds(pl.multiple_of(index * half, 32), half)
        pre_act = matmul(normed[span, :], up) + bias_ref[0:1, :]
        grad_hidden = matmul_nt(grad_out[span, :], down)
        cumulative = 0.5 + 0.5 * lax.erf(pre_act * math.sqrt(0.5))
        density = jnp.exp2(pre_act * pre_act * (-0.5 * LOG2E)) * (1.0 / math.sqrt(2.0 * math.pi))
        low = (pre_act * cumulative).astype(BF16)
        grad_low = (grad_hidden * (cumulative + pre_act * density)).astype(BF16)
        hidden[span, :] = low
        grad_pre[span, :] = grad_low
        acc[span, :] += matmul(low, down)
        acc_grad[span, :] += matmul_nt(grad_low, up)
        return grad_bias + column_sum(grad_low.astype(F32))

    grad_bias = lax.fori_loop(0, HALVES, feed, jnp.zeros((1, units), F32))
    slot = lax.rem(step, 2)
    _, cuts, quarters, share, _ = down_buf.shape
    own = units // cuts
    for cut in range(cuts):
        sums = jnp.broadcast_to(grad_bias[:, cut * own : (cut + 1) * own], (16, own)).astype(BF16)
        share_ref[step * cuts + cut, share : share + 16, 0:own] = sums
        share_ref[step * cuts + cut, share : share + 16, own:width] = jnp.zeros((16, width - own), BF16)

    def copies(at, slot):
        return (
            pltpu.make_async_copy(
                down_buf.at[slot], packed_ref.at[pl.ds(at * cuts, cuts), pl.ds(0, quarters)], down_sem.at[slot]
            ),
            pltpu.make_async_copy(up_buf.at[slot], packed_ref.at[:, quarters + at], up_sem.at[slot]),
        )

    @pl.when(step >= 2)
    def _():
        for copy in copies(step - 2, slot):
            copy.wait()

    grad_down = matmul_tn(hidden[...], grad_out[...]).astype(BF16)
    for cut in range(cuts):
        for quarter in range(quarters):
            base = (cut * quarters + quarter) * share
            down_buf[slot, cut, quarter] = grad_down[base : base + share]
    grad_up = matmul_tn(normed[...], grad_pre[...]).astype(BF16)
    for member in range(width // share):
        up_buf[slot, member] = grad_up[member * share : (member + 1) * share]
    for copy in copies(step, slot):
        copy.start()

    @pl.when(step == last)
    def _():
        ds_ref[...] = jnp.zeros_like(ds_ref)

        def chunk_step(chunk, _):
            span = rows_of_chunk(chunk)
            final = (acc[span, :] * live_ref[span, 0:1]).astype(BF16)
            for part in range(parts):
                out_ref[chunk * parts + part] = final[part * block : part * block + slots]
            unit, inverse = normalize(middle[span, :])
            incoming = acc_grad[span, :]
            start = grad_out[span, :].astype(F32)
            branch = (start + norm_back(unit, inverse, incoming, vec_ref[0:1, :])).astype(BF16)
            branch_ref[span, :] = branch
            gm_ref[span, :] = matmul_nt(branch, wo_ref[...]).astype(BF16)
            for copy in stores(chunk):
                copy.start()
            for place, term in enumerate((incoming * unit, incoming, branch.astype(F32), start)):
                ds_ref[place : place + 1, :] += column_sum(term)
            return 0

        lax.fori_loop(0, CHUNKS, chunk_step, 0)
        grad_outp = matmul_tn(mixed_ref[...], branch_ref[...]).astype(BF16)
        for member in range(width // share):
            share_ref[member, 0:share, :] = grad_outp[member * share : (member + 1) * share]
        for chunk in range(CHUNKS):
            for copy in stores(chunk):
                copy.wait()
        for copy in copies(step - 1, 1 - slot):
            copy.wait()
        for copy in copies(step, slot):
            copy.wait()


def feed_forward(
    inputs, mixed, cotangent, live_lanes, out_proj, vectors, up_proj, up_bias, down_proj, members, slots
):
    tokens, width = inputs.shape
    hidden_units = up_proj.shape[1]
    steps = hidden_units // width
    share = width // members
    cuts = members // steps
    quarters = hidden_units // members // share
    once = pl.Buffered(1)
    anywhere = pl.BlockSpec(memory_space=pl.ANY)

    def fixed(rows, columns):
        return pl.BlockSpec((rows, columns), lambda step: (0, 0), pipeline_mode=once)

    return pl.pallas_call(
        feed_forward_kernel,
        grid=(steps,),
        in_specs=[
            anywhere,
            anywhere,
            anywhere,
            fixed(tokens, LANES),
            fixed(width, width),
            fixed(8, width),
            pl.BlockSpec((width, width), lambda step: (0, step)),
            pl.BlockSpec((width, width), lambda step: (step, 0)),
            pl.BlockSpec((8, width), lambda step: (0, step)),
        ],
        out_specs=[
            anywhere,
            pl.BlockSpec((members, share + 16, width), lambda step: (0, 0, 0), pipeline_mode=once),
            anywhere,
            anywhere,
            anywhere,
            fixed(8, width),
        ],
        out_shape=[
            jax.ShapeDtypeStruct((members, 2, slots, width), BF16),
            jax.ShapeDtypeStruct((members, share + 16, width), BF16),
            jax.ShapeDtypeStruct((tokens, width), BF16),
            jax.ShapeDtypeStruct((tokens, width), BF16),
            jax.ShapeDtypeStruct((members, quarters + steps, share, width), BF16),
            jax.ShapeDtypeStruct((8, width), F32),
        ],
        scratch_shapes=[pltpu.VMEM((tokens, width), BF16)] * 3
        + [
            pltpu.VMEM((members, slots, width), BF16),
            pltpu.VMEM((tokens, width), BF16),
            pltpu.VMEM((tokens, width), BF16),
            pltpu.VMEM((tokens, width), BF16),
            pltpu.VMEM((tokens, width), BF16),
            pltpu.VMEM((tokens, width), F32),
            pltpu.VMEM((tokens, width), F32),
            pltpu.VMEM((tokens, width), F32),
            pltpu.VMEM((tokens, width), BF16),
            pltpu.VMEM((tokens, width), BF16),
            pltpu.VMEM((2, cuts, quarters, share, width), BF16),
            pltpu.VMEM((2, members, share, width), BF16),
            pltpu.SemaphoreType.DMA((2,)),
            pltpu.SemaphoreType.DMA((2,)),
            pltpu.SemaphoreType.DMA((CHUNKS, 3)),
            pltpu.SemaphoreType.DMA((CHUNKS, 3)),
        ],
        compiler_params=pltpu.CompilerParams(vmem_limit_bytes=VMEM_LIMIT),
        cost_estimate=pl.CostEstimate(
            flops=12 * tokens * width * hidden_units + 6 * tokens * width * width,
            transcendentals=2 * tokens * hidden_units,
            bytes_accessed=12 * tokens * width + 8 * width * hidden_units,
        ),
    )(inputs, mixed, cotangent, live_lanes, out_proj, vectors, up_proj, down_proj, up_bias)


def collect_joint_kernel(own_ref, *refs):
    pieces, (joint_ref, gain_ref, shift_ref, bias_ref, branch_ref, columns) = refs[:-6], refs[-6:]
    rows = pieces[0].shape[0]
    width = joint_ref.shape[1] // 3
    own = own_ref[0]
    columns[...] = jnp.zeros_like(columns)
    for place in range(len(pieces)):
        piece = pieces[place][...]
        for other in range(1, len(pieces)):
            piece = jnp.where(own == other, pieces[place ^ other][...], piece)
        piece = piece.astype(F32)
        span = slice(place * rows, (place + 1) * rows)
        joint_ref[span, :] = piece[:, : 3 * width]
        columns[span, :] = piece[:, 3 * width :]
    turned = jnp.transpose(columns[...])
    share = gain_ref.shape[1]
    gain_ref[0:1, :] = turned[0:1, 0:share]
    gain_ref[1:2, :] = turned[4:5, 0:share]
    shift_ref[0:1, :] = turned[1:2, 0:share]
    shift_ref[1:2, :] = turned[5:6, 0:share]
    bias_ref[...] = turned[2:4, 0:share]
    branch_ref[...] = turned[6:8, 0:share]


def collect_joint(own, pieces, share):
    width = (pieces[0].shape[1] - LANES) // 3
    vmem = pl.BlockSpec(memory_space=pltpu.VMEM)
    return pl.pallas_call(
        collect_joint_kernel,
        in_specs=[pl.BlockSpec(memory_space=pltpu.SMEM)] + [vmem] * len(pieces),
        out_specs=[vmem] * 5,
        out_shape=[jax.ShapeDtypeStruct((share, 3 * width), F32)] + [jax.ShapeDtypeStruct((2, share), F32)] * 4,
        scratch_shapes=[pltpu.VMEM((LANES, LANES), F32)],
        cost_estimate=pl.CostEstimate(flops=0, transcendentals=0, bytes_accessed=0),
    )(own, *pieces)


def collect_mlp_kernel(rows_ref, sums_ref, down_ref, up_ref, outp_ref, bias_ref):
    own, width = down_ref.shape
    share = outp_ref.shape[0]
    down_ref[...] = rows_ref[0:own, :].astype(F32)
    for part in range(own // share):
        rows = slice(own + part * share, own + (part + 1) * share)
        up_ref[:, part * width : (part + 1) * width] = rows_ref[rows, :].astype(F32)
    outp_ref[...] = sums_ref[0:share, :].astype(F32)
    bias_ref[...] = sums_ref[share : share + 16, 0:own].astype(F32)[0]


def collect_mlp(rows, sums, share):
    own, width = rows.shape[0] // 2, rows.shape[1]
    vmem = pl.BlockSpec(memory_space=pltpu.VMEM)
    return pl.pallas_call(
        collect_mlp_kernel,
        in_specs=[vmem] * 2,
        out_specs=[vmem] * 4,
        out_shape=[
            jax.ShapeDtypeStruct((own, width), F32),
            jax.ShapeDtypeStruct((share, own // share * width), F32),
            jax.ShapeDtypeStruct((share, width), F32),
            jax.ShapeDtypeStruct((own,), F32),
        ],
        cost_estimate=pl.CostEstimate(flops=COLLECT_FLOPS, transcendentals=0, bytes_accessed=4 * rows.size),
    )(rows, sums)


def per_device(
    patches,
    col_counts,
    norm_gain,
    norm_shift,
    joint_proj,
    proj_bias,
    out_proj,
    up_proj,
    up_bias,
    down_proj,
    out_bias,
    cotangent,
):
    slots, clips, width = patches.shape
    group = ("freq", "tm")
    freq_size = lax.axis_size("freq")
    time_size = lax.axis_size("tm")
    groups = lax.axis_size("dp")
    members = freq_size * time_size
    freq_rows = FREQ_ROWS // freq_size
    cap_cols = (slots - 2) // freq_rows
    padded = -(-slots // 16) * 16
    tokens = members * padded
    pairs = width // LANES
    share = width // members
    hidden_units = up_proj.shape[1]

    def to_clip(array):
        return lax.all_to_all(array, group, 0, 0, tiled=True)

    token_ids = jnp.arange(tokens, dtype=jnp.int32)
    block_ids = token_ids // padded
    live = live_slots(
        col_counts,
        token_ids % padded,
        block_ids // time_size,
        block_ids % time_size,
        freq_rows,
        cap_cols,
    ) & (token_ids % padded < slots)
    live_full = live.astype(F32)
    live_row = jnp.broadcast_to(live_full[None, :], (8, tokens))
    live_lanes = jnp.broadcast_to(live_full[:, None], (tokens, LANES))

    def rows_of(*vectors):
        stacked = jnp.stack(vectors).astype(F32)
        return jnp.pad(stacked, ((0, 8 - len(vectors)), (0, 0)))

    vectors1 = rows_of(norm_gain[0], norm_shift[0], proj_bias[0], proj_bias[1])
    vectors2 = rows_of(norm_gain[1], norm_shift[1], out_bias[0], out_bias[1])
    bias_rows = jnp.broadcast_to(up_bias.astype(F32)[None, :], (8, hidden_units))

    turned = jnp.transpose(cotangent, (1, 0, 2))
    cot = to_clip(jnp.pad(turned, ((0, 0), (0, padded - slots), (0, 0)))).reshape(tokens, width)
    inputs, normed1, query, keys, memory = project(
        to_clip(jnp.transpose(patches, (1, 0, 2))), live_lanes, joint_proj, vectors1
    )
    mixed, inverse, weights = attention_forward(query, keys, memory, live_row)
    output, blocks, branch, grad_mixed, packed, vector_grads = feed_forward(
        inputs, mixed, cot, live_lanes, out_proj, vectors2, up_proj, bias_rows, down_proj, members, padded
    )
    own = hidden_units // members
    mlp_rows = lax.psum_scatter(packed.reshape(members, 2 * own, width), group, scatter_dimension=0, tiled=True)[0]
    moved = lax.all_to_all(blocks, group, 0, 0, tiled=True)

    own_half = lax.axis_index("freq")
    own_group = lax.axis_index("dp")
    kept, sent, token_rows = attention_backward(
        query, keys, memory, mixed, grad_mixed, inverse, live_row, live_lanes, weights, normed1, joint_proj,
        inputs, branch, vectors1, vector_grads, own_half.reshape(1),
        output,
    )
    kept, sent, moved = lax.optimization_barrier((kept, sent, moved))
    got = lax.ppermute(sent, "freq", [(0, 1), (1, 0)])
    outp_rows = jnp.sum(moved.astype(F32), axis=0).astype(BF16)
    joint_half = (kept.astype(F32) + got.astype(F32)).astype(BF16).reshape(time_size, share, kept.shape[1])
    joint_half, mlp_rows, outp_rows = lax.optimization_barrier((joint_half, mlp_rows, outp_rows))
    mlp_sum, outp_sum = lax.psum((mlp_rows, outp_rows), "dp")
    arrived = lax.all_to_all(joint_half, "tm", 0, 0, tiled=True)
    joint_rows = jnp.sum(arrived.astype(F32), axis=0).astype(BF16)
    joint_rows, token_rows = lax.optimization_barrier((joint_rows, token_rows))

    def to_group(array, distance):
        return lax.ppermute(array, "dp", [(i, i ^ distance) for i in range(groups)])

    cut = joint_rows.reshape(groups, share // groups, kept.shape[1])
    piece = lax.dynamic_index_in_dim(cut, own_group, 0, False).astype(F32)
    for distance in range(1, groups):
        piece += to_group(lax.dynamic_index_in_dim(cut, own_group ^ distance, 0, False), distance).astype(F32)
    piece = piece.astype(BF16)
    pieces = [piece] + [to_group(piece, distance) for distance in range(1, groups)]
    token_rows = lax.all_to_all(token_rows, group, 0, 0, tiled=True)
    grad_patches, output = (jnp.transpose(token_rows[:, kind, :slots], (1, 0, 2)) for kind in range(2))

    joint_sum, gain_sum, shift_sum, bias_sum, branch_sum = collect_joint(own_group.reshape(1), pieces, share)
    joint_sum, mlp_sum, outp_sum = lax.optimization_barrier((joint_sum, mlp_sum, outp_sum))
    down_sum, up_sum, outp_sum, up_bias_sum = collect_mlp(mlp_sum, outp_sum, share)
    return (
        output,
        grad_patches,
        gain_sum,
        shift_sum,
        joint_sum,
        bias_sum,
        outp_sum,
        up_sum,
        up_bias_sum,
        down_sum,
        branch_sum,
    )


def plan(patches, *others):
    members = lax.axis_size("freq") * lax.axis_size("tm")
    if patches.shape[1] == members:
        return per_device(patches, *others)
    return per_device_gathered(patches, *others)


def solution(mesh):
    return jax.shard_map(
        plan,
        mesh=mesh,
        in_specs=(
            P(("freq", "tm"), "dp", None),
            P(),
            P(),
            P(),
            P(),
            P(),
            P(),
            P(),
            P(),
            P(),
            P(),
            P(("freq", "tm"), "dp", None),
        ),
        out_specs=(
            P(("freq", "tm"), "dp", None),
            P(("freq", "tm"), "dp", None),
            P(None, ("freq", "tm")),
            P(None, ("freq", "tm")),
            P(("freq", "tm"), None),
            P(None, ("freq", "tm")),
            P(("freq", "tm"), None),
            P(("freq", "tm"), None),
            P(("freq", "tm")),
            P(("freq", "tm"), None),
            P(None, ("freq", "tm")),
        ),
        check_vma=False,
    )
```

```python
import functools
import math

import jax
import jax.numpy as jnp
from jax import lax
from jax.experimental import pallas as pl
from jax.experimental.pallas import tpu as pltpu
from jax.sharding import PartitionSpec as P

HEADS = 12
DH = 64
FREQ_ROWS = 12


EPS = 1e-06
NEG = -1000000000.0


def live_slots(col_counts, slot_ids, freq_ids, time_ids, freq_rows, cap_cols):
    table = jnp.arange(col_counts.shape[0], dtype=jnp.int32)
    live_cols = jnp.sum(
        jnp.where(time_ids[:, None] == table[None, :], col_counts[None, :], 0), axis=1
    )
    in_grid = slot_ids < freq_rows * cap_cols
    column_live = slot_ids // freq_rows < live_cols
    extra_live = (time_ids == 0) & (freq_ids == 0)
    return jnp.where(in_grid, column_live, extra_live)


def norm_rows(values, gain, shift):
    centered = values - jnp.mean(values, axis=-1, keepdims=True)
    inverse = lax.rsqrt(jnp.mean(centered * centered, axis=-1, keepdims=True) + EPS)
    return centered * inverse * gain + shift


def gelu_exact(values):
    return jax.nn.gelu(values, approximate=False)


def matmul(left, right):
    return jnp.dot(left, right, preferred_element_type=jnp.float32)


def matmul_tn(left, right):
    return lax.dot_general(
        left, right, (((0,), (0,)), ((), ())), preferred_element_type=jnp.float32
    )


def matmul_nt(left, right):
    return lax.dot_general(
        left, right, (((1,), (1,)), ((), ())), preferred_element_type=jnp.float32
    )


def head_pair(array, offset, lane_width, head_size):
    section = lax.dynamic_slice_in_dim(array, offset, lane_width, 2)
    return section.reshape(section.shape[0], section.shape[1], 2, head_size)


def add_lanes(target, addend, offset):
    current = lax.dynamic_slice_in_dim(target, offset, addend.shape[2], 2)
    return lax.dynamic_update_slice_in_dim(target, current + addend, offset, 2)


def pair_probs(query_pair, key_pair, log_pair, mask, scale):
    scores = (
        jnp.einsum("qchd,kchd->chqk", query_pair, key_pair, preferred_element_type=jnp.float32)
        * scale
        + mask
    )
    return jnp.exp(scores - jnp.transpose(log_pair, (1, 2, 0))[..., None])


def per_device_gathered(
    patches,
    col_counts,
    norm_gain,
    norm_shift,
    joint_proj,
    proj_bias,
    out_proj,
    up_proj,
    up_bias,
    down_proj,
    out_bias,
    cotangent,
):
    slots, clips, width = patches.shape
    row_count = slots * clips
    lane_width = 2 * DH
    pair_count = HEADS // 2
    scale = 1.0 / math.sqrt(DH)
    freq_size = lax.axis_size("freq")
    time_size = lax.axis_size("tm")
    freq_rows = FREQ_ROWS // freq_size
    cap_cols = (slots - 2) // freq_rows
    key_count = slots * freq_size * time_size
    slot_ids = jnp.arange(slots, dtype=jnp.int32)
    own_live = live_slots(
        col_counts,
        slot_ids,
        jnp.full((slots,), lax.axis_index("freq"), jnp.int32),
        jnp.full((slots,), lax.axis_index("tm"), jnp.int32),
        freq_rows,
        cap_cols,
    )
    key_ids = jnp.arange(key_count, dtype=jnp.int32)
    key_group = key_ids // slots
    key_live = live_slots(
        col_counts,
        key_ids % slots,
        key_group // time_size,
        key_group % time_size,
        freq_rows,
        cap_cols,
    )
    key_mask = jnp.where(key_live, 0.0, NEG).astype(jnp.float32)
    row_live = (
        jnp.broadcast_to(own_live[:, None], (slots, clips))
        .reshape(row_count, 1)
        .astype(jnp.float32)
    )
    gain_full = norm_gain.astype(jnp.float32)
    shift_full = norm_shift.astype(jnp.float32)
    bias_full = proj_bias.astype(jnp.float32)
    outb_full = out_bias.astype(jnp.float32)
    upb_full = up_bias.astype(jnp.float32)
    inputs = patches.reshape(row_count, width).astype(jnp.float32)
    normed1, ln1_back = jax.vjp(norm_rows, inputs, gain_full[0], shift_full[0])
    normed1_low = normed1.astype(jnp.bfloat16)
    joint = matmul(normed1_low, joint_proj)
    query_low = (joint[:, :width] + bias_full[0]).astype(jnp.bfloat16)
    keys_low = joint[:, width : 2 * width].astype(jnp.bfloat16)
    memory_low = (joint[:, 2 * width :] + bias_full[1]).astype(jnp.bfloat16)
    query3 = query_low.reshape(slots, clips, width)
    key_value = jnp.concatenate([keys_low, memory_low], axis=1).reshape(slots, clips, 2 * width)
    all_memory = lax.all_gather(key_value, ("freq", "tm"), axis=0, tiled=True)

    def forward_pair(number, state):
        mixed_acc, log_acc = state
        offset = number * lane_width
        query_pair = head_pair(query3, offset, lane_width, DH)
        key_pair = head_pair(all_memory, offset, lane_width, DH)
        value_pair = head_pair(all_memory, width + offset, lane_width, DH)
        scores = (
            jnp.einsum("qchd,kchd->chqk", query_pair, key_pair, preferred_element_type=jnp.float32)
            * scale
            + key_mask
        )
        highest = jnp.max(scores, axis=-1, keepdims=True)
        exponent = jnp.exp(scores - highest)
        summed = jnp.sum(exponent, axis=-1, keepdims=True)
        attention = (exponent / summed).astype(jnp.bfloat16)
        mixed = jnp.einsum(
            "chqk,kchd->qchd", attention, value_pair, preferred_element_type=jnp.float32
        )
        log_pair = jnp.transpose((highest + jnp.log(summed))[..., 0], (2, 0, 1))
        mixed_acc = lax.dynamic_update_slice_in_dim(
            mixed_acc, mixed.reshape(slots, clips, lane_width), offset, 2
        )
        log_acc = lax.dynamic_update_slice_in_dim(log_acc, log_pair, 2 * number, 2)
        return (mixed_acc, log_acc)

    mixed_full, log_rows = lax.fori_loop(
        0,
        pair_count,
        forward_pair,
        (
            jnp.zeros((slots, clips, width), jnp.float32),
            jnp.zeros((slots, clips, HEADS), jnp.float32),
        ),
    )
    mixed_low = mixed_full.reshape(row_count, width).astype(jnp.bfloat16)
    middle = inputs + matmul(mixed_low, out_proj) + outb_full[0]
    normed2, ln2_back = jax.vjp(norm_rows, middle, gain_full[1], shift_full[1])
    normed2_low = normed2.astype(jnp.bfloat16)
    pre_act = matmul(normed2_low, up_proj) + upb_full
    activated, gelu_back = jax.vjp(gelu_exact, pre_act)
    hidden_low = activated.astype(jnp.bfloat16)
    final = middle + matmul(hidden_low, down_proj) + outb_full[1]
    output = (final * row_live).astype(jnp.bfloat16).reshape(slots, clips, width)
    grad_out_rows = cotangent.reshape(row_count, width).astype(jnp.float32) * row_live
    grad_out_low = grad_out_rows.astype(jnp.bfloat16)
    grad_down_part = matmul_tn(hidden_low, grad_out_low)
    grad_outb_mlp = jnp.sum(grad_out_rows, axis=0)
    grad_hidden = matmul_nt(grad_out_low, down_proj)
    grad_pre_low = gelu_back(grad_hidden)[0].astype(jnp.bfloat16)
    grad_up_part = matmul_tn(normed2_low, grad_pre_low)
    grad_upb_part = jnp.sum(grad_pre_low.astype(jnp.float32), axis=0)
    grad_normed2 = matmul_nt(grad_pre_low, up_proj)
    grad_mid_part, grad_gain_mlp, grad_shift_mlp = ln2_back(grad_normed2)
    grad_middle = grad_out_rows + grad_mid_part
    grad_branch = grad_middle.astype(jnp.bfloat16)
    grad_outp_part = matmul_tn(mixed_low, grad_branch)
    grad_outb_attn = jnp.sum(grad_branch.astype(jnp.float32), axis=0)
    grad_mixed_low = matmul_nt(grad_branch, out_proj).astype(jnp.bfloat16)
    grad_mixed3 = grad_mixed_low.reshape(slots, clips, width)

    def query_side(number):
        offset = number * lane_width
        query_pair = head_pair(query3, offset, lane_width, DH)
        grad_pair = head_pair(grad_mixed3, offset, lane_width, DH)
        key_pair = head_pair(all_memory, offset, lane_width, DH)
        value_pair = head_pair(all_memory, width + offset, lane_width, DH)
        log_pair = lax.dynamic_slice_in_dim(log_rows, 2 * number, 2, 2)
        probability = pair_probs(query_pair, key_pair, log_pair, key_mask, scale)
        grad_probs = jnp.einsum(
            "qchd,kchd->chqk", grad_pair, value_pair, preferred_element_type=jnp.float32
        )
        delta = jnp.sum(probability * grad_probs, axis=-1, keepdims=True)
        grad_scores = (probability * (grad_probs - delta)).astype(jnp.bfloat16)
        grad_query = (
            jnp.einsum("chqk,kchd->qchd", grad_scores, key_pair, preferred_element_type=jnp.float32)
            * scale
        )
        return (
            offset,
            query_pair,
            grad_pair,
            probability,
            grad_scores,
            delta,
            grad_query.reshape(slots, clips, lane_width),
        )

    zero_query = jnp.zeros((slots, clips, width), jnp.float32)

    def backward_pair(number, state):
        grad_query_acc, grad_memory = state
        side = query_side(number)
        offset = side[0]
        grad_keys = (
            jnp.einsum("chqk,qchd->kchd", side[4], side[1], preferred_element_type=jnp.float32)
            * scale
        )
        grad_values = jnp.einsum(
            "chqk,qchd->kchd",
            side[3].astype(jnp.bfloat16),
            side[2],
            preferred_element_type=jnp.float32,
        )
        grad_memory = add_lanes(
            grad_memory, grad_keys.reshape(key_count, clips, lane_width), offset
        )
        grad_memory = add_lanes(
            grad_memory, grad_values.reshape(key_count, clips, lane_width), width + offset
        )
        return (add_lanes(grad_query_acc, side[6], offset), grad_memory)

    grad_query_full, grad_memory_all = lax.fori_loop(
        0,
        pair_count,
        backward_pair,
        (zero_query, jnp.zeros((key_count, clips, 2 * width), jnp.float32)),
    )
    grad_memory_own = lax.psum_scatter(
        grad_memory_all, ("freq", "tm"), scatter_dimension=0, tiled=True
    )
    grad_query_low = grad_query_full.reshape(row_count, width).astype(jnp.bfloat16)
    grad_memory_low = grad_memory_own.reshape(row_count, 2 * width).astype(jnp.bfloat16)
    grad_joint = jnp.concatenate([grad_query_low, grad_memory_low], axis=1)
    grad_joint_part = matmul_tn(normed1_low, grad_joint)
    grad_bias_cols = jnp.stack(
        [
            jnp.sum(grad_query_low.astype(jnp.float32), axis=0),
            jnp.sum(grad_memory_low[:, width:].astype(jnp.float32), axis=0),
        ],
        axis=1,
    )
    grad_normed1 = matmul_nt(grad_joint, joint_proj)
    grad_in_part, grad_gain_attn, grad_shift_attn = ln1_back(grad_normed1)
    grad_patches = (grad_middle + grad_in_part).astype(jnp.bfloat16).reshape(slots, clips, width)
    shares = (
        lax.psum_scatter(
            grad_joint_part.astype(jnp.bfloat16), ("freq", "tm"), scatter_dimension=0, tiled=True
        ).astype(jnp.float32),
        lax.psum_scatter(
            grad_bias_cols.astype(jnp.bfloat16), ("freq", "tm"), scatter_dimension=0, tiled=True
        ).astype(jnp.float32),
        lax.psum_scatter(
            grad_outp_part.astype(jnp.bfloat16), ("freq", "tm"), scatter_dimension=0, tiled=True
        ).astype(jnp.float32),
        lax.psum_scatter(
            grad_outb_attn.astype(jnp.bfloat16), ("freq", "tm"), scatter_dimension=0, tiled=True
        ).astype(jnp.float32),
        lax.psum_scatter(
            grad_gain_attn.astype(jnp.bfloat16), ("freq", "tm"), scatter_dimension=0, tiled=True
        ).astype(jnp.float32),
        lax.psum_scatter(
            grad_shift_attn.astype(jnp.bfloat16), ("freq", "tm"), scatter_dimension=0, tiled=True
        ).astype(jnp.float32),
        lax.psum_scatter(
            grad_up_part.astype(jnp.bfloat16), ("freq", "tm"), scatter_dimension=0, tiled=True
        ).astype(jnp.float32),
        lax.psum_scatter(
            grad_upb_part.astype(jnp.bfloat16), ("freq", "tm"), scatter_dimension=0, tiled=True
        ).astype(jnp.float32),
        lax.psum_scatter(
            grad_down_part.astype(jnp.bfloat16), ("freq", "tm"), scatter_dimension=0, tiled=True
        ).astype(jnp.float32),
        lax.psum_scatter(
            grad_outb_mlp.astype(jnp.bfloat16), ("freq", "tm"), scatter_dimension=0, tiled=True
        ).astype(jnp.float32),
        lax.psum_scatter(
            grad_gain_mlp.astype(jnp.bfloat16), ("freq", "tm"), scatter_dimension=0, tiled=True
        ).astype(jnp.float32),
        lax.psum_scatter(
            grad_shift_mlp.astype(jnp.bfloat16), ("freq", "tm"), scatter_dimension=0, tiled=True
        ).astype(jnp.float32),
    )
    summed_all = (
        lax.psum(shares[0].astype(jnp.bfloat16), "dp").astype(jnp.float32),
        lax.psum(shares[1].astype(jnp.bfloat16), "dp").astype(jnp.float32),
        lax.psum(shares[2].astype(jnp.bfloat16), "dp").astype(jnp.float32),
        lax.psum(shares[3].astype(jnp.bfloat16), "dp").astype(jnp.float32),
        lax.psum(shares[4].astype(jnp.bfloat16), "dp").astype(jnp.float32),
        lax.psum(shares[5].astype(jnp.bfloat16), "dp").astype(jnp.float32),
        lax.psum(shares[6].astype(jnp.bfloat16), "dp").astype(jnp.float32),
        lax.psum(shares[7].astype(jnp.bfloat16), "dp").astype(jnp.float32),
        lax.psum(shares[8].astype(jnp.bfloat16), "dp").astype(jnp.float32),
        lax.psum(shares[9].astype(jnp.bfloat16), "dp").astype(jnp.float32),
        lax.psum(shares[10].astype(jnp.bfloat16), "dp").astype(jnp.float32),
        lax.psum(shares[11].astype(jnp.bfloat16), "dp").astype(jnp.float32),
    )
    attn_summed = summed_all[:6]
    mlp_summed = summed_all[6:]
    grad_norm_gain = jnp.stack([attn_summed[4], mlp_summed[4]])
    grad_norm_shift = jnp.stack([attn_summed[5], mlp_summed[5]])
    grad_out_bias = jnp.stack([attn_summed[3], mlp_summed[3]])
    grad_proj_bias = jnp.transpose(attn_summed[1])
    return (
        output,
        grad_patches,
        grad_norm_gain,
        grad_norm_shift,
        attn_summed[0],
        grad_proj_bias,
        attn_summed[2],
        mlp_summed[0],
        mlp_summed[1],
        mlp_summed[2],
        grad_out_bias,
    )


LOG2E = 1.4426950408889634
LANES = 128
F32 = jnp.float32
BF16 = jnp.bfloat16
VMEM_LIMIT = 62 << 20
SAFE_RANGE = 100.0
CHUNKS = 4
HALVES = 2
SPAN = 1024
COLLECT_FLOPS = 30 * 10**9


def normalize(values):
    centered = values - jnp.mean(values, axis=-1, keepdims=True)
    inverse = lax.rsqrt(jnp.mean(centered * centered, axis=-1, keepdims=True) + EPS)
    return centered * inverse, inverse


def norm_back(normed, inverse, incoming, gain):
    scaled = incoming * gain
    mean = jnp.mean(scaled, axis=-1, keepdims=True)
    slope = jnp.mean(scaled * normed, axis=-1, keepdims=True)
    return (scaled - mean - normed * slope) * inverse


def spans_of(tokens):
    return [slice(at, min(at + SPAN, 2 * tokens)) for at in range(0, 2 * tokens, SPAN)]


def column_sum(values):
    return jnp.sum(values, axis=0, keepdims=True)


def project_kernel(x_ref, live_ref, w_ref, vec_ref, rows_ref, n_ref, q_ref, k_ref, v_ref, first_key, rows):
    blocks, slots, width = x_ref.shape
    padded = rows.shape[0] // blocks

    @pl.when(pl.program_id(0) == 0)
    def _():
        rows[...] = jnp.zeros_like(rows)

    for block in range(blocks):
        rows[block * padded : block * padded + slots] = x_ref[block].astype(F32)
    rows_ref[...] = rows[...].astype(BF16)
    normed, _ = normalize(rows[...])
    low = (normed * vec_ref[0:1, :] + vec_ref[1:2, :]).astype(BF16)
    n_ref[...] = low
    q_ref[...] = (matmul(low, w_ref[:, 0:width]) + vec_ref[2:3, :]).astype(BF16)
    keys = matmul(low, w_ref[:, width : 2 * width]).astype(BF16).astype(F32)

    @pl.when(pl.program_id(0) == 0)
    def _():
        first_key[...] = jnp.broadcast_to(keys[0:1, :], first_key.shape)

    k_ref[...] = jnp.where(live_ref[:, 0:1] > 0, keys, first_key[0:1, :]).astype(BF16)
    v_ref[...] = (matmul(low, w_ref[:, 2 * width : 3 * width]) + vec_ref[3:4, :]).astype(BF16)


def project(blocks, live_lanes, joint_proj, vectors, steps=4):
    members, slots, width = blocks.shape
    tokens = live_lanes.shape[0]
    rows = tokens // steps
    block = pl.BlockSpec((rows, width), lambda step: (step, 0))
    return pl.pallas_call(
        project_kernel,
        grid=(steps,),
        in_specs=[
            pl.BlockSpec((members // steps, slots, width), lambda step: (step, 0, 0)),
            pl.BlockSpec((rows, LANES), lambda step: (step, 0)),
            pl.BlockSpec((width, 3 * width), lambda step: (0, 0), pipeline_mode=pl.Buffered(1)),
            pl.BlockSpec((8, width), lambda step: (0, 0)),
        ],
        out_specs=[block] * 5,
        out_shape=[jax.ShapeDtypeStruct((tokens, width), BF16)] * 5,
        scratch_shapes=[pltpu.VMEM((8, width), F32), pltpu.VMEM((rows, width), F32)],
        compiler_params=pltpu.CompilerParams(vmem_limit_bytes=VMEM_LIMIT),
        cost_estimate=pl.CostEstimate(
            flops=6 * tokens * width * width, transcendentals=tokens, bytes_accessed=10 * tokens * width
        ),
    )(blocks, live_lanes, joint_proj, vectors)


def attention_forward_kernel(q_ref, k_ref, v_ref, live_ref, o_ref, rn_ref, p_ref, qs, vt, ot, sa, p_buf, p_sem):
    tokens = q_ref.shape[0]
    pair = pl.program_id(0)
    slot = lax.rem(pair, 2)
    spans = spans_of(tokens)

    def copy_of(pair, slot, index):
        span = spans[index]
        columns = pl.ds(span.start, span.stop - span.start)
        return pltpu.make_async_copy(
            p_buf.at[slot, :, columns], p_ref.at[pair, :, columns], p_sem.at[slot, index]
        )

    @pl.when(pair >= 2)
    def _():
        for index in range(len(spans)):
            copy_of(pair - 2, slot, index).wait()

    lane = lax.broadcasted_iota(jnp.int32, (tokens, LANES), 1)
    query = q_ref[...].astype(F32) * (1.0 / math.sqrt(DH))
    keys = k_ref[...].astype(F32)
    qs[0:tokens, :] = jnp.where(lane < DH, query, 0.0).astype(BF16)
    qs[tokens : 2 * tokens, :] = jnp.where(lane < DH, 0.0, query).astype(BF16)
    live = live_ref[0:1, :]
    vt[0:LANES, :] = (jnp.transpose(v_ref[...].astype(F32)) * live).astype(BF16)
    vt[LANES : LANES + 16, :] = jnp.broadcast_to(live, (16, tokens)).astype(BF16)

    def largest(values, head):
        squares = jnp.where((lane < DH) == (head == 0), values * values, 0.0)
        return jnp.max(jnp.sum(squares, axis=1, keepdims=True))

    limit = (SAFE_RANGE / LOG2E) ** 2
    bound = jnp.maximum(
        largest(query, 0) * largest(keys, 0), largest(query, 1) * largest(keys, 1)
    )
    bounded = bound <= limit

    def finish(span, weight):
        p_buf[slot, :, span] = weight
        ot[:, span] = matmul(vt[...], weight)

    @pl.when(bounded)
    def _():
        for index, span in enumerate(spans):
            finish(span, jnp.exp2(matmul_nt(k_ref[...], qs[span, :]) * LOG2E).astype(BF16))
            copy_of(pair, slot, index).start()

    @pl.when(jnp.logical_not(bounded))
    def _():
        def column(index, _):
            part = pl.ds(pl.multiple_of(index * LANES, LANES), LANES)
            sa[...] = matmul_nt(k_ref[...], qs[part, :])
            score = sa[...]
            highest = jnp.max(score, axis=0, keepdims=True)
            finish(part, jnp.exp2(score * LOG2E - highest * LOG2E).astype(BF16))
            return 0

        lax.fori_loop(0, 2 * tokens // LANES, column, 0)
        for index in range(len(spans)):
            copy_of(pair, slot, index).start()

    row = lax.broadcasted_iota(jnp.int32, (LANES, tokens), 0)
    inverse = jnp.where(
        row < DH,
        jnp.broadcast_to(1.0 / ot[LANES : LANES + 1, 0:tokens], (LANES, tokens)),
        jnp.broadcast_to(1.0 / ot[LANES : LANES + 1, tokens : 2 * tokens], (LANES, tokens)),
    )
    mixed = jnp.where(row < DH, ot[0:LANES, 0:tokens], ot[0:LANES, tokens : 2 * tokens]) * inverse
    o_ref[...] = jnp.transpose(mixed).astype(BF16)
    rn_ref[...] = jnp.transpose(inverse)

    @pl.when(pair == pl.num_programs(0) - 1)
    def _():
        for index in range(len(spans)):
            copy_of(pair - 1, 1 - slot, index).wait()
        for index in range(len(spans)):
            copy_of(pair, slot, index).wait()


def attention_forward(query, keys, memory, live_row):
    tokens, width = query.shape
    pairs = width // LANES
    block = pl.BlockSpec((tokens, LANES), lambda pair: (0, pair))
    return pl.pallas_call(
        attention_forward_kernel,
        grid=(pairs,),
        in_specs=[block, block, block, pl.BlockSpec((8, tokens), lambda pair: (0, 0))],
        out_specs=[block, block, pl.BlockSpec(memory_space=pl.ANY)],
        out_shape=[
            jax.ShapeDtypeStruct((tokens, width), BF16),
            jax.ShapeDtypeStruct((tokens, width), F32),
            jax.ShapeDtypeStruct((pairs, tokens, 2 * tokens), BF16),
        ],
        scratch_shapes=[
            pltpu.VMEM((2 * tokens, LANES), BF16),
            pltpu.VMEM((LANES + 16, tokens), BF16),
            pltpu.VMEM((LANES + 16, 2 * tokens), F32),
            pltpu.VMEM((tokens, LANES), F32),
            pltpu.VMEM((2, tokens, 2 * tokens), BF16),
            pltpu.SemaphoreType.DMA((2, len(spans_of(tokens)))),
        ],
        compiler_params=pltpu.CompilerParams(vmem_limit_bytes=VMEM_LIMIT),
        cost_estimate=pl.CostEstimate(
            flops=8 * pairs * tokens * tokens * LANES,
            transcendentals=2 * pairs * tokens * tokens,
            bytes_accessed=4 * pairs * tokens * tokens,
        ),
    )(query, keys, memory, live_row)


def attention_backward_kernel(
    q_ref, k_ref, v_ref, o_ref, do_ref, rn_ref, live_ref, keep_ref, p_ref, n_ref, w_ref,
    x_ref, res_ref, vec_ref, sums_ref, half_ref, out_ref,
    kept_ref, sent_ref, rows_ref, qs, gs, kt, dqt, delta, dj, vecs, n_buf, w_buf, x_buf, res_buf, dx_buf, sem, dx_sem,
):
    tokens = q_ref.shape[0]
    pair = pl.program_id(0)

    late = [
        pltpu.make_async_copy(source, target, sem.at[index])
        for index, (source, target) in enumerate(
            ((n_ref, n_buf), (w_ref, w_buf), (x_ref, x_buf), (res_ref, res_buf))
        )
    ]

    @pl.when(pair == 0)
    def _():
        for copy in late:
            copy.start()

    scale = 1.0 / math.sqrt(DH)
    lane = lax.broadcasted_iota(jnp.int32, (tokens, LANES), 1)
    query = q_ref[...].astype(F32) * scale
    qs[0:tokens, :] = jnp.where(lane < DH, query, 0.0).astype(BF16)
    qs[tokens : 2 * tokens, :] = jnp.where(lane < DH, 0.0, query).astype(BF16)
    grad = do_ref[...].astype(F32) * rn_ref[...]
    gs[0:tokens, :] = jnp.where(lane < DH, grad, 0.0).astype(BF16)
    gs[tokens : 2 * tokens, :] = jnp.where(lane < DH, 0.0, grad).astype(BF16)
    kt[...] = (jnp.transpose(k_ref[...].astype(F32)) * (live_ref[0:1, :] * scale)).astype(BF16)
    product = jnp.transpose(grad * o_ref[...].astype(F32))
    for head in range(2):
        total = column_sum(product[head * DH : (head + 1) * DH])
        delta[:, head * tokens : (head + 1) * tokens] = jnp.broadcast_to(total, (8, tokens))
    grad_keys = grad_values = None
    for span in spans_of(tokens):
        weight = p_ref[0, :, span]
        grad_weight = matmul_nt(v_ref[...], gs[span, :])
        grad_score = (weight.astype(F32) * (grad_weight - delta[0:1, span])).astype(BF16)
        dqt[:, span] = matmul(kt[...], grad_score)
        part_values = matmul(weight, gs[span, :])
        part_keys = matmul(grad_score, qs[span, :])
        grad_values = part_values if grad_values is None else grad_values + part_values
        grad_keys = part_keys if grad_keys is None else grad_keys + part_keys
    row = lax.broadcasted_iota(jnp.int32, (LANES, tokens), 0)
    grad_query = jnp.transpose(jnp.where(row < DH, dqt[:, 0:tokens], dqt[:, tokens : 2 * tokens]))
    keep = keep_ref[...] > 0
    width = x_buf.shape[1]
    parts = (
        grad_query.astype(BF16),
        jnp.where(keep, grad_keys, 0.0).astype(BF16),
        jnp.where(keep, grad_values, 0.0).astype(BF16),
    )
    for part, value in enumerate(parts):
        columns = pl.ds(pl.multiple_of(part * width + pl.program_id(0) * LANES, LANES), LANES)
        dj[:, columns] = value
        if part != 1:
            columns = pl.ds(pl.multiple_of(pl.program_id(0) * LANES, LANES), LANES)
            vecs[2 + part // 2 : 3 + part // 2, columns] = column_sum(value.astype(F32))

    @pl.when(pl.program_id(0) == pl.num_programs(0) - 1)
    def _():
        for copy in late:
            copy.wait()
        first = half_ref[0] == 0
        half = width // 2
        for part in range(3):
            span = slice(part * width, (part + 1) * width)
            grad_weights = matmul_tn(n_buf[...], dj[:, span]).astype(BF16)
            kept_ref[:, span] = jnp.where(first, grad_weights[:half], grad_weights[half:])
            sent_ref[:, span] = jnp.where(first, grad_weights[half:], grad_weights[:half])
        vecs[4:8, :] = sums_ref[0:4, :]
        rows = tokens // CHUNKS
        block = tokens // rows_ref.shape[0]
        stores = []
        gain_sum = shift_sum = 0.0
        for start in range(0, tokens, rows):
            span = slice(start, start + rows)
            incoming = matmul_nt(dj[span, :], w_buf[...])
            normed, inverse = normalize(x_buf[span, :].astype(F32))
            gain_sum += column_sum(incoming * normed)
            shift_sum += column_sum(incoming)
            back = norm_back(normed, inverse, incoming, vec_ref[0:1, :])
            grad_rows = (res_buf[span, :].astype(F32) + back).astype(BF16)
            for part in range(rows // block):
                dx_buf[start // block + part] = grad_rows[part * block : part * block + dx_buf.shape[1]]
            stores.append(
                pltpu.make_async_copy(
                    dx_buf.at[pl.ds(start // block, rows // block)],
                    rows_ref.at[pl.ds(start // block, rows // block), 0],
                    dx_sem.at[start // rows],
                )
            )
            stores[-1].start()
        vecs[0:1, :] = gain_sum
        vecs[1:2, :] = shift_sum
        turned = jnp.transpose(jnp.concatenate([vecs[...]] * (LANES // 8), axis=0)).astype(BF16)
        tail = kept_ref.shape[1] - LANES
        kept_ref[:, tail:] = jnp.where(first, turned[:half], turned[half:])
        sent_ref[:, tail:] = jnp.where(first, turned[half:], turned[:half])
        for copy in stores:
            copy.wait()


def attention_backward(
    query, keys, memory, mixed, grad_mixed, inverse, live_row, live_lanes, weights, normed, joint_proj,
    inputs, residual, vectors, vector_grads, own_half, output,
):
    tokens, width = query.shape
    pairs = width // LANES
    block = pl.BlockSpec((tokens, LANES), lambda pair: (0, pair))
    once = pl.Buffered(1)
    anywhere = pl.BlockSpec(memory_space=pl.ANY)

    def fixed(rows, columns):
        return pl.BlockSpec((rows, columns), lambda pair: (0, 0), pipeline_mode=once)

    return pl.pallas_call(
        attention_backward_kernel,
        grid=(pairs,),
        in_specs=[block] * 6
        + [
            fixed(8, tokens),
            fixed(tokens, LANES),
            pl.BlockSpec((1, tokens, 2 * tokens), lambda pair: (pair, 0, 0)),
            anywhere,
            anywhere,
            anywhere,
            anywhere,
            fixed(8, width),
            fixed(8, width),
            pl.BlockSpec(memory_space=pltpu.SMEM),
            anywhere,
        ],
        out_specs=[fixed(width // 2, 3 * width + LANES), fixed(width // 2, 3 * width + LANES), anywhere],
        out_shape=[
            jax.ShapeDtypeStruct((width // 2, 3 * width + LANES), BF16),
            jax.ShapeDtypeStruct((width // 2, 3 * width + LANES), BF16),
            jax.ShapeDtypeStruct(output.shape, BF16),
        ],
        scratch_shapes=[
            pltpu.VMEM((2 * tokens, LANES), BF16),
            pltpu.VMEM((2 * tokens, LANES), BF16),
            pltpu.VMEM((LANES, tokens), BF16),
            pltpu.VMEM((LANES, 2 * tokens), F32),
            pltpu.VMEM((8, 2 * tokens), F32),
            pltpu.VMEM((tokens, 3 * width), BF16),
            pltpu.VMEM((8, width), F32),
            pltpu.VMEM((tokens, width), BF16),
            pltpu.VMEM((width, 3 * width), BF16),
            pltpu.VMEM((tokens, width), BF16),
            pltpu.VMEM((tokens, width), BF16),
            pltpu.VMEM((output.shape[0],) + output.shape[2:], BF16),
            pltpu.SemaphoreType.DMA((4,)),
            pltpu.SemaphoreType.DMA((CHUNKS,)),
        ],
        input_output_aliases={16: 2},
        compiler_params=pltpu.CompilerParams(vmem_limit_bytes=VMEM_LIMIT),
        cost_estimate=pl.CostEstimate(
            flops=16 * pairs * tokens * tokens * LANES,
            transcendentals=0,
            bytes_accessed=4 * pairs * tokens * tokens,
        ),
    )(
        query, keys, memory, mixed, grad_mixed, inverse, live_row, live_lanes, weights, normed,
        joint_proj, inputs, residual, vectors, vector_grads,
        own_half, output,
    )


def feed_forward_kernel(
    x_hbm, mixed_hbm, cot_hbm, live_ref, wo_ref, vec_ref, up_ref, down_ref, bias_ref,
    out_hbm, share_ref, branch_hbm, gm_hbm, packed_ref, ds_ref,
    x_ref, mixed_ref, cot_ref, out_ref, branch_ref, gm_ref,
    normed, grad_out, middle, acc, acc_grad, hidden, grad_pre, down_buf, up_buf, down_sem, up_sem, in_sem, out_sem,
):
    step = pl.program_id(0)
    last = pl.num_programs(0) - 1
    tokens, width = x_ref.shape
    units = up_ref.shape[1]
    rows = tokens // CHUNKS

    block = tokens // out_ref.shape[0]
    slots = out_ref.shape[1]
    parts = rows // block

    def rows_of_chunk(chunk):
        return pl.ds(pl.multiple_of(chunk * rows, 32), rows)

    def fetches(chunk):
        span = rows_of_chunk(chunk)
        pairs = ((x_hbm, x_ref), (mixed_hbm, mixed_ref), (cot_hbm, cot_ref))
        return [
            pltpu.make_async_copy(source.at[span], target.at[span], in_sem.at[chunk, index])
            for index, (source, target) in enumerate(pairs)
        ]

    def stores(chunk):
        span = rows_of_chunk(chunk)
        return [
            pltpu.make_async_copy(source.at[span], target.at[span], out_sem.at[chunk, index])
            for index, (source, target) in enumerate(((branch_ref, branch_hbm), (gm_ref, gm_hbm)))
        ] + [
            pltpu.make_async_copy(
                out_ref.at[pl.ds(chunk * parts, parts)],
                out_hbm.at[pl.ds(chunk * parts, parts), 1],
                out_sem.at[chunk, 2],
            )
        ]

    @pl.when(step == 0)
    def _():
        for chunk in range(CHUNKS):
            for copy in fetches(chunk):
                copy.start()

        def chunk_step(chunk, _):
            span = rows_of_chunk(chunk)
            for copy in fetches(chunk):
                copy.wait()
            values = x_ref[span, :].astype(F32) + matmul(mixed_ref[span, :], wo_ref[...]) + vec_ref[2:3, :]
            middle[span, :] = values
            acc[span, :] = values + vec_ref[3:4, :]
            unit, _ = normalize(values)
            normed[span, :] = (unit * vec_ref[0:1, :] + vec_ref[1:2, :]).astype(BF16)
            grad_out[span, :] = (cot_ref[span, :].astype(F32) * live_ref[span, 0:1]).astype(BF16)
            acc_grad[span, :] = jnp.zeros((rows, width), F32)
            return 0

        lax.fori_loop(0, CHUNKS, chunk_step, 0)

    up = up_ref[...]
    down = down_ref[...]
    half = tokens // HALVES

    def feed(index, grad_bias):
        span = pl.ds(pl.multiple_of(index * half, 32), half)
        pre_act = matmul(normed[span, :], up) + bias_ref[0:1, :]
        grad_hidden = matmul_nt(grad_out[span, :], down)
        cumulative = 0.5 + 0.5 * lax.erf(pre_act * math.sqrt(0.5))
        density = jnp.exp2(pre_act * pre_act * (-0.5 * LOG2E)) * (1.0 / math.sqrt(2.0 * math.pi))
        low = (pre_act * cumulative).astype(BF16)
        grad_low = (grad_hidden * (cumulative + pre_act * density)).astype(BF16)
        hidden[span, :] = low
        grad_pre[span, :] = grad_low
        acc[span, :] += matmul(low, down)
        acc_grad[span, :] += matmul_nt(grad_low, up)
        return grad_bias + column_sum(grad_low.astype(F32))

    grad_bias = lax.fori_loop(0, HALVES, feed, jnp.zeros((1, units), F32))
    slot = lax.rem(step, 2)
    _, cuts, quarters, share, _ = down_buf.shape
    own = units // cuts
    for cut in range(cuts):
        sums = jnp.broadcast_to(grad_bias[:, cut * own : (cut + 1) * own], (16, own)).astype(BF16)
        share_ref[step * cuts + cut, share : share + 16, 0:own] = sums
        share_ref[step * cuts + cut, share : share + 16, own:width] = jnp.zeros((16, width - own), BF16)

    def copies(at, slot):
        return (
            pltpu.make_async_copy(
                down_buf.at[slot], packed_ref.at[pl.ds(at * cuts, cuts), pl.ds(0, quarters)], down_sem.at[slot]
            ),
            pltpu.make_async_copy(up_buf.at[slot], packed_ref.at[:, quarters + at], up_sem.at[slot]),
        )

    @pl.when(step >= 2)
    def _():
        for copy in copies(step - 2, slot):
            copy.wait()

    grad_down = matmul_tn(hidden[...], grad_out[...]).astype(BF16)
    for cut in range(cuts):
        for quarter in range(quarters):
            base = (cut * quarters + quarter) * share
            down_buf[slot, cut, quarter] = grad_down[base : base + share]
    grad_up = matmul_tn(normed[...], grad_pre[...]).astype(BF16)
    for member in range(width // share):
        up_buf[slot, member] = grad_up[member * share : (member + 1) * share]
    for copy in copies(step, slot):
        copy.start()

    @pl.when(step == last)
    def _():
        ds_ref[...] = jnp.zeros_like(ds_ref)

        def chunk_step(chunk, _):
            span = rows_of_chunk(chunk)
            final = (acc[span, :] * live_ref[span, 0:1]).astype(BF16)
            for part in range(parts):
                out_ref[chunk * parts + part] = final[part * block : part * block + slots]
            unit, inverse = normalize(middle[span, :])
            incoming = acc_grad[span, :]
            start = grad_out[span, :].astype(F32)
            branch = (start + norm_back(unit, inverse, incoming, vec_ref[0:1, :])).astype(BF16)
            branch_ref[span, :] = branch
            gm_ref[span, :] = matmul_nt(branch, wo_ref[...]).astype(BF16)
            for copy in stores(chunk):
                copy.start()
            for place, term in enumerate((incoming * unit, incoming, branch.astype(F32), start)):
                ds_ref[place : place + 1, :] += column_sum(term)
            return 0

        lax.fori_loop(0, CHUNKS, chunk_step, 0)
        grad_outp = matmul_tn(mixed_ref[...], branch_ref[...]).astype(BF16)
        for member in range(width // share):
            share_ref[member, 0:share, :] = grad_outp[member * share : (member + 1) * share]
        for chunk in range(CHUNKS):
            for copy in stores(chunk):
                copy.wait()
        for copy in copies(step - 1, 1 - slot):
            copy.wait()
        for copy in copies(step, slot):
            copy.wait()


def feed_forward(
    inputs, mixed, cotangent, live_lanes, out_proj, vectors, up_proj, up_bias, down_proj, members, slots
):
    tokens, width = inputs.shape
    hidden_units = up_proj.shape[1]
    steps = hidden_units // width
    share = width // members
    cuts = members // steps
    quarters = hidden_units // members // share
    once = pl.Buffered(1)
    anywhere = pl.BlockSpec(memory_space=pl.ANY)

    def fixed(rows, columns):
        return pl.BlockSpec((rows, columns), lambda step: (0, 0), pipeline_mode=once)

    return pl.pallas_call(
        feed_forward_kernel,
        grid=(steps,),
        in_specs=[
            anywhere,
            anywhere,
            anywhere,
            fixed(tokens, LANES),
            fixed(width, width),
            fixed(8, width),
            pl.BlockSpec((width, width), lambda step: (0, step)),
            pl.BlockSpec((width, width), lambda step: (step, 0)),
            pl.BlockSpec((8, width), lambda step: (0, step)),
        ],
        out_specs=[
            anywhere,
            pl.BlockSpec((members, share + 16, width), lambda step: (0, 0, 0), pipeline_mode=once),
            anywhere,
            anywhere,
            anywhere,
            fixed(8, width),
        ],
        out_shape=[
            jax.ShapeDtypeStruct((members, 2, slots, width), BF16),
            jax.ShapeDtypeStruct((members, share + 16, width), BF16),
            jax.ShapeDtypeStruct((tokens, width), BF16),
            jax.ShapeDtypeStruct((tokens, width), BF16),
            jax.ShapeDtypeStruct((members, quarters + steps, share, width), BF16),
            jax.ShapeDtypeStruct((8, width), F32),
        ],
        scratch_shapes=[pltpu.VMEM((tokens, width), BF16)] * 3
        + [
            pltpu.VMEM((members, slots, width), BF16),
            pltpu.VMEM((tokens, width), BF16),
            pltpu.VMEM((tokens, width), BF16),
            pltpu.VMEM((tokens, width), BF16),
            pltpu.VMEM((tokens, width), BF16),
            pltpu.VMEM((tokens, width), F32),
            pltpu.VMEM((tokens, width), F32),
            pltpu.VMEM((tokens, width), F32),
            pltpu.VMEM((tokens, width), BF16),
            pltpu.VMEM((tokens, width), BF16),
            pltpu.VMEM((2, cuts, quarters, share, width), BF16),
            pltpu.VMEM((2, members, share, width), BF16),
            pltpu.SemaphoreType.DMA((2,)),
            pltpu.SemaphoreType.DMA((2,)),
            pltpu.SemaphoreType.DMA((CHUNKS, 3)),
            pltpu.SemaphoreType.DMA((CHUNKS, 3)),
        ],
        compiler_params=pltpu.CompilerParams(vmem_limit_bytes=VMEM_LIMIT),
        cost_estimate=pl.CostEstimate(
            flops=12 * tokens * width * hidden_units + 6 * tokens * width * width,
            transcendentals=2 * tokens * hidden_units,
            bytes_accessed=12 * tokens * width + 8 * width * hidden_units,
        ),
    )(inputs, mixed, cotangent, live_lanes, out_proj, vectors, up_proj, down_proj, up_bias)


def collect_joint_kernel(own_ref, *refs):
    pieces, (joint_ref, gain_ref, shift_ref, bias_ref, branch_ref, columns) = refs[:-6], refs[-6:]
    rows = pieces[0].shape[0]
    width = joint_ref.shape[1] // 3
    own = own_ref[0]
    columns[...] = jnp.zeros_like(columns)
    for place in range(len(pieces)):
        piece = pieces[place][...]
        for other in range(1, len(pieces)):
            piece = jnp.where(own == other, pieces[place ^ other][...], piece)
        piece = piece.astype(F32)
        span = slice(place * rows, (place + 1) * rows)
        joint_ref[span, :] = piece[:, : 3 * width]
        columns[span, :] = piece[:, 3 * width :]
    turned = jnp.transpose(columns[...])
    share = gain_ref.shape[1]
    gain_ref[0:1, :] = turned[0:1, 0:share]
    gain_ref[1:2, :] = turned[4:5, 0:share]
    shift_ref[0:1, :] = turned[1:2, 0:share]
    shift_ref[1:2, :] = turned[5:6, 0:share]
    bias_ref[...] = turned[2:4, 0:share]
    branch_ref[...] = turned[6:8, 0:share]


def collect_joint(own, pieces, share):
    width = (pieces[0].shape[1] - LANES) // 3
    vmem = pl.BlockSpec(memory_space=pltpu.VMEM)
    return pl.pallas_call(
        collect_joint_kernel,
        in_specs=[pl.BlockSpec(memory_space=pltpu.SMEM)] + [vmem] * len(pieces),
        out_specs=[vmem] * 5,
        out_shape=[jax.ShapeDtypeStruct((share, 3 * width), F32)] + [jax.ShapeDtypeStruct((2, share), F32)] * 4,
        scratch_shapes=[pltpu.VMEM((LANES, LANES), F32)],
        cost_estimate=pl.CostEstimate(flops=0, transcendentals=0, bytes_accessed=0),
    )(own, *pieces)


def collect_mlp_kernel(rows_ref, sums_ref, down_ref, up_ref, outp_ref, bias_ref):
    own, width = down_ref.shape
    share = outp_ref.shape[0]
    down_ref[...] = rows_ref[0:own, :].astype(F32)
    for part in range(own // share):
        rows = slice(own + part * share, own + (part + 1) * share)
        up_ref[:, part * width : (part + 1) * width] = rows_ref[rows, :].astype(F32)
    outp_ref[...] = sums_ref[0:share, :].astype(F32)
    bias_ref[...] = sums_ref[share : share + 16, 0:own].astype(F32)[0]


def collect_mlp(rows, sums, share):
    own, width = rows.shape[0] // 2, rows.shape[1]
    vmem = pl.BlockSpec(memory_space=pltpu.VMEM)
    return pl.pallas_call(
        collect_mlp_kernel,
        in_specs=[vmem] * 2,
        out_specs=[vmem] * 4,
        out_shape=[
            jax.ShapeDtypeStruct((own, width), F32),
            jax.ShapeDtypeStruct((share, own // share * width), F32),
            jax.ShapeDtypeStruct((share, width), F32),
            jax.ShapeDtypeStruct((own,), F32),
        ],
        cost_estimate=pl.CostEstimate(flops=COLLECT_FLOPS, transcendentals=0, bytes_accessed=4 * rows.size),
    )(rows, sums)


def per_device(
    patches,
    col_counts,
    norm_gain,
    norm_shift,
    joint_proj,
    proj_bias,
    out_proj,
    up_proj,
    up_bias,
    down_proj,
    out_bias,
    cotangent,
):
    slots, clips, width = patches.shape
    group = ("freq", "tm")
    freq_size = lax.axis_size("freq")
    time_size = lax.axis_size("tm")
    groups = lax.axis_size("dp")
    members = freq_size * time_size
    freq_rows = FREQ_ROWS // freq_size
    cap_cols = (slots - 2) // freq_rows
    padded = -(-slots // 16) * 16
    tokens = members * padded
    pairs = width // LANES
    share = width // members
    hidden_units = up_proj.shape[1]

    def to_clip(array):
        return lax.all_to_all(array, group, 0, 0, tiled=True)

    token_ids = jnp.arange(tokens, dtype=jnp.int32)
    block_ids = token_ids // padded
    live = live_slots(
        col_counts,
        token_ids % padded,
        block_ids // time_size,
        block_ids % time_size,
        freq_rows,
        cap_cols,
    ) & (token_ids % padded < slots)
    live_full = live.astype(F32)
    live_row = jnp.broadcast_to(live_full[None, :], (8, tokens))
    live_lanes = jnp.broadcast_to(live_full[:, None], (tokens, LANES))

    def rows_of(*vectors):
        stacked = jnp.stack(vectors).astype(F32)
        return jnp.pad(stacked, ((0, 8 - len(vectors)), (0, 0)))

    vectors1 = rows_of(norm_gain[0], norm_shift[0], proj_bias[0], proj_bias[1])
    vectors2 = rows_of(norm_gain[1], norm_shift[1], out_bias[0], out_bias[1])
    bias_rows = jnp.broadcast_to(up_bias.astype(F32)[None, :], (8, hidden_units))

    arrived = to_clip(jnp.transpose(patches, (1, 0, 2)))
    turned = jnp.pad(jnp.transpose(cotangent, (1, 0, 2)), ((0, 0), (0, padded - slots), (0, 0)))
    turned, live_lanes, live_row, vectors1, vectors2, bias_rows = lax.optimization_barrier(
        (turned, live_lanes, live_row, vectors1, vectors2, bias_rows)
    )
    cot = to_clip(turned).reshape(tokens, width)
    inputs, normed1, query, keys, memory = project(arrived, live_lanes, joint_proj, vectors1)
    mixed, inverse, weights = attention_forward(query, keys, memory, live_row)
    output, blocks, branch, grad_mixed, packed, vector_grads = feed_forward(
        inputs, mixed, cot, live_lanes, out_proj, vectors2, up_proj, bias_rows, down_proj, members, padded
    )
    own = hidden_units // members
    mlp_rows = lax.psum_scatter(packed.reshape(members, 2 * own, width), group, scatter_dimension=0, tiled=True)[0]
    moved = lax.all_to_all(blocks, group, 0, 0, tiled=True)

    own_half = lax.axis_index("freq")
    own_group = lax.axis_index("dp")
    kept, sent, token_rows = attention_backward(
        query, keys, memory, mixed, grad_mixed, inverse, live_row, live_lanes, weights, normed1, joint_proj,
        inputs, branch, vectors1, vector_grads, own_half.reshape(1),
        output,
    )
    kept, sent, moved = lax.optimization_barrier((kept, sent, moved))
    got = lax.ppermute(sent, "freq", [(0, 1), (1, 0)])
    outp_rows = jnp.sum(moved.astype(F32), axis=0).astype(BF16)
    joint_half = (kept.astype(F32) + got.astype(F32)).astype(BF16).reshape(time_size, share, kept.shape[1])
    joint_half, mlp_rows, outp_rows = lax.optimization_barrier((joint_half, mlp_rows, outp_rows))
    mlp_sum, outp_sum = lax.psum((mlp_rows, outp_rows), "dp")
    arrived = lax.all_to_all(joint_half, "tm", 0, 0, tiled=True)
    joint_rows = jnp.sum(arrived.astype(F32), axis=0).astype(BF16)
    joint_rows, token_rows = lax.optimization_barrier((joint_rows, token_rows))

    def to_group(array, distance):
        return lax.ppermute(array, "dp", [(i, i ^ distance) for i in range(groups)])

    cut = joint_rows.reshape(groups, share // groups, kept.shape[1])
    piece = lax.dynamic_index_in_dim(cut, own_group, 0, False).astype(F32)
    for distance in range(1, groups):
        piece += to_group(lax.dynamic_index_in_dim(cut, own_group ^ distance, 0, False), distance).astype(F32)
    piece = piece.astype(BF16)
    pieces = [piece] + [to_group(piece, distance) for distance in range(1, groups)]
    token_rows = lax.all_to_all(token_rows, group, 0, 0, tiled=True)
    grad_patches, output = (jnp.transpose(token_rows[:, kind, :slots], (1, 0, 2)) for kind in range(2))

    joint_sum, gain_sum, shift_sum, bias_sum, branch_sum = collect_joint(own_group.reshape(1), pieces, share)
    joint_sum, mlp_sum, outp_sum = lax.optimization_barrier((joint_sum, mlp_sum, outp_sum))
    down_sum, up_sum, outp_sum, up_bias_sum = collect_mlp(mlp_sum, outp_sum, share)
    return (
        output,
        grad_patches,
        gain_sum,
        shift_sum,
        joint_sum,
        bias_sum,
        outp_sum,
        up_sum,
        up_bias_sum,
        down_sum,
        branch_sum,
    )


def plan(patches, *others):
    members = lax.axis_size("freq") * lax.axis_size("tm")
    if patches.shape[1] == members:
        return per_device(patches, *others)
    return per_device_gathered(patches, *others)


def solution(mesh):
    return jax.shard_map(
        plan,
        mesh=mesh,
        in_specs=(
            P(("freq", "tm"), "dp", None),
            P(),
            P(),
            P(),
            P(),
            P(),
            P(),
            P(),
            P(),
            P(),
            P(),
            P(("freq", "tm"), "dp", None),
        ),
        out_specs=(
            P(("freq", "tm"), "dp", None),
            P(("freq", "tm"), "dp", None),
            P(None, ("freq", "tm")),
            P(None, ("freq", "tm")),
            P(("freq", "tm"), None),
            P(None, ("freq", "tm")),
            P(("freq", "tm"), None),
            P(("freq", "tm"), None),
            P(("freq", "tm")),
            P(("freq", "tm"), None),
            P(None, ("freq", "tm")),
        ),
        check_vma=False,
    )
```

```python
import functools
import math

import jax
import jax.numpy as jnp
from jax import lax
from jax.experimental import pallas as pl
from jax.experimental.pallas import tpu as pltpu
from jax.sharding import PartitionSpec as P

HEADS = 12
DH = 64
FREQ_ROWS = 12


EPS = 1e-06
NEG = -1000000000.0


def live_slots(col_counts, slot_ids, freq_ids, time_ids, freq_rows, cap_cols):
    table = jnp.arange(col_counts.shape[0], dtype=jnp.int32)
    live_cols = jnp.sum(
        jnp.where(time_ids[:, None] == table[None, :], col_counts[None, :], 0), axis=1
    )
    in_grid = slot_ids < freq_rows * cap_cols
    column_live = slot_ids // freq_rows < live_cols
    extra_live = (time_ids == 0) & (freq_ids == 0)
    return jnp.where(in_grid, column_live, extra_live)


def norm_rows(values, gain, shift):
    centered = values - jnp.mean(values, axis=-1, keepdims=True)
    inverse = lax.rsqrt(jnp.mean(centered * centered, axis=-1, keepdims=True) + EPS)
    return centered * inverse * gain + shift


def gelu_exact(values):
    return jax.nn.gelu(values, approximate=False)


def matmul(left, right):
    return jnp.dot(left, right, preferred_element_type=jnp.float32)


def matmul_tn(left, right):
    return lax.dot_general(
        left, right, (((0,), (0,)), ((), ())), preferred_element_type=jnp.float32
    )


def matmul_nt(left, right):
    return lax.dot_general(
        left, right, (((1,), (1,)), ((), ())), preferred_element_type=jnp.float32
    )


def head_pair(array, offset, lane_width, head_size):
    section = lax.dynamic_slice_in_dim(array, offset, lane_width, 2)
    return section.reshape(section.shape[0], section.shape[1], 2, head_size)


def add_lanes(target, addend, offset):
    current = lax.dynamic_slice_in_dim(target, offset, addend.shape[2], 2)
    return lax.dynamic_update_slice_in_dim(target, current + addend, offset, 2)


def pair_probs(query_pair, key_pair, log_pair, mask, scale):
    scores = (
        jnp.einsum("qchd,kchd->chqk", query_pair, key_pair, preferred_element_type=jnp.float32)
        * scale
        + mask
    )
    return jnp.exp(scores - jnp.transpose(log_pair, (1, 2, 0))[..., None])


def per_device_gathered(
    patches,
    col_counts,
    norm_gain,
    norm_shift,
    joint_proj,
    proj_bias,
    out_proj,
    up_proj,
    up_bias,
    down_proj,
    out_bias,
    cotangent,
):
    slots, clips, width = patches.shape
    row_count = slots * clips
    lane_width = 2 * DH
    pair_count = HEADS // 2
    scale = 1.0 / math.sqrt(DH)
    freq_size = lax.axis_size("freq")
    time_size = lax.axis_size("tm")
    freq_rows = FREQ_ROWS // freq_size
    cap_cols = (slots - 2) // freq_rows
    key_count = slots * freq_size * time_size
    slot_ids = jnp.arange(slots, dtype=jnp.int32)
    own_live = live_slots(
        col_counts,
        slot_ids,
        jnp.full((slots,), lax.axis_index("freq"), jnp.int32),
        jnp.full((slots,), lax.axis_index("tm"), jnp.int32),
        freq_rows,
        cap_cols,
    )
    key_ids = jnp.arange(key_count, dtype=jnp.int32)
    key_group = key_ids // slots
    key_live = live_slots(
        col_counts,
        key_ids % slots,
        key_group // time_size,
        key_group % time_size,
        freq_rows,
        cap_cols,
    )
    key_mask = jnp.where(key_live, 0.0, NEG).astype(jnp.float32)
    row_live = (
        jnp.broadcast_to(own_live[:, None], (slots, clips))
        .reshape(row_count, 1)
        .astype(jnp.float32)
    )
    gain_full = norm_gain.astype(jnp.float32)
    shift_full = norm_shift.astype(jnp.float32)
    bias_full = proj_bias.astype(jnp.float32)
    outb_full = out_bias.astype(jnp.float32)
    upb_full = up_bias.astype(jnp.float32)
    inputs = patches.reshape(row_count, width).astype(jnp.float32)
    normed1, ln1_back = jax.vjp(norm_rows, inputs, gain_full[0], shift_full[0])
    normed1_low = normed1.astype(jnp.bfloat16)
    joint = matmul(normed1_low, joint_proj)
    query_low = (joint[:, :width] + bias_full[0]).astype(jnp.bfloat16)
    keys_low = joint[:, width : 2 * width].astype(jnp.bfloat16)
    memory_low = (joint[:, 2 * width :] + bias_full[1]).astype(jnp.bfloat16)
    query3 = query_low.reshape(slots, clips, width)
    key_value = jnp.concatenate([keys_low, memory_low], axis=1).reshape(slots, clips, 2 * width)
    all_memory = lax.all_gather(key_value, ("freq", "tm"), axis=0, tiled=True)

    def forward_pair(number, state):
        mixed_acc, log_acc = state
        offset = number * lane_width
        query_pair = head_pair(query3, offset, lane_width, DH)
        key_pair = head_pair(all_memory, offset, lane_width, DH)
        value_pair = head_pair(all_memory, width + offset, lane_width, DH)
        scores = (
            jnp.einsum("qchd,kchd->chqk", query_pair, key_pair, preferred_element_type=jnp.float32)
            * scale
            + key_mask
        )
        highest = jnp.max(scores, axis=-1, keepdims=True)
        exponent = jnp.exp(scores - highest)
        summed = jnp.sum(exponent, axis=-1, keepdims=True)
        attention = (exponent / summed).astype(jnp.bfloat16)
        mixed = jnp.einsum(
            "chqk,kchd->qchd", attention, value_pair, preferred_element_type=jnp.float32
        )
        log_pair = jnp.transpose((highest + jnp.log(summed))[..., 0], (2, 0, 1))
        mixed_acc = lax.dynamic_update_slice_in_dim(
            mixed_acc, mixed.reshape(slots, clips, lane_width), offset, 2
        )
        log_acc = lax.dynamic_update_slice_in_dim(log_acc, log_pair, 2 * number, 2)
        return (mixed_acc, log_acc)

    mixed_full, log_rows = lax.fori_loop(
        0,
        pair_count,
        forward_pair,
        (
            jnp.zeros((slots, clips, width), jnp.float32),
            jnp.zeros((slots, clips, HEADS), jnp.float32),
        ),
    )
    mixed_low = mixed_full.reshape(row_count, width).astype(jnp.bfloat16)
    middle = inputs + matmul(mixed_low, out_proj) + outb_full[0]
    normed2, ln2_back = jax.vjp(norm_rows, middle, gain_full[1], shift_full[1])
    normed2_low = normed2.astype(jnp.bfloat16)
    pre_act = matmul(normed2_low, up_proj) + upb_full
    activated, gelu_back = jax.vjp(gelu_exact, pre_act)
    hidden_low = activated.astype(jnp.bfloat16)
    final = middle + matmul(hidden_low, down_proj) + outb_full[1]
    output = (final * row_live).astype(jnp.bfloat16).reshape(slots, clips, width)
    grad_out_rows = cotangent.reshape(row_count, width).astype(jnp.float32) * row_live
    grad_out_low = grad_out_rows.astype(jnp.bfloat16)
    grad_down_part = matmul_tn(hidden_low, grad_out_low)
    grad_outb_mlp = jnp.sum(grad_out_rows, axis=0)
    grad_hidden = matmul_nt(grad_out_low, down_proj)
    grad_pre_low = gelu_back(grad_hidden)[0].astype(jnp.bfloat16)
    grad_up_part = matmul_tn(normed2_low, grad_pre_low)
    grad_upb_part = jnp.sum(grad_pre_low.astype(jnp.float32), axis=0)
    grad_normed2 = matmul_nt(grad_pre_low, up_proj)
    grad_mid_part, grad_gain_mlp, grad_shift_mlp = ln2_back(grad_normed2)
    grad_middle = grad_out_rows + grad_mid_part
    grad_branch = grad_middle.astype(jnp.bfloat16)
    grad_outp_part = matmul_tn(mixed_low, grad_branch)
    grad_outb_attn = jnp.sum(grad_branch.astype(jnp.float32), axis=0)
    grad_mixed_low = matmul_nt(grad_branch, out_proj).astype(jnp.bfloat16)
    grad_mixed3 = grad_mixed_low.reshape(slots, clips, width)

    def query_side(number):
        offset = number * lane_width
        query_pair = head_pair(query3, offset, lane_width, DH)
        grad_pair = head_pair(grad_mixed3, offset, lane_width, DH)
        key_pair = head_pair(all_memory, offset, lane_width, DH)
        value_pair = head_pair(all_memory, width + offset, lane_width, DH)
        log_pair = lax.dynamic_slice_in_dim(log_rows, 2 * number, 2, 2)
        probability = pair_probs(query_pair, key_pair, log_pair, key_mask, scale)
        grad_probs = jnp.einsum(
            "qchd,kchd->chqk", grad_pair, value_pair, preferred_element_type=jnp.float32
        )
        delta = jnp.sum(probability * grad_probs, axis=-1, keepdims=True)
        grad_scores = (probability * (grad_probs - delta)).astype(jnp.bfloat16)
        grad_query = (
            jnp.einsum("chqk,kchd->qchd", grad_scores, key_pair, preferred_element_type=jnp.float32)
            * scale
        )
        return (
            offset,
            query_pair,
            grad_pair,
            probability,
            grad_scores,
            delta,
            grad_query.reshape(slots, clips, lane_width),
        )

    zero_query = jnp.zeros((slots, clips, width), jnp.float32)

    def backward_pair(number, state):
        grad_query_acc, grad_memory = state
        side = query_side(number)
        offset = side[0]
        grad_keys = (
            jnp.einsum("chqk,qchd->kchd", side[4], side[1], preferred_element_type=jnp.float32)
            * scale
        )
        grad_values = jnp.einsum(
            "chqk,qchd->kchd",
            side[3].astype(jnp.bfloat16),
            side[2],
            preferred_element_type=jnp.float32,
        )
        grad_memory = add_lanes(
            grad_memory, grad_keys.reshape(key_count, clips, lane_width), offset
        )
        grad_memory = add_lanes(
            grad_memory, grad_values.reshape(key_count, clips, lane_width), width + offset
        )
        return (add_lanes(grad_query_acc, side[6], offset), grad_memory)

    grad_query_full, grad_memory_all = lax.fori_loop(
        0,
        pair_count,
        backward_pair,
        (zero_query, jnp.zeros((key_count, clips, 2 * width), jnp.float32)),
    )
    grad_memory_own = lax.psum_scatter(
        grad_memory_all, ("freq", "tm"), scatter_dimension=0, tiled=True
    )
    grad_query_low = grad_query_full.reshape(row_count, width).astype(jnp.bfloat16)
    grad_memory_low = grad_memory_own.reshape(row_count, 2 * width).astype(jnp.bfloat16)
    grad_joint = jnp.concatenate([grad_query_low, grad_memory_low], axis=1)
    grad_joint_part = matmul_tn(normed1_low, grad_joint)
    grad_bias_cols = jnp.stack(
        [
            jnp.sum(grad_query_low.astype(jnp.float32), axis=0),
            jnp.sum(grad_memory_low[:, width:].astype(jnp.float32), axis=0),
        ],
        axis=1,
    )
    grad_normed1 = matmul_nt(grad_joint, joint_proj)
    grad_in_part, grad_gain_attn, grad_shift_attn = ln1_back(grad_normed1)
    grad_patches = (grad_middle + grad_in_part).astype(jnp.bfloat16).reshape(slots, clips, width)
    shares = (
        lax.psum_scatter(
            grad_joint_part.astype(jnp.bfloat16), ("freq", "tm"), scatter_dimension=0, tiled=True
        ).astype(jnp.float32),
        lax.psum_scatter(
            grad_bias_cols.astype(jnp.bfloat16), ("freq", "tm"), scatter_dimension=0, tiled=True
        ).astype(jnp.float32),
        lax.psum_scatter(
            grad_outp_part.astype(jnp.bfloat16), ("freq", "tm"), scatter_dimension=0, tiled=True
        ).astype(jnp.float32),
        lax.psum_scatter(
            grad_outb_attn.astype(jnp.bfloat16), ("freq", "tm"), scatter_dimension=0, tiled=True
        ).astype(jnp.float32),
        lax.psum_scatter(
            grad_gain_attn.astype(jnp.bfloat16), ("freq", "tm"), scatter_dimension=0, tiled=True
        ).astype(jnp.float32),
        lax.psum_scatter(
            grad_shift_attn.astype(jnp.bfloat16), ("freq", "tm"), scatter_dimension=0, tiled=True
        ).astype(jnp.float32),
        lax.psum_scatter(
            grad_up_part.astype(jnp.bfloat16), ("freq", "tm"), scatter_dimension=0, tiled=True
        ).astype(jnp.float32),
        lax.psum_scatter(
            grad_upb_part.astype(jnp.bfloat16), ("freq", "tm"), scatter_dimension=0, tiled=True
        ).astype(jnp.float32),
        lax.psum_scatter(
            grad_down_part.astype(jnp.bfloat16), ("freq", "tm"), scatter_dimension=0, tiled=True
        ).astype(jnp.float32),
        lax.psum_scatter(
            grad_outb_mlp.astype(jnp.bfloat16), ("freq", "tm"), scatter_dimension=0, tiled=True
        ).astype(jnp.float32),
        lax.psum_scatter(
            grad_gain_mlp.astype(jnp.bfloat16), ("freq", "tm"), scatter_dimension=0, tiled=True
        ).astype(jnp.float32),
        lax.psum_scatter(
            grad_shift_mlp.astype(jnp.bfloat16), ("freq", "tm"), scatter_dimension=0, tiled=True
        ).astype(jnp.float32),
    )
    summed_all = (
        lax.psum(shares[0].astype(jnp.bfloat16), "dp").astype(jnp.float32),
        lax.psum(shares[1].astype(jnp.bfloat16), "dp").astype(jnp.float32),
        lax.psum(shares[2].astype(jnp.bfloat16), "dp").astype(jnp.float32),
        lax.psum(shares[3].astype(jnp.bfloat16), "dp").astype(jnp.float32),
        lax.psum(shares[4].astype(jnp.bfloat16), "dp").astype(jnp.float32),
        lax.psum(shares[5].astype(jnp.bfloat16), "dp").astype(jnp.float32),
        lax.psum(shares[6].astype(jnp.bfloat16), "dp").astype(jnp.float32),
        lax.psum(shares[7].astype(jnp.bfloat16), "dp").astype(jnp.float32),
        lax.psum(shares[8].astype(jnp.bfloat16), "dp").astype(jnp.float32),
        lax.psum(shares[9].astype(jnp.bfloat16), "dp").astype(jnp.float32),
        lax.psum(shares[10].astype(jnp.bfloat16), "dp").astype(jnp.float32),
        lax.psum(shares[11].astype(jnp.bfloat16), "dp").astype(jnp.float32),
    )
    attn_summed = summed_all[:6]
    mlp_summed = summed_all[6:]
    grad_norm_gain = jnp.stack([attn_summed[4], mlp_summed[4]])
    grad_norm_shift = jnp.stack([attn_summed[5], mlp_summed[5]])
    grad_out_bias = jnp.stack([attn_summed[3], mlp_summed[3]])
    grad_proj_bias = jnp.transpose(attn_summed[1])
    return (
        output,
        grad_patches,
        grad_norm_gain,
        grad_norm_shift,
        attn_summed[0],
        grad_proj_bias,
        attn_summed[2],
        mlp_summed[0],
        mlp_summed[1],
        mlp_summed[2],
        grad_out_bias,
    )


LOG2E = 1.4426950408889634
LANES = 128
F32 = jnp.float32
BF16 = jnp.bfloat16
VMEM_LIMIT = 62 << 20
SAFE_RANGE = 100.0
CHUNKS = 4
HALVES = 2
SPAN = 1024
BACK_SPAN = 512
COLLECT_FLOPS = 30 * 10**9


def normalize(values):
    centered = values - jnp.mean(values, axis=-1, keepdims=True)
    inverse = lax.rsqrt(jnp.mean(centered * centered, axis=-1, keepdims=True) + EPS)
    return centered * inverse, inverse


def norm_back(normed, inverse, incoming, gain):
    scaled = incoming * gain
    mean = jnp.mean(scaled, axis=-1, keepdims=True)
    slope = jnp.mean(scaled * normed, axis=-1, keepdims=True)
    return (scaled - mean - normed * slope) * inverse


def spans_of(tokens, size=SPAN):
    return [slice(at, min(at + size, 2 * tokens)) for at in range(0, 2 * tokens, size)]


def column_sum(values):
    return jnp.sum(values, axis=0, keepdims=True)


def project_kernel(x_ref, live_ref, w_ref, vec_ref, rows_ref, n_ref, q_ref, k_ref, v_ref, first_key, rows):
    blocks, slots, width = x_ref.shape
    padded = rows.shape[0] // blocks

    @pl.when(pl.program_id(0) == 0)
    def _():
        rows[...] = jnp.zeros_like(rows)

    for block in range(blocks):
        rows[block * padded : block * padded + slots] = x_ref[block].astype(F32)
    rows_ref[...] = rows[...].astype(BF16)
    normed, _ = normalize(rows[...])
    low = (normed * vec_ref[0:1, :] + vec_ref[1:2, :]).astype(BF16)
    n_ref[...] = low
    q_ref[...] = (matmul(low, w_ref[:, 0:width]) + vec_ref[2:3, :]).astype(BF16)
    keys = matmul(low, w_ref[:, width : 2 * width]).astype(BF16).astype(F32)

    @pl.when(pl.program_id(0) == 0)
    def _():
        first_key[...] = jnp.broadcast_to(keys[0:1, :], first_key.shape)

    k_ref[...] = jnp.where(live_ref[:, 0:1] > 0, keys, first_key[0:1, :]).astype(BF16)
    v_ref[...] = (matmul(low, w_ref[:, 2 * width : 3 * width]) + vec_ref[3:4, :]).astype(BF16)


def project(blocks, live_lanes, joint_proj, vectors, steps=4):
    members, slots, width = blocks.shape
    tokens = live_lanes.shape[0]
    rows = tokens // steps
    block = pl.BlockSpec((rows, width), lambda step: (step, 0))
    return pl.pallas_call(
        project_kernel,
        grid=(steps,),
        in_specs=[
            pl.BlockSpec((members // steps, slots, width), lambda step: (step, 0, 0)),
            pl.BlockSpec((rows, LANES), lambda step: (step, 0)),
            pl.BlockSpec((width, 3 * width), lambda step: (0, 0), pipeline_mode=pl.Buffered(1)),
            pl.BlockSpec((8, width), lambda step: (0, 0)),
        ],
        out_specs=[block] * 5,
        out_shape=[jax.ShapeDtypeStruct((tokens, width), BF16)] * 5,
        scratch_shapes=[pltpu.VMEM((8, width), F32), pltpu.VMEM((rows, width), F32)],
        compiler_params=pltpu.CompilerParams(vmem_limit_bytes=VMEM_LIMIT),
        cost_estimate=pl.CostEstimate(
            flops=6 * tokens * width * width, transcendentals=tokens, bytes_accessed=10 * tokens * width
        ),
    )(blocks, live_lanes, joint_proj, vectors)


def attention_forward_kernel(q_ref, k_ref, v_ref, live_ref, o_ref, rn_ref, p_ref, qs, vt, ot, sa, p_buf, p_sem):
    tokens = q_ref.shape[0]
    pair = pl.program_id(0)
    slot = lax.rem(pair, 2)
    spans = spans_of(tokens)

    def copy_of(pair, slot, index):
        span = spans[index]
        columns = pl.ds(span.start, span.stop - span.start)
        return pltpu.make_async_copy(
            p_buf.at[slot, :, columns], p_ref.at[pair, :, columns], p_sem.at[slot, index]
        )

    @pl.when(pair >= 2)
    def _():
        for index in range(len(spans)):
            copy_of(pair - 2, slot, index).wait()

    lane = lax.broadcasted_iota(jnp.int32, (tokens, LANES), 1)
    query = q_ref[...].astype(F32) * (1.0 / math.sqrt(DH))
    keys = k_ref[...].astype(F32)
    qs[0:tokens, :] = jnp.where(lane < DH, query, 0.0).astype(BF16)
    qs[tokens : 2 * tokens, :] = jnp.where(lane < DH, 0.0, query).astype(BF16)
    live = live_ref[0:1, :]
    vt[0:LANES, :] = (jnp.transpose(v_ref[...].astype(F32)) * live).astype(BF16)
    vt[LANES : LANES + 16, :] = jnp.broadcast_to(live, (16, tokens)).astype(BF16)

    def largest(values, head):
        squares = jnp.where((lane < DH) == (head == 0), values * values, 0.0)
        return jnp.max(jnp.sum(squares, axis=1, keepdims=True))

    limit = (SAFE_RANGE / LOG2E) ** 2
    bound = jnp.maximum(
        largest(query, 0) * largest(keys, 0), largest(query, 1) * largest(keys, 1)
    )
    bounded = bound <= limit

    def finish(span, weight):
        p_buf[slot, :, span] = weight
        ot[:, span] = matmul(vt[...], weight)

    @pl.when(bounded)
    def _():
        for index, span in enumerate(spans):
            finish(span, jnp.exp2(matmul_nt(k_ref[...], qs[span, :]) * LOG2E).astype(BF16))
            copy_of(pair, slot, index).start()

    @pl.when(jnp.logical_not(bounded))
    def _():
        def column(index, _):
            part = pl.ds(pl.multiple_of(index * LANES, LANES), LANES)
            sa[...] = matmul_nt(k_ref[...], qs[part, :])
            score = sa[...]
            highest = jnp.max(score, axis=0, keepdims=True)
            finish(part, jnp.exp2(score * LOG2E - highest * LOG2E).astype(BF16))
            return 0

        lax.fori_loop(0, 2 * tokens // LANES, column, 0)
        for index in range(len(spans)):
            copy_of(pair, slot, index).start()

    row = lax.broadcasted_iota(jnp.int32, (LANES, tokens), 0)
    inverse = jnp.where(
        row < DH,
        jnp.broadcast_to(1.0 / ot[LANES : LANES + 1, 0:tokens], (LANES, tokens)),
        jnp.broadcast_to(1.0 / ot[LANES : LANES + 1, tokens : 2 * tokens], (LANES, tokens)),
    )
    mixed = jnp.where(row < DH, ot[0:LANES, 0:tokens], ot[0:LANES, tokens : 2 * tokens]) * inverse
    o_ref[...] = jnp.transpose(mixed).astype(BF16)
    rn_ref[...] = jnp.transpose(inverse)

    @pl.when(pair == pl.num_programs(0) - 1)
    def _():
        for index in range(len(spans)):
            copy_of(pair - 1, 1 - slot, index).wait()
        for index in range(len(spans)):
            copy_of(pair, slot, index).wait()


def attention_forward(query, keys, memory, live_row):
    tokens, width = query.shape
    pairs = width // LANES
    block = pl.BlockSpec((tokens, LANES), lambda pair: (0, pair))
    return pl.pallas_call(
        attention_forward_kernel,
        grid=(pairs,),
        in_specs=[block, block, block, pl.BlockSpec((8, tokens), lambda pair: (0, 0))],
        out_specs=[block, block, pl.BlockSpec(memory_space=pl.ANY)],
        out_shape=[
            jax.ShapeDtypeStruct((tokens, width), BF16),
            jax.ShapeDtypeStruct((tokens, width), F32),
            jax.ShapeDtypeStruct((pairs, tokens, 2 * tokens), BF16),
        ],
        scratch_shapes=[
            pltpu.VMEM((2 * tokens, LANES), BF16),
            pltpu.VMEM((LANES + 16, tokens), BF16),
            pltpu.VMEM((LANES + 16, 2 * tokens), F32),
            pltpu.VMEM((tokens, LANES), F32),
            pltpu.VMEM((2, tokens, 2 * tokens), BF16),
            pltpu.SemaphoreType.DMA((2, len(spans_of(tokens)))),
        ],
        compiler_params=pltpu.CompilerParams(vmem_limit_bytes=VMEM_LIMIT),
        cost_estimate=pl.CostEstimate(
            flops=8 * pairs * tokens * tokens * LANES,
            transcendentals=2 * pairs * tokens * tokens,
            bytes_accessed=4 * pairs * tokens * tokens,
        ),
    )(query, keys, memory, live_row)


def attention_backward_kernel(
    q_ref, k_ref, v_ref, o_ref, do_ref, rn_ref, live_ref, keep_ref, p_ref, n_ref, w_ref,
    x_ref, res_ref, vec_ref, sums_ref, half_ref, out_ref,
    kept_ref, sent_ref, rows_ref, qs, gs, kt, dqt, delta, dj, vecs, n_buf, w_buf, x_buf, res_buf, dx_buf, sem, dx_sem,
):
    tokens = q_ref.shape[0]
    pair = pl.program_id(0)

    late = [
        pltpu.make_async_copy(source, target, sem.at[index])
        for index, (source, target) in enumerate(
            ((n_ref, n_buf), (w_ref, w_buf), (x_ref, x_buf), (res_ref, res_buf))
        )
    ]

    @pl.when(pair == 0)
    def _():
        for copy in late:
            copy.start()

    scale = 1.0 / math.sqrt(DH)
    lane = lax.broadcasted_iota(jnp.int32, (tokens, LANES), 1)
    query = q_ref[...].astype(F32) * scale
    qs[0:tokens, :] = jnp.where(lane < DH, query, 0.0).astype(BF16)
    qs[tokens : 2 * tokens, :] = jnp.where(lane < DH, 0.0, query).astype(BF16)
    grad = do_ref[...].astype(F32) * rn_ref[...]
    gs[0:tokens, :] = jnp.where(lane < DH, grad, 0.0).astype(BF16)
    gs[tokens : 2 * tokens, :] = jnp.where(lane < DH, 0.0, grad).astype(BF16)
    kt[...] = (jnp.transpose(k_ref[...].astype(F32)) * (live_ref[0:1, :] * scale)).astype(BF16)
    product = jnp.transpose(grad * o_ref[...].astype(F32))
    for head in range(2):
        total = column_sum(product[head * DH : (head + 1) * DH])
        delta[:, head * tokens : (head + 1) * tokens] = jnp.broadcast_to(total, (8, tokens))
    grad_keys = grad_values = None
    for span in spans_of(tokens, BACK_SPAN):
        weight = p_ref[0, :, span]
        grad_weight = matmul_nt(v_ref[...], gs[span, :])
        grad_score = (weight.astype(F32) * (grad_weight - delta[0:1, span])).astype(BF16)
        dqt[:, span] = matmul(kt[...], grad_score)
        part_values = matmul(weight, gs[span, :])
        part_keys = matmul(grad_score, qs[span, :])
        grad_values = part_values if grad_values is None else grad_values + part_values
        grad_keys = part_keys if grad_keys is None else grad_keys + part_keys
    row = lax.broadcasted_iota(jnp.int32, (LANES, tokens), 0)
    grad_query = jnp.transpose(jnp.where(row < DH, dqt[:, 0:tokens], dqt[:, tokens : 2 * tokens]))
    keep = keep_ref[...] > 0
    width = x_buf.shape[1]
    parts = (
        grad_query.astype(BF16),
        jnp.where(keep, grad_keys, 0.0).astype(BF16),
        jnp.where(keep, grad_values, 0.0).astype(BF16),
    )
    for part, value in enumerate(parts):
        columns = pl.ds(pl.multiple_of(part * width + pl.program_id(0) * LANES, LANES), LANES)
        dj[:, columns] = value
        if part != 1:
            columns = pl.ds(pl.multiple_of(pl.program_id(0) * LANES, LANES), LANES)
            vecs[2 + part // 2 : 3 + part // 2, columns] = column_sum(value.astype(F32))

    @pl.when(pl.program_id(0) == pl.num_programs(0) - 1)
    def _():
        for copy in late:
            copy.wait()
        first = half_ref[0] == 0
        half = width // 2
        for part in range(3):
            span = slice(part * width, (part + 1) * width)
            grad_weights = matmul_tn(n_buf[...], dj[:, span]).astype(BF16)
            kept_ref[:, span] = jnp.where(first, grad_weights[:half], grad_weights[half:])
            sent_ref[:, span] = jnp.where(first, grad_weights[half:], grad_weights[:half])
        vecs[4:8, :] = sums_ref[0:4, :]
        rows = tokens // CHUNKS
        block = tokens // rows_ref.shape[0]
        stores = []
        gain_sum = shift_sum = 0.0
        for start in range(0, tokens, rows):
            span = slice(start, start + rows)
            incoming = matmul_nt(dj[span, :], w_buf[...])
            normed, inverse = normalize(x_buf[span, :].astype(F32))
            gain_sum += column_sum(incoming * normed)
            shift_sum += column_sum(incoming)
            back = norm_back(normed, inverse, incoming, vec_ref[0:1, :])
            grad_rows = (res_buf[span, :].astype(F32) + back).astype(BF16)
            for part in range(rows // block):
                dx_buf[start // block + part] = grad_rows[part * block : part * block + dx_buf.shape[1]]
            stores.append(
                pltpu.make_async_copy(
                    dx_buf.at[pl.ds(start // block, rows // block)],
                    rows_ref.at[pl.ds(start // block, rows // block), 0],
                    dx_sem.at[start // rows],
                )
            )
            stores[-1].start()
        vecs[0:1, :] = gain_sum
        vecs[1:2, :] = shift_sum
        turned = jnp.transpose(jnp.concatenate([vecs[...]] * (LANES // 8), axis=0)).astype(BF16)
        tail = kept_ref.shape[1] - LANES
        kept_ref[:, tail:] = jnp.where(first, turned[:half], turned[half:])
        sent_ref[:, tail:] = jnp.where(first, turned[half:], turned[:half])
        for copy in stores:
            copy.wait()


def attention_backward(
    query, keys, memory, mixed, grad_mixed, inverse, live_row, live_lanes, weights, normed, joint_proj,
    inputs, residual, vectors, vector_grads, own_half, output,
):
    tokens, width = query.shape
    pairs = width // LANES
    block = pl.BlockSpec((tokens, LANES), lambda pair: (0, pair))
    once = pl.Buffered(1)
    anywhere = pl.BlockSpec(memory_space=pl.ANY)

    def fixed(rows, columns):
        return pl.BlockSpec((rows, columns), lambda pair: (0, 0), pipeline_mode=once)

    return pl.pallas_call(
        attention_backward_kernel,
        grid=(pairs,),
        in_specs=[block] * 6
        + [
            fixed(8, tokens),
            fixed(tokens, LANES),
            pl.BlockSpec((1, tokens, 2 * tokens), lambda pair: (pair, 0, 0)),
            anywhere,
            anywhere,
            anywhere,
            anywhere,
            fixed(8, width),
            fixed(8, width),
            pl.BlockSpec(memory_space=pltpu.SMEM),
            anywhere,
        ],
        out_specs=[fixed(width // 2, 3 * width + LANES), fixed(width // 2, 3 * width + LANES), anywhere],
        out_shape=[
            jax.ShapeDtypeStruct((width // 2, 3 * width + LANES), BF16),
            jax.ShapeDtypeStruct((width // 2, 3 * width + LANES), BF16),
            jax.ShapeDtypeStruct(output.shape, BF16),
        ],
        scratch_shapes=[
            pltpu.VMEM((2 * tokens, LANES), BF16),
            pltpu.VMEM((2 * tokens, LANES), BF16),
            pltpu.VMEM((LANES, tokens), BF16),
            pltpu.VMEM((LANES, 2 * tokens), F32),
            pltpu.VMEM((8, 2 * tokens), F32),
            pltpu.VMEM((tokens, 3 * width), BF16),
            pltpu.VMEM((8, width), F32),
            pltpu.VMEM((tokens, width), BF16),
            pltpu.VMEM((width, 3 * width), BF16),
            pltpu.VMEM((tokens, width), BF16),
            pltpu.VMEM((tokens, width), BF16),
            pltpu.VMEM((output.shape[0],) + output.shape[2:], BF16),
            pltpu.SemaphoreType.DMA((4,)),
            pltpu.SemaphoreType.DMA((CHUNKS,)),
        ],
        input_output_aliases={16: 2},
        compiler_params=pltpu.CompilerParams(vmem_limit_bytes=VMEM_LIMIT),
        cost_estimate=pl.CostEstimate(
            flops=16 * pairs * tokens * tokens * LANES,
            transcendentals=0,
            bytes_accessed=4 * pairs * tokens * tokens,
        ),
    )(
        query, keys, memory, mixed, grad_mixed, inverse, live_row, live_lanes, weights, normed,
        joint_proj, inputs, residual, vectors, vector_grads,
        own_half, output,
    )


def feed_forward_kernel(
    x_hbm, mixed_hbm, cot_hbm, live_ref, wo_ref, vec_ref, up_ref, down_ref, bias_ref,
    out_hbm, share_ref, branch_hbm, gm_hbm, packed_ref, ds_ref,
    x_ref, mixed_ref, cot_ref, out_ref, branch_ref, gm_ref,
    normed, grad_out, middle, acc, acc_grad, hidden, grad_pre, down_buf, up_buf, down_sem, up_sem, in_sem, out_sem,
):
    step = pl.program_id(0)
    last = pl.num_programs(0) - 1
    tokens, width = x_ref.shape
    units = up_ref.shape[1]
    rows = tokens // CHUNKS

    block = tokens // out_ref.shape[0]
    slots = out_ref.shape[1]
    parts = rows // block

    def rows_of_chunk(chunk):
        return pl.ds(pl.multiple_of(chunk * rows, 32), rows)

    def fetches(chunk):
        span = rows_of_chunk(chunk)
        pairs = ((x_hbm, x_ref), (mixed_hbm, mixed_ref), (cot_hbm, cot_ref))
        return [
            pltpu.make_async_copy(source.at[span], target.at[span], in_sem.at[chunk, index])
            for index, (source, target) in enumerate(pairs)
        ]

    def stores(chunk):
        span = rows_of_chunk(chunk)
        return [
            pltpu.make_async_copy(source.at[span], target.at[span], out_sem.at[chunk, index])
            for index, (source, target) in enumerate(((branch_ref, branch_hbm), (gm_ref, gm_hbm)))
        ] + [
            pltpu.make_async_copy(
                out_ref.at[pl.ds(chunk * parts, parts)],
                out_hbm.at[pl.ds(chunk * parts, parts), 1],
                out_sem.at[chunk, 2],
            )
        ]

    @pl.when(step == 0)
    def _():
        for chunk in range(CHUNKS):
            for copy in fetches(chunk):
                copy.start()

        def chunk_step(chunk, _):
            span = rows_of_chunk(chunk)
            for copy in fetches(chunk):
                copy.wait()
            values = x_ref[span, :].astype(F32) + matmul(mixed_ref[span, :], wo_ref[...]) + vec_ref[2:3, :]
            middle[span, :] = values
            acc[span, :] = values + vec_ref[3:4, :]
            unit, _ = normalize(values)
            normed[span, :] = (unit * vec_ref[0:1, :] + vec_ref[1:2, :]).astype(BF16)
            grad_out[span, :] = (cot_ref[span, :].astype(F32) * live_ref[span, 0:1]).astype(BF16)
            acc_grad[span, :] = jnp.zeros((rows, width), F32)
            return 0

        lax.fori_loop(0, CHUNKS, chunk_step, 0)

    up = up_ref[...]
    down = down_ref[...]
    half = tokens // HALVES

    def feed(index, grad_bias):
        span = pl.ds(pl.multiple_of(index * half, 32), half)
        pre_act = matmul(normed[span, :], up) + bias_ref[0:1, :]
        grad_hidden = matmul_nt(grad_out[span, :], down)
        cumulative = 0.5 + 0.5 * lax.erf(pre_act * math.sqrt(0.5))
        density = jnp.exp2(pre_act * pre_act * (-0.5 * LOG2E)) * (1.0 / math.sqrt(2.0 * math.pi))
        low = (pre_act * cumulative).astype(BF16)
        grad_low = (grad_hidden * (cumulative + pre_act * density)).astype(BF16)
        hidden[span, :] = low
        grad_pre[span, :] = grad_low
        acc[span, :] += matmul(low, down)
        acc_grad[span, :] += matmul_nt(grad_low, up)
        return grad_bias + column_sum(grad_low.astype(F32))

    grad_bias = lax.fori_loop(0, HALVES, feed, jnp.zeros((1, units), F32))
    slot = lax.rem(step, 2)
    _, cuts, quarters, share, _ = down_buf.shape
    own = units // cuts
    for cut in range(cuts):
        sums = jnp.broadcast_to(grad_bias[:, cut * own : (cut + 1) * own], (16, own)).astype(BF16)
        share_ref[step * cuts + cut, share : share + 16, 0:own] = sums
        share_ref[step * cuts + cut, share : share + 16, own:width] = jnp.zeros((16, width - own), BF16)

    def copies(at, slot):
        return (
            pltpu.make_async_copy(
                down_buf.at[slot], packed_ref.at[pl.ds(at * cuts, cuts), pl.ds(0, quarters)], down_sem.at[slot]
            ),
            pltpu.make_async_copy(up_buf.at[slot], packed_ref.at[:, quarters + at], up_sem.at[slot]),
        )

    @pl.when(step >= 2)
    def _():
        for copy in copies(step - 2, slot):
            copy.wait()

    grad_down = matmul_tn(hidden[...], grad_out[...]).astype(BF16)
    for cut in range(cuts):
        for quarter in range(quarters):
            base = (cut * quarters + quarter) * share
            down_buf[slot, cut, quarter] = grad_down[base : base + share]
    grad_up = matmul_tn(normed[...], grad_pre[...]).astype(BF16)
    for member in range(width // share):
        up_buf[slot, member] = grad_up[member * share : (member + 1) * share]
    for copy in copies(step, slot):
        copy.start()

    @pl.when(step == last)
    def _():
        ds_ref[...] = jnp.zeros_like(ds_ref)

        def chunk_step(chunk, _):
            span = rows_of_chunk(chunk)
            final = (acc[span, :] * live_ref[span, 0:1]).astype(BF16)
            for part in range(parts):
                out_ref[chunk * parts + part] = final[part * block : part * block + slots]
            unit, inverse = normalize(middle[span, :])
            incoming = acc_grad[span, :]
            start = grad_out[span, :].astype(F32)
            branch = (start + norm_back(unit, inverse, incoming, vec_ref[0:1, :])).astype(BF16)
            branch_ref[span, :] = branch
            gm_ref[span, :] = matmul_nt(branch, wo_ref[...]).astype(BF16)
            for copy in stores(chunk):
                copy.start()
            for place, term in enumerate((incoming * unit, incoming, branch.astype(F32), start)):
                ds_ref[place : place + 1, :] += column_sum(term)
            return 0

        lax.fori_loop(0, CHUNKS, chunk_step, 0)
        grad_outp = matmul_tn(mixed_ref[...], branch_ref[...]).astype(BF16)
        for member in range(width // share):
            share_ref[member, 0:share, :] = grad_outp[member * share : (member + 1) * share]
        for chunk in range(CHUNKS):
            for copy in stores(chunk):
                copy.wait()
        for copy in copies(step - 1, 1 - slot):
            copy.wait()
        for copy in copies(step, slot):
            copy.wait()


def feed_forward(
    inputs, mixed, cotangent, live_lanes, out_proj, vectors, up_proj, up_bias, down_proj, members, slots
):
    tokens, width = inputs.shape
    hidden_units = up_proj.shape[1]
    steps = hidden_units // width
    share = width // members
    cuts = members // steps
    quarters = hidden_units // members // share
    once = pl.Buffered(1)
    anywhere = pl.BlockSpec(memory_space=pl.ANY)

    def fixed(rows, columns):
        return pl.BlockSpec((rows, columns), lambda step: (0, 0), pipeline_mode=once)

    return pl.pallas_call(
        feed_forward_kernel,
        grid=(steps,),
        in_specs=[
            anywhere,
            anywhere,
            anywhere,
            fixed(tokens, LANES),
            fixed(width, width),
            fixed(8, width),
            pl.BlockSpec((width, width), lambda step: (0, step)),
            pl.BlockSpec((width, width), lambda step: (step, 0)),
            pl.BlockSpec((8, width), lambda step: (0, step)),
        ],
        out_specs=[
            anywhere,
            pl.BlockSpec((members, share + 16, width), lambda step: (0, 0, 0), pipeline_mode=once),
            anywhere,
            anywhere,
            anywhere,
            fixed(8, width),
        ],
        out_shape=[
            jax.ShapeDtypeStruct((members, 2, slots, width), BF16),
            jax.ShapeDtypeStruct((members, share + 16, width), BF16),
            jax.ShapeDtypeStruct((tokens, width), BF16),
            jax.ShapeDtypeStruct((tokens, width), BF16),
            jax.ShapeDtypeStruct((members, quarters + steps, share, width), BF16),
            jax.ShapeDtypeStruct((8, width), F32),
        ],
        scratch_shapes=[pltpu.VMEM((tokens, width), BF16)] * 3
        + [
            pltpu.VMEM((members, slots, width), BF16),
            pltpu.VMEM((tokens, width), BF16),
            pltpu.VMEM((tokens, width), BF16),
            pltpu.VMEM((tokens, width), BF16),
            pltpu.VMEM((tokens, width), BF16),
            pltpu.VMEM((tokens, width), F32),
            pltpu.VMEM((tokens, width), F32),
            pltpu.VMEM((tokens, width), F32),
            pltpu.VMEM((tokens, width), BF16),
            pltpu.VMEM((tokens, width), BF16),
            pltpu.VMEM((2, cuts, quarters, share, width), BF16),
            pltpu.VMEM((2, members, share, width), BF16),
            pltpu.SemaphoreType.DMA((2,)),
            pltpu.SemaphoreType.DMA((2,)),
            pltpu.SemaphoreType.DMA((CHUNKS, 3)),
            pltpu.SemaphoreType.DMA((CHUNKS, 3)),
        ],
        compiler_params=pltpu.CompilerParams(vmem_limit_bytes=VMEM_LIMIT),
        cost_estimate=pl.CostEstimate(
            flops=12 * tokens * width * hidden_units + 6 * tokens * width * width,
            transcendentals=2 * tokens * hidden_units,
            bytes_accessed=12 * tokens * width + 8 * width * hidden_units,
        ),
    )(inputs, mixed, cotangent, live_lanes, out_proj, vectors, up_proj, down_proj, up_bias)


def collect_joint_kernel(own_ref, *refs):
    pieces, (joint_ref, gain_ref, shift_ref, bias_ref, branch_ref, columns) = refs[:-6], refs[-6:]
    rows = pieces[0].shape[0]
    width = joint_ref.shape[1] // 3
    own = own_ref[0]
    columns[...] = jnp.zeros_like(columns)
    for place in range(len(pieces)):
        piece = pieces[place][...]
        for other in range(1, len(pieces)):
            piece = jnp.where(own == other, pieces[place ^ other][...], piece)
        piece = piece.astype(F32)
        span = slice(place * rows, (place + 1) * rows)
        joint_ref[span, :] = piece[:, : 3 * width]
        columns[span, :] = piece[:, 3 * width :]
    turned = jnp.transpose(columns[...])
    share = gain_ref.shape[1]
    gain_ref[0:1, :] = turned[0:1, 0:share]
    gain_ref[1:2, :] = turned[4:5, 0:share]
    shift_ref[0:1, :] = turned[1:2, 0:share]
    shift_ref[1:2, :] = turned[5:6, 0:share]
    bias_ref[...] = turned[2:4, 0:share]
    branch_ref[...] = turned[6:8, 0:share]


def collect_joint(own, pieces, share):
    width = (pieces[0].shape[1] - LANES) // 3
    vmem = pl.BlockSpec(memory_space=pltpu.VMEM)
    return pl.pallas_call(
        collect_joint_kernel,
        in_specs=[pl.BlockSpec(memory_space=pltpu.SMEM)] + [vmem] * len(pieces),
        out_specs=[vmem] * 5,
        out_shape=[jax.ShapeDtypeStruct((share, 3 * width), F32)] + [jax.ShapeDtypeStruct((2, share), F32)] * 4,
        scratch_shapes=[pltpu.VMEM((LANES, LANES), F32)],
        cost_estimate=pl.CostEstimate(flops=0, transcendentals=0, bytes_accessed=0),
    )(own, *pieces)


def collect_mlp_kernel(rows_ref, sums_ref, down_ref, up_ref, outp_ref, bias_ref):
    own, width = down_ref.shape
    share = outp_ref.shape[0]
    down_ref[...] = rows_ref[0:own, :].astype(F32)
    for part in range(own // share):
        rows = slice(own + part * share, own + (part + 1) * share)
        up_ref[:, part * width : (part + 1) * width] = rows_ref[rows, :].astype(F32)
    outp_ref[...] = sums_ref[0:share, :].astype(F32)
    bias_ref[...] = sums_ref[share : share + 16, 0:own].astype(F32)[0]


def collect_mlp(rows, sums, share):
    own, width = rows.shape[0] // 2, rows.shape[1]
    vmem = pl.BlockSpec(memory_space=pltpu.VMEM)
    return pl.pallas_call(
        collect_mlp_kernel,
        in_specs=[vmem] * 2,
        out_specs=[vmem] * 4,
        out_shape=[
            jax.ShapeDtypeStruct((own, width), F32),
            jax.ShapeDtypeStruct((share, own // share * width), F32),
            jax.ShapeDtypeStruct((share, width), F32),
            jax.ShapeDtypeStruct((own,), F32),
        ],
        cost_estimate=pl.CostEstimate(flops=COLLECT_FLOPS, transcendentals=0, bytes_accessed=4 * rows.size),
    )(rows, sums)


def per_device(
    patches,
    col_counts,
    norm_gain,
    norm_shift,
    joint_proj,
    proj_bias,
    out_proj,
    up_proj,
    up_bias,
    down_proj,
    out_bias,
    cotangent,
):
    slots, clips, width = patches.shape
    group = ("freq", "tm")
    freq_size = lax.axis_size("freq")
    time_size = lax.axis_size("tm")
    groups = lax.axis_size("dp")
    members = freq_size * time_size
    freq_rows = FREQ_ROWS // freq_size
    cap_cols = (slots - 2) // freq_rows
    padded = -(-slots // 16) * 16
    tokens = members * padded
    pairs = width // LANES
    share = width // members
    hidden_units = up_proj.shape[1]

    def to_clip(array):
        return lax.all_to_all(array, group, 0, 0, tiled=True)

    token_ids = jnp.arange(tokens, dtype=jnp.int32)
    block_ids = token_ids // padded
    live = live_slots(
        col_counts,
        token_ids % padded,
        block_ids // time_size,
        block_ids % time_size,
        freq_rows,
        cap_cols,
    ) & (token_ids % padded < slots)
    live_full = live.astype(F32)
    live_row = jnp.broadcast_to(live_full[None, :], (8, tokens))
    live_lanes = jnp.broadcast_to(live_full[:, None], (tokens, LANES))

    def rows_of(*vectors):
        stacked = jnp.stack(vectors).astype(F32)
        return jnp.pad(stacked, ((0, 8 - len(vectors)), (0, 0)))

    vectors1 = rows_of(norm_gain[0], norm_shift[0], proj_bias[0], proj_bias[1])
    vectors2 = rows_of(norm_gain[1], norm_shift[1], out_bias[0], out_bias[1])
    bias_rows = jnp.broadcast_to(up_bias.astype(F32)[None, :], (8, hidden_units))

    arrived = to_clip(jnp.transpose(patches, (1, 0, 2)))
    turned = jnp.pad(jnp.transpose(cotangent, (1, 0, 2)), ((0, 0), (0, padded - slots), (0, 0)))
    turned, live_lanes, live_row, vectors1, vectors2, bias_rows = lax.optimization_barrier(
        (turned, live_lanes, live_row, vectors1, vectors2, bias_rows)
    )
    cot = to_clip(turned).reshape(tokens, width)
    inputs, normed1, query, keys, memory = project(arrived, live_lanes, joint_proj, vectors1)
    mixed, inverse, weights = attention_forward(query, keys, memory, live_row)
    output, blocks, branch, grad_mixed, packed, vector_grads = feed_forward(
        inputs, mixed, cot, live_lanes, out_proj, vectors2, up_proj, bias_rows, down_proj, members, padded
    )
    own = hidden_units // members
    mlp_rows = lax.psum_scatter(packed.reshape(members, 2 * own, width), group, scatter_dimension=0, tiled=True)[0]
    moved = lax.all_to_all(blocks, group, 0, 0, tiled=True)

    own_half = lax.axis_index("freq")
    own_group = lax.axis_index("dp")
    kept, sent, token_rows = attention_backward(
        query, keys, memory, mixed, grad_mixed, inverse, live_row, live_lanes, weights, normed1, joint_proj,
        inputs, branch, vectors1, vector_grads, own_half.reshape(1),
        output,
    )
    kept, sent, moved = lax.optimization_barrier((kept, sent, moved))
    got = lax.ppermute(sent, "freq", [(0, 1), (1, 0)])
    outp_rows = jnp.sum(moved.astype(F32), axis=0).astype(BF16)
    joint_half = (kept.astype(F32) + got.astype(F32)).astype(BF16).reshape(time_size, share, kept.shape[1])
    joint_half, mlp_rows, outp_rows = lax.optimization_barrier((joint_half, mlp_rows, outp_rows))
    mlp_sum, outp_sum = lax.psum((mlp_rows, outp_rows), "dp")
    arrived = lax.all_to_all(joint_half, "tm", 0, 0, tiled=True)
    joint_rows = jnp.sum(arrived.astype(F32), axis=0).astype(BF16)
    joint_rows, token_rows = lax.optimization_barrier((joint_rows, token_rows))

    def to_group(array, distance):
        return lax.ppermute(array, "dp", [(i, i ^ distance) for i in range(groups)])

    cut = joint_rows.reshape(groups, share // groups, kept.shape[1])
    piece = lax.dynamic_index_in_dim(cut, own_group, 0, False).astype(F32)
    for distance in range(1, groups):
        piece += to_group(lax.dynamic_index_in_dim(cut, own_group ^ distance, 0, False), distance).astype(F32)
    piece = piece.astype(BF16)
    pieces = [piece] + [to_group(piece, distance) for distance in range(1, groups)]
    token_rows = lax.all_to_all(token_rows, group, 0, 0, tiled=True)
    grad_patches, output = (jnp.transpose(token_rows[:, kind, :slots], (1, 0, 2)) for kind in range(2))

    joint_sum, gain_sum, shift_sum, bias_sum, branch_sum = collect_joint(own_group.reshape(1), pieces, share)
    joint_sum, mlp_sum, outp_sum = lax.optimization_barrier((joint_sum, mlp_sum, outp_sum))
    down_sum, up_sum, outp_sum, up_bias_sum = collect_mlp(mlp_sum, outp_sum, share)
    return (
        output,
        grad_patches,
        gain_sum,
        shift_sum,
        joint_sum,
        bias_sum,
        outp_sum,
        up_sum,
        up_bias_sum,
        down_sum,
        branch_sum,
    )


def plan(patches, *others):
    members = lax.axis_size("freq") * lax.axis_size("tm")
    if patches.shape[1] == members:
        return per_device(patches, *others)
    return per_device_gathered(patches, *others)


def solution(mesh):
    return jax.shard_map(
        plan,
        mesh=mesh,
        in_specs=(
            P(("freq", "tm"), "dp", None),
            P(),
            P(),
            P(),
            P(),
            P(),
            P(),
            P(),
            P(),
            P(),
            P(),
            P(("freq", "tm"), "dp", None),
        ),
        out_specs=(
            P(("freq", "tm"), "dp", None),
            P(("freq", "tm"), "dp", None),
            P(None, ("freq", "tm")),
            P(None, ("freq", "tm")),
            P(("freq", "tm"), None),
            P(None, ("freq", "tm")),
            P(("freq", "tm"), None),
            P(("freq", "tm"), None),
            P(("freq", "tm")),
            P(("freq", "tm"), None),
            P(None, ("freq", "tm")),
        ),
        check_vma=False,
    )
```

```python
import functools
import math

import jax
import jax.numpy as jnp
from jax import lax
from jax.experimental import pallas as pl
from jax.experimental.pallas import tpu as pltpu
from jax.sharding import PartitionSpec as P

HEADS = 12
DH = 64
FREQ_ROWS = 12


EPS = 1e-06
NEG = -1000000000.0


def live_slots(col_counts, slot_ids, freq_ids, time_ids, freq_rows, cap_cols):
    table = jnp.arange(col_counts.shape[0], dtype=jnp.int32)
    live_cols = jnp.sum(
        jnp.where(time_ids[:, None] == table[None, :], col_counts[None, :], 0), axis=1
    )
    in_grid = slot_ids < freq_rows * cap_cols
    column_live = slot_ids // freq_rows < live_cols
    extra_live = (time_ids == 0) & (freq_ids == 0)
    return jnp.where(in_grid, column_live, extra_live)


def norm_rows(values, gain, shift):
    centered = values - jnp.mean(values, axis=-1, keepdims=True)
    inverse = lax.rsqrt(jnp.mean(centered * centered, axis=-1, keepdims=True) + EPS)
    return centered * inverse * gain + shift


def gelu_exact(values):
    return jax.nn.gelu(values, approximate=False)


def matmul(left, right):
    return jnp.dot(left, right, preferred_element_type=jnp.float32)


def matmul_tn(left, right):
    return lax.dot_general(
        left, right, (((0,), (0,)), ((), ())), preferred_element_type=jnp.float32
    )


def matmul_nt(left, right):
    return lax.dot_general(
        left, right, (((1,), (1,)), ((), ())), preferred_element_type=jnp.float32
    )


def head_pair(array, offset, lane_width, head_size):
    section = lax.dynamic_slice_in_dim(array, offset, lane_width, 2)
    return section.reshape(section.shape[0], section.shape[1], 2, head_size)


def add_lanes(target, addend, offset):
    current = lax.dynamic_slice_in_dim(target, offset, addend.shape[2], 2)
    return lax.dynamic_update_slice_in_dim(target, current + addend, offset, 2)


def pair_probs(query_pair, key_pair, log_pair, mask, scale):
    scores = (
        jnp.einsum("qchd,kchd->chqk", query_pair, key_pair, preferred_element_type=jnp.float32)
        * scale
        + mask
    )
    return jnp.exp(scores - jnp.transpose(log_pair, (1, 2, 0))[..., None])


def per_device_gathered(
    patches,
    col_counts,
    norm_gain,
    norm_shift,
    joint_proj,
    proj_bias,
    out_proj,
    up_proj,
    up_bias,
    down_proj,
    out_bias,
    cotangent,
):
    slots, clips, width = patches.shape
    row_count = slots * clips
    lane_width = 2 * DH
    pair_count = HEADS // 2
    scale = 1.0 / math.sqrt(DH)
    freq_size = lax.axis_size("freq")
    time_size = lax.axis_size("tm")
    freq_rows = FREQ_ROWS // freq_size
    cap_cols = (slots - 2) // freq_rows
    key_count = slots * freq_size * time_size
    slot_ids = jnp.arange(slots, dtype=jnp.int32)
    own_live = live_slots(
        col_counts,
        slot_ids,
        jnp.full((slots,), lax.axis_index("freq"), jnp.int32),
        jnp.full((slots,), lax.axis_index("tm"), jnp.int32),
        freq_rows,
        cap_cols,
    )
    key_ids = jnp.arange(key_count, dtype=jnp.int32)
    key_group = key_ids // slots
    key_live = live_slots(
        col_counts,
        key_ids % slots,
        key_group // time_size,
        key_group % time_size,
        freq_rows,
        cap_cols,
    )
    key_mask = jnp.where(key_live, 0.0, NEG).astype(jnp.float32)
    row_live = (
        jnp.broadcast_to(own_live[:, None], (slots, clips))
        .reshape(row_count, 1)
        .astype(jnp.float32)
    )
    gain_full = norm_gain.astype(jnp.float32)
    shift_full = norm_shift.astype(jnp.float32)
    bias_full = proj_bias.astype(jnp.float32)
    outb_full = out_bias.astype(jnp.float32)
    upb_full = up_bias.astype(jnp.float32)
    inputs = patches.reshape(row_count, width).astype(jnp.float32)
    normed1, ln1_back = jax.vjp(norm_rows, inputs, gain_full[0], shift_full[0])
    normed1_low = normed1.astype(jnp.bfloat16)
    joint = matmul(normed1_low, joint_proj)
    query_low = (joint[:, :width] + bias_full[0]).astype(jnp.bfloat16)
    keys_low = joint[:, width : 2 * width].astype(jnp.bfloat16)
    memory_low = (joint[:, 2 * width :] + bias_full[1]).astype(jnp.bfloat16)
    query3 = query_low.reshape(slots, clips, width)
    key_value = jnp.concatenate([keys_low, memory_low], axis=1).reshape(slots, clips, 2 * width)
    all_memory = lax.all_gather(key_value, ("freq", "tm"), axis=0, tiled=True)

    def forward_pair(number, state):
        mixed_acc, log_acc = state
        offset = number * lane_width
        query_pair = head_pair(query3, offset, lane_width, DH)
        key_pair = head_pair(all_memory, offset, lane_width, DH)
        value_pair = head_pair(all_memory, width + offset, lane_width, DH)
        scores = (
            jnp.einsum("qchd,kchd->chqk", query_pair, key_pair, preferred_element_type=jnp.float32)
            * scale
            + key_mask
        )
        highest = jnp.max(scores, axis=-1, keepdims=True)
        exponent = jnp.exp(scores - highest)
        summed = jnp.sum(exponent, axis=-1, keepdims=True)
        attention = (exponent / summed).astype(jnp.bfloat16)
        mixed = jnp.einsum(
            "chqk,kchd->qchd", attention, value_pair, preferred_element_type=jnp.float32
        )
        log_pair = jnp.transpose((highest + jnp.log(summed))[..., 0], (2, 0, 1))
        mixed_acc = lax.dynamic_update_slice_in_dim(
            mixed_acc, mixed.reshape(slots, clips, lane_width), offset, 2
        )
        log_acc = lax.dynamic_update_slice_in_dim(log_acc, log_pair, 2 * number, 2)
        return (mixed_acc, log_acc)

    mixed_full, log_rows = lax.fori_loop(
        0,
        pair_count,
        forward_pair,
        (
            jnp.zeros((slots, clips, width), jnp.float32),
            jnp.zeros((slots, clips, HEADS), jnp.float32),
        ),
    )
    mixed_low = mixed_full.reshape(row_count, width).astype(jnp.bfloat16)
    middle = inputs + matmul(mixed_low, out_proj) + outb_full[0]
    normed2, ln2_back = jax.vjp(norm_rows, middle, gain_full[1], shift_full[1])
    normed2_low = normed2.astype(jnp.bfloat16)
    pre_act = matmul(normed2_low, up_proj) + upb_full
    activated, gelu_back = jax.vjp(gelu_exact, pre_act)
    hidden_low = activated.astype(jnp.bfloat16)
    final = middle + matmul(hidden_low, down_proj) + outb_full[1]
    output = (final * row_live).astype(jnp.bfloat16).reshape(slots, clips, width)
    grad_out_rows = cotangent.reshape(row_count, width).astype(jnp.float32) * row_live
    grad_out_low = grad_out_rows.astype(jnp.bfloat16)
    grad_down_part = matmul_tn(hidden_low, grad_out_low)
    grad_outb_mlp = jnp.sum(grad_out_rows, axis=0)
    grad_hidden = matmul_nt(grad_out_low, down_proj)
    grad_pre_low = gelu_back(grad_hidden)[0].astype(jnp.bfloat16)
    grad_up_part = matmul_tn(normed2_low, grad_pre_low)
    grad_upb_part = jnp.sum(grad_pre_low.astype(jnp.float32), axis=0)
    grad_normed2 = matmul_nt(grad_pre_low, up_proj)
    grad_mid_part, grad_gain_mlp, grad_shift_mlp = ln2_back(grad_normed2)
    grad_middle = grad_out_rows + grad_mid_part
    grad_branch = grad_middle.astype(jnp.bfloat16)
    grad_outp_part = matmul_tn(mixed_low, grad_branch)
    grad_outb_attn = jnp.sum(grad_branch.astype(jnp.float32), axis=0)
    grad_mixed_low = matmul_nt(grad_branch, out_proj).astype(jnp.bfloat16)
    grad_mixed3 = grad_mixed_low.reshape(slots, clips, width)

    def query_side(number):
        offset = number * lane_width
        query_pair = head_pair(query3, offset, lane_width, DH)
        grad_pair = head_pair(grad_mixed3, offset, lane_width, DH)
        key_pair = head_pair(all_memory, offset, lane_width, DH)
        value_pair = head_pair(all_memory, width + offset, lane_width, DH)
        log_pair = lax.dynamic_slice_in_dim(log_rows, 2 * number, 2, 2)
        probability = pair_probs(query_pair, key_pair, log_pair, key_mask, scale)
        grad_probs = jnp.einsum(
            "qchd,kchd->chqk", grad_pair, value_pair, preferred_element_type=jnp.float32
        )
        delta = jnp.sum(probability * grad_probs, axis=-1, keepdims=True)
        grad_scores = (probability * (grad_probs - delta)).astype(jnp.bfloat16)
        grad_query = (
            jnp.einsum("chqk,kchd->qchd", grad_scores, key_pair, preferred_element_type=jnp.float32)
            * scale
        )
        return (
            offset,
            query_pair,
            grad_pair,
            probability,
            grad_scores,
            delta,
            grad_query.reshape(slots, clips, lane_width),
        )

    zero_query = jnp.zeros((slots, clips, width), jnp.float32)

    def backward_pair(number, state):
        grad_query_acc, grad_memory = state
        side = query_side(number)
        offset = side[0]
        grad_keys = (
            jnp.einsum("chqk,qchd->kchd", side[4], side[1], preferred_element_type=jnp.float32)
            * scale
        )
        grad_values = jnp.einsum(
            "chqk,qchd->kchd",
            side[3].astype(jnp.bfloat16),
            side[2],
            preferred_element_type=jnp.float32,
        )
        grad_memory = add_lanes(
            grad_memory, grad_keys.reshape(key_count, clips, lane_width), offset
        )
        grad_memory = add_lanes(
            grad_memory, grad_values.reshape(key_count, clips, lane_width), width + offset
        )
        return (add_lanes(grad_query_acc, side[6], offset), grad_memory)

    grad_query_full, grad_memory_all = lax.fori_loop(
        0,
        pair_count,
        backward_pair,
        (zero_query, jnp.zeros((key_count, clips, 2 * width), jnp.float32)),
    )
    grad_memory_own = lax.psum_scatter(
        grad_memory_all, ("freq", "tm"), scatter_dimension=0, tiled=True
    )
    grad_query_low = grad_query_full.reshape(row_count, width).astype(jnp.bfloat16)
    grad_memory_low = grad_memory_own.reshape(row_count, 2 * width).astype(jnp.bfloat16)
    grad_joint = jnp.concatenate([grad_query_low, grad_memory_low], axis=1)
    grad_joint_part = matmul_tn(normed1_low, grad_joint)
    grad_bias_cols = jnp.stack(
        [
            jnp.sum(grad_query_low.astype(jnp.float32), axis=0),
            jnp.sum(grad_memory_low[:, width:].astype(jnp.float32), axis=0),
        ],
        axis=1,
    )
    grad_normed1 = matmul_nt(grad_joint, joint_proj)
    grad_in_part, grad_gain_attn, grad_shift_attn = ln1_back(grad_normed1)
    grad_patches = (grad_middle + grad_in_part).astype(jnp.bfloat16).reshape(slots, clips, width)
    shares = (
        lax.psum_scatter(
            grad_joint_part.astype(jnp.bfloat16), ("freq", "tm"), scatter_dimension=0, tiled=True
        ).astype(jnp.float32),
        lax.psum_scatter(
            grad_bias_cols.astype(jnp.bfloat16), ("freq", "tm"), scatter_dimension=0, tiled=True
        ).astype(jnp.float32),
        lax.psum_scatter(
            grad_outp_part.astype(jnp.bfloat16), ("freq", "tm"), scatter_dimension=0, tiled=True
        ).astype(jnp.float32),
        lax.psum_scatter(
            grad_outb_attn.astype(jnp.bfloat16), ("freq", "tm"), scatter_dimension=0, tiled=True
        ).astype(jnp.float32),
        lax.psum_scatter(
            grad_gain_attn.astype(jnp.bfloat16), ("freq", "tm"), scatter_dimension=0, tiled=True
        ).astype(jnp.float32),
        lax.psum_scatter(
            grad_shift_attn.astype(jnp.bfloat16), ("freq", "tm"), scatter_dimension=0, tiled=True
        ).astype(jnp.float32),
        lax.psum_scatter(
            grad_up_part.astype(jnp.bfloat16), ("freq", "tm"), scatter_dimension=0, tiled=True
        ).astype(jnp.float32),
        lax.psum_scatter(
            grad_upb_part.astype(jnp.bfloat16), ("freq", "tm"), scatter_dimension=0, tiled=True
        ).astype(jnp.float32),
        lax.psum_scatter(
            grad_down_part.astype(jnp.bfloat16), ("freq", "tm"), scatter_dimension=0, tiled=True
        ).astype(jnp.float32),
        lax.psum_scatter(
            grad_outb_mlp.astype(jnp.bfloat16), ("freq", "tm"), scatter_dimension=0, tiled=True
        ).astype(jnp.float32),
        lax.psum_scatter(
            grad_gain_mlp.astype(jnp.bfloat16), ("freq", "tm"), scatter_dimension=0, tiled=True
        ).astype(jnp.float32),
        lax.psum_scatter(
            grad_shift_mlp.astype(jnp.bfloat16), ("freq", "tm"), scatter_dimension=0, tiled=True
        ).astype(jnp.float32),
    )
    summed_all = (
        lax.psum(shares[0].astype(jnp.bfloat16), "dp").astype(jnp.float32),
        lax.psum(shares[1].astype(jnp.bfloat16), "dp").astype(jnp.float32),
        lax.psum(shares[2].astype(jnp.bfloat16), "dp").astype(jnp.float32),
        lax.psum(shares[3].astype(jnp.bfloat16), "dp").astype(jnp.float32),
        lax.psum(shares[4].astype(jnp.bfloat16), "dp").astype(jnp.float32),
        lax.psum(shares[5].astype(jnp.bfloat16), "dp").astype(jnp.float32),
        lax.psum(shares[6].astype(jnp.bfloat16), "dp").astype(jnp.float32),
        lax.psum(shares[7].astype(jnp.bfloat16), "dp").astype(jnp.float32),
        lax.psum(shares[8].astype(jnp.bfloat16), "dp").astype(jnp.float32),
        lax.psum(shares[9].astype(jnp.bfloat16), "dp").astype(jnp.float32),
        lax.psum(shares[10].astype(jnp.bfloat16), "dp").astype(jnp.float32),
        lax.psum(shares[11].astype(jnp.bfloat16), "dp").astype(jnp.float32),
    )
    attn_summed = summed_all[:6]
    mlp_summed = summed_all[6:]
    grad_norm_gain = jnp.stack([attn_summed[4], mlp_summed[4]])
    grad_norm_shift = jnp.stack([attn_summed[5], mlp_summed[5]])
    grad_out_bias = jnp.stack([attn_summed[3], mlp_summed[3]])
    grad_proj_bias = jnp.transpose(attn_summed[1])
    return (
        output,
        grad_patches,
        grad_norm_gain,
        grad_norm_shift,
        attn_summed[0],
        grad_proj_bias,
        attn_summed[2],
        mlp_summed[0],
        mlp_summed[1],
        mlp_summed[2],
        grad_out_bias,
    )


LOG2E = 1.4426950408889634
LANES = 128
F32 = jnp.float32
BF16 = jnp.bfloat16
VMEM_LIMIT = 62 << 20
SAFE_RANGE = 100.0
CHUNKS = 4
HALVES = 2
SPAN = 1024
BACK_SPAN = 512
COLLECT_FLOPS = 30 * 10**9


def normalize(values):
    centered = values - jnp.mean(values, axis=-1, keepdims=True)
    inverse = lax.rsqrt(jnp.mean(centered * centered, axis=-1, keepdims=True) + EPS)
    return centered * inverse, inverse


def norm_back(normed, inverse, incoming, gain):
    scaled = incoming * gain
    mean = jnp.mean(scaled, axis=-1, keepdims=True)
    slope = jnp.mean(scaled * normed, axis=-1, keepdims=True)
    return (scaled - mean - normed * slope) * inverse


def spans_of(tokens, size=SPAN):
    return [slice(at, min(at + size, 2 * tokens)) for at in range(0, 2 * tokens, size)]


def column_sum(values):
    return jnp.sum(values, axis=0, keepdims=True)


def project_kernel(x_ref, live_ref, w_ref, vec_ref, rows_ref, n_ref, q_ref, k_ref, v_ref, first_key, rows):
    blocks, slots, width = x_ref.shape
    padded = rows.shape[0] // blocks

    @pl.when(pl.program_id(0) == 0)
    def _():
        rows[...] = jnp.zeros_like(rows)

    for block in range(blocks):
        rows[block * padded : block * padded + slots] = x_ref[block].astype(F32)
    rows_ref[...] = rows[...].astype(BF16)
    normed, _ = normalize(rows[...])
    low = (normed * vec_ref[0:1, :] + vec_ref[1:2, :]).astype(BF16)
    n_ref[...] = low
    q_ref[...] = (matmul(low, w_ref[:, 0:width]) + vec_ref[2:3, :]).astype(BF16)
    keys = matmul(low, w_ref[:, width : 2 * width]).astype(BF16).astype(F32)

    @pl.when(pl.program_id(0) == 0)
    def _():
        first_key[...] = jnp.broadcast_to(keys[0:1, :], first_key.shape)

    k_ref[...] = jnp.where(live_ref[:, 0:1] > 0, keys, first_key[0:1, :]).astype(BF16)
    v_ref[...] = (matmul(low, w_ref[:, 2 * width : 3 * width]) + vec_ref[3:4, :]).astype(BF16)


def project(blocks, live_lanes, joint_proj, vectors, steps=4):
    members, slots, width = blocks.shape
    tokens = live_lanes.shape[0]
    rows = tokens // steps
    block = pl.BlockSpec((rows, width), lambda step: (step, 0))
    return pl.pallas_call(
        project_kernel,
        grid=(steps,),
        in_specs=[
            pl.BlockSpec((members // steps, slots, width), lambda step: (step, 0, 0)),
            pl.BlockSpec((rows, LANES), lambda step: (step, 0)),
            pl.BlockSpec((width, 3 * width), lambda step: (0, 0), pipeline_mode=pl.Buffered(1)),
            pl.BlockSpec((8, width), lambda step: (0, 0)),
        ],
        out_specs=[block] * 5,
        out_shape=[jax.ShapeDtypeStruct((tokens, width), BF16)] * 5,
        scratch_shapes=[pltpu.VMEM((8, width), F32), pltpu.VMEM((rows, width), F32)],
        compiler_params=pltpu.CompilerParams(vmem_limit_bytes=VMEM_LIMIT),
        cost_estimate=pl.CostEstimate(
            flops=6 * tokens * width * width, transcendentals=tokens, bytes_accessed=10 * tokens * width
        ),
    )(blocks, live_lanes, joint_proj, vectors)


def attention_forward_kernel(q_ref, k_ref, v_ref, live_ref, o_ref, rn_ref, p_ref, qs, vt, ot, sa, p_buf, p_sem):
    tokens = q_ref.shape[0]
    pair = pl.program_id(0)
    slot = lax.rem(pair, 2)
    spans = spans_of(tokens)

    def copy_of(pair, slot, index):
        span = spans[index]
        columns = pl.ds(span.start, span.stop - span.start)
        return pltpu.make_async_copy(
            p_buf.at[slot, :, columns], p_ref.at[pair, :, columns], p_sem.at[slot, index]
        )

    @pl.when(pair >= 2)
    def _():
        for index in range(len(spans)):
            copy_of(pair - 2, slot, index).wait()

    lane = lax.broadcasted_iota(jnp.int32, (tokens, LANES), 1)
    query = q_ref[...].astype(F32) * (1.0 / math.sqrt(DH))
    keys = k_ref[...].astype(F32)
    qs[0:tokens, :] = jnp.where(lane < DH, query, 0.0).astype(BF16)
    qs[tokens : 2 * tokens, :] = jnp.where(lane < DH, 0.0, query).astype(BF16)
    live = live_ref[0:1, :]
    vt[0:LANES, :] = (jnp.transpose(v_ref[...].astype(F32)) * live).astype(BF16)
    vt[LANES : LANES + 16, :] = jnp.broadcast_to(live, (16, tokens)).astype(BF16)

    def largest(values, head):
        squares = jnp.where((lane < DH) == (head == 0), values * values, 0.0)
        return jnp.max(jnp.sum(squares, axis=1, keepdims=True))

    limit = (SAFE_RANGE / LOG2E) ** 2
    bound = jnp.maximum(
        largest(query, 0) * largest(keys, 0), largest(query, 1) * largest(keys, 1)
    )
    bounded = bound <= limit

    def finish(span, weight):
        p_buf[slot, :, span] = weight
        ot[:, span] = matmul(vt[...], weight)

    @pl.when(bounded)
    def _():
        for index, span in enumerate(spans):
            finish(span, jnp.exp2(matmul_nt(k_ref[...], qs[span, :]) * LOG2E).astype(BF16))
            copy_of(pair, slot, index).start()

    @pl.when(jnp.logical_not(bounded))
    def _():
        def column(index, _):
            part = pl.ds(pl.multiple_of(index * LANES, LANES), LANES)
            sa[...] = matmul_nt(k_ref[...], qs[part, :])
            score = sa[...]
            highest = jnp.max(score, axis=0, keepdims=True)
            finish(part, jnp.exp2(score * LOG2E - highest * LOG2E).astype(BF16))
            return 0

        lax.fori_loop(0, 2 * tokens // LANES, column, 0)
        for index in range(len(spans)):
            copy_of(pair, slot, index).start()

    row = lax.broadcasted_iota(jnp.int32, (LANES, tokens), 0)
    inverse = jnp.where(
        row < DH,
        jnp.broadcast_to(1.0 / ot[LANES : LANES + 1, 0:tokens], (LANES, tokens)),
        jnp.broadcast_to(1.0 / ot[LANES : LANES + 1, tokens : 2 * tokens], (LANES, tokens)),
    )
    mixed = jnp.where(row < DH, ot[0:LANES, 0:tokens], ot[0:LANES, tokens : 2 * tokens]) * inverse
    o_ref[...] = jnp.transpose(mixed).astype(BF16)
    rn_ref[...] = jnp.transpose(inverse)

    @pl.when(pair == pl.num_programs(0) - 1)
    def _():
        for index in range(len(spans)):
            copy_of(pair - 1, 1 - slot, index).wait()
        for index in range(len(spans)):
            copy_of(pair, slot, index).wait()


def attention_forward(query, keys, memory, live_row):
    tokens, width = query.shape
    pairs = width // LANES
    block = pl.BlockSpec((tokens, LANES), lambda pair: (0, pair))
    return pl.pallas_call(
        attention_forward_kernel,
        grid=(pairs,),
        in_specs=[block, block, block, pl.BlockSpec((8, tokens), lambda pair: (0, 0))],
        out_specs=[block, block, pl.BlockSpec(memory_space=pl.ANY)],
        out_shape=[
            jax.ShapeDtypeStruct((tokens, width), BF16),
            jax.ShapeDtypeStruct((tokens, width), F32),
            jax.ShapeDtypeStruct((pairs, tokens, 2 * tokens), BF16),
        ],
        scratch_shapes=[
            pltpu.VMEM((2 * tokens, LANES), BF16),
            pltpu.VMEM((LANES + 16, tokens), BF16),
            pltpu.VMEM((LANES + 16, 2 * tokens), F32),
            pltpu.VMEM((tokens, LANES), F32),
            pltpu.VMEM((2, tokens, 2 * tokens), BF16),
            pltpu.SemaphoreType.DMA((2, len(spans_of(tokens)))),
        ],
        compiler_params=pltpu.CompilerParams(vmem_limit_bytes=VMEM_LIMIT),
        cost_estimate=pl.CostEstimate(
            flops=8 * pairs * tokens * tokens * LANES,
            transcendentals=2 * pairs * tokens * tokens,
            bytes_accessed=4 * pairs * tokens * tokens,
        ),
    )(query, keys, memory, live_row)


def attention_backward_kernel(
    q_ref, k_ref, v_ref, o_ref, do_ref, rn_ref, live_ref, keep_ref, p_ref, n_ref, w_ref,
    x_ref, res_ref, vec_ref, sums_ref, half_ref, out_ref,
    kept_ref, sent_ref, rows_ref, qs, gs, kt, dqt, delta, dj, vecs, n_buf, w_buf, x_buf, res_buf, dx_buf, sem, dx_sem,
):
    tokens = q_ref.shape[0]
    pair = pl.program_id(0)

    late = [
        pltpu.make_async_copy(source, target, sem.at[index])
        for index, (source, target) in enumerate(
            ((n_ref, n_buf), (w_ref, w_buf), (x_ref, x_buf), (res_ref, res_buf))
        )
    ]

    @pl.when(pair == 0)
    def _():
        for copy in late:
            copy.start()

    scale = 1.0 / math.sqrt(DH)
    lane = lax.broadcasted_iota(jnp.int32, (tokens, LANES), 1)
    query = q_ref[...].astype(F32) * scale
    qs[0:tokens, :] = jnp.where(lane < DH, query, 0.0).astype(BF16)
    qs[tokens : 2 * tokens, :] = jnp.where(lane < DH, 0.0, query).astype(BF16)
    grad = do_ref[...].astype(F32) * rn_ref[...]
    gs[0:tokens, :] = jnp.where(lane < DH, grad, 0.0).astype(BF16)
    gs[tokens : 2 * tokens, :] = jnp.where(lane < DH, 0.0, grad).astype(BF16)
    kt[...] = (jnp.transpose(k_ref[...].astype(F32)) * (live_ref[0:1, :] * scale)).astype(BF16)
    product = jnp.transpose(grad * o_ref[...].astype(F32))
    for head in range(2):
        total = column_sum(product[head * DH : (head + 1) * DH])
        delta[:, head * tokens : (head + 1) * tokens] = jnp.broadcast_to(total, (8, tokens))
    grad_keys = grad_values = None
    for span in spans_of(tokens, BACK_SPAN):
        weight = p_ref[0, :, span]
        grad_weight = matmul_nt(v_ref[...], gs[span, :])
        grad_score = (weight.astype(F32) * (grad_weight - delta[0:1, span])).astype(BF16)
        dqt[:, span] = matmul(kt[...], grad_score)
        part_values = matmul(weight, gs[span, :])
        part_keys = matmul(grad_score, qs[span, :])
        grad_values = part_values if grad_values is None else grad_values + part_values
        grad_keys = part_keys if grad_keys is None else grad_keys + part_keys
    row = lax.broadcasted_iota(jnp.int32, (LANES, tokens), 0)
    grad_query = jnp.transpose(jnp.where(row < DH, dqt[:, 0:tokens], dqt[:, tokens : 2 * tokens]))
    keep = keep_ref[...] > 0
    width = x_buf.shape[1]
    parts = (
        grad_query.astype(BF16),
        jnp.where(keep, grad_keys, 0.0).astype(BF16),
        jnp.where(keep, grad_values, 0.0).astype(BF16),
    )
    for part, value in enumerate(parts):
        columns = pl.ds(pl.multiple_of(part * width + pl.program_id(0) * LANES, LANES), LANES)
        dj[:, columns] = value
        if part != 1:
            columns = pl.ds(pl.multiple_of(pl.program_id(0) * LANES, LANES), LANES)
            vecs[2 + part // 2 : 3 + part // 2, columns] = column_sum(value.astype(F32))

    @pl.when(pl.program_id(0) == pl.num_programs(0) - 1)
    def _():
        for copy in late:
            copy.wait()
        first = half_ref[0] == 0
        half = width // 2
        for part in range(3):
            span = slice(part * width, (part + 1) * width)
            grad_weights = matmul_tn(n_buf[...], dj[:, span]).astype(BF16)
            kept_ref[:, span] = jnp.where(first, grad_weights[:half], grad_weights[half:])
            sent_ref[:, span] = jnp.where(first, grad_weights[half:], grad_weights[:half])
        vecs[4:8, :] = sums_ref[0:4, :]
        rows = tokens // CHUNKS
        block = tokens // rows_ref.shape[0]
        stores = []
        gain_sum = shift_sum = 0.0
        for start in range(0, tokens, rows):
            span = slice(start, start + rows)
            incoming = matmul_nt(dj[span, :], w_buf[...])
            normed, inverse = normalize(x_buf[span, :].astype(F32))
            gain_sum += column_sum(incoming * normed)
            shift_sum += column_sum(incoming)
            back = norm_back(normed, inverse, incoming, vec_ref[0:1, :])
            grad_rows = (res_buf[span, :].astype(F32) + back).astype(BF16)
            for part in range(rows // block):
                dx_buf[start // block + part] = grad_rows[part * block : part * block + dx_buf.shape[1]]
            stores.append(
                pltpu.make_async_copy(
                    dx_buf.at[pl.ds(start // block, rows // block)],
                    rows_ref.at[pl.ds(start // block, rows // block), 0],
                    dx_sem.at[start // rows],
                )
            )
            stores[-1].start()
        vecs[0:1, :] = gain_sum
        vecs[1:2, :] = shift_sum
        turned = jnp.transpose(jnp.concatenate([vecs[...]] * (LANES // 8), axis=0)).astype(BF16)
        tail = kept_ref.shape[1] - LANES
        kept_ref[:, tail:] = jnp.where(first, turned[:half], turned[half:])
        sent_ref[:, tail:] = jnp.where(first, turned[half:], turned[:half])
        for copy in stores:
            copy.wait()


def attention_backward(
    query, keys, memory, mixed, grad_mixed, inverse, live_row, live_lanes, weights, normed, joint_proj,
    inputs, residual, vectors, vector_grads, own_half, output,
):
    tokens, width = query.shape
    pairs = width // LANES
    block = pl.BlockSpec((tokens, LANES), lambda pair: (0, pair))
    once = pl.Buffered(1)
    anywhere = pl.BlockSpec(memory_space=pl.ANY)

    def fixed(rows, columns):
        return pl.BlockSpec((rows, columns), lambda pair: (0, 0), pipeline_mode=once)

    return pl.pallas_call(
        attention_backward_kernel,
        grid=(pairs,),
        in_specs=[block] * 6
        + [
            fixed(8, tokens),
            fixed(tokens, LANES),
            pl.BlockSpec((1, tokens, 2 * tokens), lambda pair: (pair, 0, 0)),
            anywhere,
            anywhere,
            anywhere,
            anywhere,
            fixed(8, width),
            fixed(8, width),
            pl.BlockSpec(memory_space=pltpu.SMEM),
            anywhere,
        ],
        out_specs=[fixed(width // 2, 3 * width + LANES), fixed(width // 2, 3 * width + LANES), anywhere],
        out_shape=[
            jax.ShapeDtypeStruct((width // 2, 3 * width + LANES), BF16),
            jax.ShapeDtypeStruct((width // 2, 3 * width + LANES), BF16),
            jax.ShapeDtypeStruct(output.shape, BF16),
        ],
        scratch_shapes=[
            pltpu.VMEM((2 * tokens, LANES), BF16),
            pltpu.VMEM((2 * tokens, LANES), BF16),
            pltpu.VMEM((LANES, tokens), BF16),
            pltpu.VMEM((LANES, 2 * tokens), F32),
            pltpu.VMEM((8, 2 * tokens), F32),
            pltpu.VMEM((tokens, 3 * width), BF16),
            pltpu.VMEM((8, width), F32),
            pltpu.VMEM((tokens, width), BF16),
            pltpu.VMEM((width, 3 * width), BF16),
            pltpu.VMEM((tokens, width), BF16),
            pltpu.VMEM((tokens, width), BF16),
            pltpu.VMEM((output.shape[0],) + output.shape[2:], BF16),
            pltpu.SemaphoreType.DMA((4,)),
            pltpu.SemaphoreType.DMA((CHUNKS,)),
        ],
        input_output_aliases={16: 2},
        compiler_params=pltpu.CompilerParams(vmem_limit_bytes=VMEM_LIMIT),
        cost_estimate=pl.CostEstimate(
            flops=16 * pairs * tokens * tokens * LANES,
            transcendentals=0,
            bytes_accessed=4 * pairs * tokens * tokens,
        ),
    )(
        query, keys, memory, mixed, grad_mixed, inverse, live_row, live_lanes, weights, normed,
        joint_proj, inputs, residual, vectors, vector_grads,
        own_half, output,
    )


def feed_forward_kernel(
    x_hbm, mixed_hbm, cot_hbm, live_ref, wo_ref, vec_ref, up_ref, down_ref, bias_ref,
    out_hbm, share_ref, branch_hbm, gm_hbm, packed_ref, ds_ref,
    x_ref, mixed_ref, cot_ref, out_ref, branch_ref, gm_ref,
    normed, grad_out, middle, acc, acc_grad, hidden, grad_pre, down_buf, up_buf, down_sem, up_sem, in_sem, out_sem,
):
    step = pl.program_id(0)
    last = pl.num_programs(0) - 1
    tokens, width = x_ref.shape
    units = up_ref.shape[1]
    rows = tokens // CHUNKS

    block = tokens // out_ref.shape[0]
    slots = out_ref.shape[1]
    parts = rows // block

    def rows_of_chunk(chunk):
        return pl.ds(pl.multiple_of(chunk * rows, 32), rows)

    def fetches(chunk):
        span = rows_of_chunk(chunk)
        pairs = ((x_hbm, x_ref), (mixed_hbm, mixed_ref), (cot_hbm, cot_ref))
        return [
            pltpu.make_async_copy(source.at[span], target.at[span], in_sem.at[chunk, index])
            for index, (source, target) in enumerate(pairs)
        ]

    def stores(chunk):
        span = rows_of_chunk(chunk)
        return [
            pltpu.make_async_copy(source.at[span], target.at[span], out_sem.at[chunk, index])
            for index, (source, target) in enumerate(((branch_ref, branch_hbm), (gm_ref, gm_hbm)))
        ] + [
            pltpu.make_async_copy(
                out_ref.at[pl.ds(chunk * parts, parts)],
                out_hbm.at[pl.ds(chunk * parts, parts), 1],
                out_sem.at[chunk, 2],
            )
        ]

    @pl.when(step == 0)
    def _():
        for chunk in range(CHUNKS):
            for copy in fetches(chunk):
                copy.start()

        def chunk_step(chunk, _):
            span = rows_of_chunk(chunk)
            for copy in fetches(chunk):
                copy.wait()
            values = x_ref[span, :].astype(F32) + matmul(mixed_ref[span, :], wo_ref[...]) + vec_ref[2:3, :]
            middle[span, :] = values
            acc[span, :] = values + vec_ref[3:4, :]
            unit, _ = normalize(values)
            normed[span, :] = (unit * vec_ref[0:1, :] + vec_ref[1:2, :]).astype(BF16)
            grad_out[span, :] = (cot_ref[span, :].astype(F32) * live_ref[span, 0:1]).astype(BF16)
            acc_grad[span, :] = jnp.zeros((rows, width), F32)
            return 0

        lax.fori_loop(0, CHUNKS, chunk_step, 0)

    up = up_ref[...]
    down = down_ref[...]
    half = tokens // HALVES

    def feed(index, grad_bias):
        span = pl.ds(pl.multiple_of(index * half, 32), half)
        pre_act = matmul(normed[span, :], up) + bias_ref[0:1, :]
        grad_hidden = matmul_nt(grad_out[span, :], down)
        cumulative = 0.5 + 0.5 * lax.erf(pre_act * math.sqrt(0.5))
        density = jnp.exp2(pre_act * pre_act * (-0.5 * LOG2E)) * (1.0 / math.sqrt(2.0 * math.pi))
        low = (pre_act * cumulative).astype(BF16)
        grad_low = (grad_hidden * (cumulative + pre_act * density)).astype(BF16)
        hidden[span, :] = low
        grad_pre[span, :] = grad_low
        acc[span, :] += matmul(low, down)
        acc_grad[span, :] += matmul_nt(grad_low, up)
        return grad_bias + column_sum(grad_low.astype(F32))

    grad_bias = lax.fori_loop(0, HALVES, feed, jnp.zeros((1, units), F32))
    slot = lax.rem(step, 2)
    _, cuts, quarters, share, _ = down_buf.shape
    own = units // cuts
    for cut in range(cuts):
        sums = jnp.broadcast_to(grad_bias[:, cut * own : (cut + 1) * own], (16, own)).astype(BF16)
        share_ref[step * cuts + cut, share : share + 16, 0:own] = sums
        share_ref[step * cuts + cut, share : share + 16, own:width] = jnp.zeros((16, width - own), BF16)

    def copies(at, slot):
        return (
            pltpu.make_async_copy(
                down_buf.at[slot], packed_ref.at[pl.ds(at * cuts, cuts), pl.ds(0, quarters)], down_sem.at[slot]
            ),
            pltpu.make_async_copy(up_buf.at[slot], packed_ref.at[:, quarters + at], up_sem.at[slot]),
        )

    @pl.when(step >= 2)
    def _():
        for copy in copies(step - 2, slot):
            copy.wait()

    grad_down = matmul_tn(hidden[...], grad_out[...]).astype(BF16)
    for cut in range(cuts):
        for quarter in range(quarters):
            base = (cut * quarters + quarter) * share
            down_buf[slot, cut, quarter] = grad_down[base : base + share]
    grad_up = matmul_tn(normed[...], grad_pre[...]).astype(BF16)
    for member in range(width // share):
        up_buf[slot, member] = grad_up[member * share : (member + 1) * share]
    for copy in copies(step, slot):
        copy.start()

    @pl.when(step == last)
    def _():
        ds_ref[...] = jnp.zeros_like(ds_ref)

        def chunk_step(chunk, _):
            span = rows_of_chunk(chunk)
            final = (acc[span, :] * live_ref[span, 0:1]).astype(BF16)
            for part in range(parts):
                out_ref[chunk * parts + part] = final[part * block : part * block + slots]
            unit, inverse = normalize(middle[span, :])
            incoming = acc_grad[span, :]
            start = grad_out[span, :].astype(F32)
            branch = (start + norm_back(unit, inverse, incoming, vec_ref[0:1, :])).astype(BF16)
            branch_ref[span, :] = branch
            gm_ref[span, :] = matmul_nt(branch, wo_ref[...]).astype(BF16)
            for copy in stores(chunk):
                copy.start()
            for place, term in enumerate((incoming * unit, incoming, branch.astype(F32), start)):
                ds_ref[place : place + 1, :] += column_sum(term)
            return 0

        lax.fori_loop(0, CHUNKS, chunk_step, 0)
        grad_outp = matmul_tn(mixed_ref[...], branch_ref[...]).astype(BF16)
        for member in range(width // share):
            share_ref[member, 0:share, :] = grad_outp[member * share : (member + 1) * share]
        for chunk in range(CHUNKS):
            for copy in stores(chunk):
                copy.wait()
        for copy in copies(step - 1, 1 - slot):
            copy.wait()
        for copy in copies(step, slot):
            copy.wait()


def feed_forward(
    inputs, mixed, cotangent, live_lanes, out_proj, vectors, up_proj, up_bias, down_proj, members, slots
):
    tokens, width = inputs.shape
    hidden_units = up_proj.shape[1]
    steps = hidden_units // width
    share = width // members
    cuts = members // steps
    quarters = hidden_units // members // share
    once = pl.Buffered(1)
    anywhere = pl.BlockSpec(memory_space=pl.ANY)

    def fixed(rows, columns):
        return pl.BlockSpec((rows, columns), lambda step: (0, 0), pipeline_mode=once)

    return pl.pallas_call(
        feed_forward_kernel,
        grid=(steps,),
        in_specs=[
            anywhere,
            anywhere,
            anywhere,
            fixed(tokens, LANES),
            fixed(width, width),
            fixed(8, width),
            pl.BlockSpec((width, width), lambda step: (0, step)),
            pl.BlockSpec((width, width), lambda step: (step, 0)),
            pl.BlockSpec((8, width), lambda step: (0, step)),
        ],
        out_specs=[
            anywhere,
            pl.BlockSpec((members, share + 16, width), lambda step: (0, 0, 0), pipeline_mode=once),
            anywhere,
            anywhere,
            anywhere,
            fixed(8, width),
        ],
        out_shape=[
            jax.ShapeDtypeStruct((members, 2, slots, width), BF16),
            jax.ShapeDtypeStruct((members, share + 16, width), BF16),
            jax.ShapeDtypeStruct((tokens, width), BF16),
            jax.ShapeDtypeStruct((tokens, width), BF16),
            jax.ShapeDtypeStruct((members, quarters + steps, share, width), BF16),
            jax.ShapeDtypeStruct((8, width), F32),
        ],
        scratch_shapes=[pltpu.VMEM((tokens, width), BF16)] * 3
        + [
            pltpu.VMEM((members, slots, width), BF16),
            pltpu.VMEM((tokens, width), BF16),
            pltpu.VMEM((tokens, width), BF16),
            pltpu.VMEM((tokens, width), BF16),
            pltpu.VMEM((tokens, width), BF16),
            pltpu.VMEM((tokens, width), F32),
            pltpu.VMEM((tokens, width), F32),
            pltpu.VMEM((tokens, width), F32),
            pltpu.VMEM((tokens, width), BF16),
            pltpu.VMEM((tokens, width), BF16),
            pltpu.VMEM((2, cuts, quarters, share, width), BF16),
            pltpu.VMEM((2, members, share, width), BF16),
            pltpu.SemaphoreType.DMA((2,)),
            pltpu.SemaphoreType.DMA((2,)),
            pltpu.SemaphoreType.DMA((CHUNKS, 3)),
            pltpu.SemaphoreType.DMA((CHUNKS, 3)),
        ],
        compiler_params=pltpu.CompilerParams(vmem_limit_bytes=VMEM_LIMIT),
        cost_estimate=pl.CostEstimate(
            flops=12 * tokens * width * hidden_units + 6 * tokens * width * width,
            transcendentals=2 * tokens * hidden_units,
            bytes_accessed=12 * tokens * width + 8 * width * hidden_units,
        ),
    )(inputs, mixed, cotangent, live_lanes, out_proj, vectors, up_proj, down_proj, up_bias)


def collect_joint_kernel(own_ref, *refs):
    pieces, (joint_ref, gain_ref, shift_ref, bias_ref, branch_ref, columns) = refs[:-6], refs[-6:]
    rows = pieces[0].shape[0]
    width = joint_ref.shape[1] // 3
    own = own_ref[0]
    columns[...] = jnp.zeros_like(columns)
    for place in range(len(pieces)):
        piece = pieces[place][...]
        for other in range(1, len(pieces)):
            piece = jnp.where(own == other, pieces[place ^ other][...], piece)
        piece = piece.astype(F32)
        span = slice(place * rows, (place + 1) * rows)
        joint_ref[span, :] = piece[:, : 3 * width]
        columns[span, :] = piece[:, 3 * width :]
    turned = jnp.transpose(columns[...])
    share = gain_ref.shape[1]
    gain_ref[0:1, :] = turned[0:1, 0:share]
    gain_ref[1:2, :] = turned[4:5, 0:share]
    shift_ref[0:1, :] = turned[1:2, 0:share]
    shift_ref[1:2, :] = turned[5:6, 0:share]
    bias_ref[...] = turned[2:4, 0:share]
    branch_ref[...] = turned[6:8, 0:share]


def collect_joint(own, pieces, share):
    width = (pieces[0].shape[1] - LANES) // 3
    vmem = pl.BlockSpec(memory_space=pltpu.VMEM)
    return pl.pallas_call(
        collect_joint_kernel,
        in_specs=[pl.BlockSpec(memory_space=pltpu.SMEM)] + [vmem] * len(pieces),
        out_specs=[vmem] * 5,
        out_shape=[jax.ShapeDtypeStruct((share, 3 * width), F32)] + [jax.ShapeDtypeStruct((2, share), F32)] * 4,
        scratch_shapes=[pltpu.VMEM((LANES, LANES), F32)],
        cost_estimate=pl.CostEstimate(flops=0, transcendentals=0, bytes_accessed=0),
    )(own, *pieces)


def collect_mlp_kernel(rows_ref, sums_ref, down_ref, up_ref, outp_ref, bias_ref):
    own, width = down_ref.shape
    share = outp_ref.shape[0]
    down_ref[...] = rows_ref[0:own, :].astype(F32)
    for part in range(own // share):
        rows = slice(own + part * share, own + (part + 1) * share)
        up_ref[:, part * width : (part + 1) * width] = rows_ref[rows, :].astype(F32)
    outp_ref[...] = sums_ref[0:share, :].astype(F32)
    bias_ref[...] = sums_ref[share : share + 8, 0:own].astype(F32)[0]


def collect_mlp(rows, sums, share):
    own, width = rows.shape[0] // 2, rows.shape[1]
    vmem = pl.BlockSpec(memory_space=pltpu.VMEM)
    return pl.pallas_call(
        collect_mlp_kernel,
        in_specs=[vmem] * 2,
        out_specs=[vmem] * 4,
        out_shape=[
            jax.ShapeDtypeStruct((own, width), F32),
            jax.ShapeDtypeStruct((share, own // share * width), F32),
            jax.ShapeDtypeStruct((share, width), F32),
            jax.ShapeDtypeStruct((own,), F32),
        ],
        cost_estimate=pl.CostEstimate(flops=COLLECT_FLOPS, transcendentals=0, bytes_accessed=4 * rows.size),
    )(rows, sums)


def per_device(
    patches,
    col_counts,
    norm_gain,
    norm_shift,
    joint_proj,
    proj_bias,
    out_proj,
    up_proj,
    up_bias,
    down_proj,
    out_bias,
    cotangent,
):
    slots, clips, width = patches.shape
    group = ("freq", "tm")
    freq_size = lax.axis_size("freq")
    time_size = lax.axis_size("tm")
    groups = lax.axis_size("dp")
    members = freq_size * time_size
    freq_rows = FREQ_ROWS // freq_size
    cap_cols = (slots - 2) // freq_rows
    padded = -(-slots // 16) * 16
    tokens = members * padded
    pairs = width // LANES
    share = width // members
    hidden_units = up_proj.shape[1]

    def to_clip(array):
        return lax.all_to_all(array, group, 0, 0, tiled=True)

    token_ids = jnp.arange(tokens, dtype=jnp.int32)
    block_ids = token_ids // padded
    live = live_slots(
        col_counts,
        token_ids % padded,
        block_ids // time_size,
        block_ids % time_size,
        freq_rows,
        cap_cols,
    ) & (token_ids % padded < slots)
    live_full = live.astype(F32)
    live_row = jnp.broadcast_to(live_full[None, :], (8, tokens))
    live_lanes = jnp.broadcast_to(live_full[:, None], (tokens, LANES))

    def rows_of(*vectors):
        stacked = jnp.stack(vectors).astype(F32)
        return jnp.pad(stacked, ((0, 8 - len(vectors)), (0, 0)))

    vectors1 = rows_of(norm_gain[0], norm_shift[0], proj_bias[0], proj_bias[1])
    vectors2 = rows_of(norm_gain[1], norm_shift[1], out_bias[0], out_bias[1])
    bias_rows = jnp.broadcast_to(up_bias.astype(F32)[None, :], (8, hidden_units))

    arrived = to_clip(jnp.transpose(patches, (1, 0, 2)))
    turned = jnp.pad(jnp.transpose(cotangent, (1, 0, 2)), ((0, 0), (0, padded - slots), (0, 0)))
    turned, live_lanes, live_row, vectors1, vectors2, bias_rows = lax.optimization_barrier(
        (turned, live_lanes, live_row, vectors1, vectors2, bias_rows)
    )
    cot = to_clip(turned).reshape(tokens, width)
    inputs, normed1, query, keys, memory = project(arrived, live_lanes, joint_proj, vectors1)
    mixed, inverse, weights = attention_forward(query, keys, memory, live_row)
    output, blocks, branch, grad_mixed, packed, vector_grads = feed_forward(
        inputs, mixed, cot, live_lanes, out_proj, vectors2, up_proj, bias_rows, down_proj, members, padded
    )
    own = hidden_units // members
    mlp_rows = lax.psum_scatter(packed.reshape(members, 2 * own, width), group, scatter_dimension=0, tiled=True)[0]
    moved = lax.all_to_all(blocks, group, 0, 0, tiled=True)

    own_half = lax.axis_index("freq")
    own_group = lax.axis_index("dp")
    kept, sent, token_rows = attention_backward(
        query, keys, memory, mixed, grad_mixed, inverse, live_row, live_lanes, weights, normed1, joint_proj,
        inputs, branch, vectors1, vector_grads, own_half.reshape(1),
        output,
    )
    kept, sent, moved = lax.optimization_barrier((kept, sent, moved))
    got = lax.ppermute(sent, "freq", [(0, 1), (1, 0)])
    outp_rows = jnp.sum(moved[:, : share + 8].astype(F32), axis=0).astype(BF16)
    joint_half = (kept.astype(F32) + got.astype(F32)).astype(BF16).reshape(time_size, share, kept.shape[1])
    joint_half, mlp_rows, outp_rows = lax.optimization_barrier((joint_half, mlp_rows, outp_rows))
    mlp_sum, outp_sum = lax.psum((mlp_rows, outp_rows), "dp")
    arrived = lax.all_to_all(joint_half, "tm", 0, 0, tiled=True)
    joint_rows = jnp.sum(arrived.astype(F32), axis=0).astype(BF16)
    joint_rows, token_rows = lax.optimization_barrier((joint_rows, token_rows))

    def to_group(array, distance):
        return lax.ppermute(array, "dp", [(i, i ^ distance) for i in range(groups)])

    cut = joint_rows.reshape(groups, share // groups, kept.shape[1])
    piece = lax.dynamic_index_in_dim(cut, own_group, 0, False).astype(F32)
    for distance in range(1, groups):
        piece += to_group(lax.dynamic_index_in_dim(cut, own_group ^ distance, 0, False), distance).astype(F32)
    piece = piece.astype(BF16)
    pieces = [piece] + [to_group(piece, distance) for distance in range(1, groups)]
    token_rows = lax.all_to_all(token_rows, group, 0, 0, tiled=True)
    grad_patches, output = (jnp.transpose(token_rows[:, kind, :slots], (1, 0, 2)) for kind in range(2))

    joint_sum, gain_sum, shift_sum, bias_sum, branch_sum = collect_joint(own_group.reshape(1), pieces, share)
    joint_sum, mlp_sum, outp_sum = lax.optimization_barrier((joint_sum, mlp_sum, outp_sum))
    down_sum, up_sum, outp_sum, up_bias_sum = collect_mlp(mlp_sum, outp_sum, share)
    return (
        output,
        grad_patches,
        gain_sum,
        shift_sum,
        joint_sum,
        bias_sum,
        outp_sum,
        up_sum,
        up_bias_sum,
        down_sum,
        branch_sum,
    )


def plan(patches, *others):
    members = lax.axis_size("freq") * lax.axis_size("tm")
    if patches.shape[1] == members:
        return per_device(patches, *others)
    return per_device_gathered(patches, *others)


def solution(mesh):
    return jax.shard_map(
        plan,
        mesh=mesh,
        in_specs=(
            P(("freq", "tm"), "dp", None),
            P(),
            P(),
            P(),
            P(),
            P(),
            P(),
            P(),
            P(),
            P(),
            P(),
            P(("freq", "tm"), "dp", None),
        ),
        out_specs=(
            P(("freq", "tm"), "dp", None),
            P(("freq", "tm"), "dp", None),
            P(None, ("freq", "tm")),
            P(None, ("freq", "tm")),
            P(("freq", "tm"), None),
            P(None, ("freq", "tm")),
            P(("freq", "tm"), None),
            P(("freq", "tm"), None),
            P(("freq", "tm")),
            P(("freq", "tm"), None),
            P(None, ("freq", "tm")),
        ),
        check_vma=False,
    )
```
